32 devices in a mesh: fsdp: 4 (over z), ctx: 2 (over x), tp: 4 (over y, core).
Axes of the slice: x: 2, y: 2, z: 4, core: 2. Of those that a mesh axis runs over, the one named last changes fastest.
Arguments:
- block_input: bfloat16 [4, 1024, 1024], P('fsdp', 'ctx'), may hold values from -6 to 6
- segment_ids: int32 [4, 1024], P('fsdp'), may hold values from 0 to 15, never falling along the last dimension, each value on 1 to 512 neighbouring positions
- cotangent: bfloat16 [4, 1024, 1024], P('fsdp', 'ctx'), may hold values from -6 to 6
- qkv_weight: float32 [1024, 3, 1024], P('fsdp', None, 'tp'), may hold values from -0.1875 to 0.1875
- qv_bias: float32 [2, 1024], P(None, ('tp', 'fsdp')), may hold values from -3 to 3
- out_weight: float32 [1024, 1024], P('tp', 'fsdp'), may hold values from -0.5 to 0.5
- out_bias: float32 [1024], P('fsdp'), may hold values from -3 to 3
- norm1_gain: float32 [1024], P('fsdp'), may hold values from 0.1 to 1.9
- norm1_shift: float32 [1024], P('fsdp'), may hold values from -3 to 3
- fc_weight: float32 [1024, 4096], P('fsdp', 'tp'), may hold values from -0.1875 to 0.1875
- fc_bias: float32 [4096], P(('tp', 'fsdp')), may hold values from -3 to 3
- proj_weight: float32 [4096, 1024], P('tp', 'fsdp'), may hold values from -0.09375 to 0.09375
- proj_bias: float32 [1024], P('fsdp'), may hold values from -3 to 3
- norm2_gain: float32 [1024], P('fsdp'), may hold values from 0.1 to 1.9
- norm2_shift: float32 [1024], P('fsdp'), may hold values from -3 to 3
Outputs:
- block_output: bfloat16 [4, 1024, 1024], P('fsdp', 'ctx')
- input_grad: bfloat16 [4, 1024, 1024], P('fsdp', 'ctx')
- wqkv_grad: float32 [1024, 3, 1024], P('fsdp', None, 'tp')
- bqv_grad: float32 [2, 1024], P(None, ('tp', 'fsdp'))
- wout_grad: float32 [1024, 1024], P('tp', 'fsdp')
- bout_grad: float32 [1024], P('fsdp')
- gain1_grad: float32 [1024], P('fsdp')
- shift1_grad: float32 [1024], P('fsdp')
- wfc_grad: float32 [1024, 4096], P('fsdp', 'tp')
- bfc_grad: float32 [4096], P(('tp', 'fsdp'))
- wproj_grad: float32 [4096, 1024], P('tp', 'fsdp')
- bproj_grad: float32 [1024], P('fsdp')
- gain2_grad: float32 [1024], P('fsdp')
- shift2_grad: float32 [1024], P('fsdp')
The draws below stay inside these ranges and needn't reach their ends.
Inputs may be any that keep to these rules, and one draw needn't show every extreme that they name: `segment_ids`: segment numbers never fall along a sequence, and each document has at most 512 positions.
All inputs are finite; a program needn't handle non-finite values.
Results may differ from the reference program's by a relative error of at most 0.02.
Values may be sent and summed in bfloat16 or wider, within the bound.
A program may use at most 128 MiB of HBM per device.

```python
import math
import jax
import jax.numpy as jnp
import numpy as np
from jax import lax

D = 1024
H = 16
HD = 64
FF = 4096
LEN = 1024
DOCS = 16
SEQS = 4


def spiked(array, rng, source, target, parts, factor):
    owner, partner = [(jnp.arange(array.shape[position]) // (array.shape[position] // parts)).reshape([-1 if axis == position else 1 for axis in range(array.ndim)]) for position in (source, target)]
    chosen = jax.random.permutation(rng, parts)[partner]
    strong = (owner == chosen) | (owner == (partner + parts // 2) % parts)
    return jnp.where(strong, factor * array, array)


def levels(rng, shape, pieces, low, high):
    loudness = 1.0
    for dim, blocks in pieces:
        draws = jax.random.uniform(jax.random.fold_in(jax.random.fold_in(rng, 6), dim), (blocks,), jnp.float32, low / len(pieces), high / len(pieces))
        loudness = loudness * jnp.repeat(jnp.exp(draws), shape[dim] // blocks).reshape((-1,) + (1,) * (len(shape) - 1 - dim))
    return loudness


def profile(amount, total, limit, skew):
    loads = [(1 << 20) // math.isqrt(rank ** skew) + 1 for rank in range(2, amount + 1)]
    surplus, given = total - limit - (amount - 1), [1] * (amount - 1)
    while surplus > 0:
        free = [i for i in range(amount - 1) if given[i] < limit]
        mass, remaining = sum([loads[i] for i in free]), surplus
        for i in free:
            more = min(limit - given[i], max(1, remaining * loads[i] // mass), surplus)
            given[i] = given[i] + more
            surplus = surplus - more
    return np.array([limit] + given)


def ragged_sizes(stream_key, amount, total, most, skew):
    if amount == 2:
        one = jax.random.randint(stream_key, (), max(1, total - most), min(most, total - 1) + 1)
        return jnp.stack([one, total - one])
    sizes = jnp.asarray(profile(amount, total, most, skew), jnp.int32)
    couples = (amount - 1) // 2
    donor, sink = sizes[1:1 + 2 * couples:2], sizes[2:2 + 2 * couples:2]
    slack = jnp.minimum(donor - 1, most - sink)
    passed = jax.random.randint(jax.random.fold_in(stream_key, 1), (couples,), 0, 1 << 20) % (slack + 1)
    sizes = sizes.at[1:1 + 2 * couples:2].set(donor - passed).at[2:2 + 2 * couples:2].set(sink + passed)
    return sizes[jax.random.permutation(jax.random.fold_in(stream_key, 2), amount)]


def bell_draw(stream_key, shape, scale, bound, split=(), kind=jnp.bfloat16):
    factor_of = levels(stream_key, shape, split, -0.22, 0.18) if split else 1.0
    values = jax.random.normal(stream_key, shape, jnp.float32) * scale * factor_of
    return jnp.minimum(jnp.maximum(values, -bound), bound).astype(kind)


def bell_draw_with(rng, shape, deviation, limit, cuts, heavy, dtype=jnp.bfloat16):
    drawn = deviation * jax.random.normal(rng, shape, jnp.float32)
    if cuts:
        drawn = drawn * levels(rng, shape, cuts, -0.22, 0.18)
    return jnp.clip(spiked(drawn, jax.random.fold_in(rng, 3), *heavy), -limit, limit).astype(dtype)


def setup_inputs(seed: int = 0) -> dict:
    key_list = jax.random.split(jax.random.key(seed), 16)
    block_input = bell_draw(key_list[0], (SEQS, LEN, D), 1.0, 6.0, ((0, 4), (1, 2)))
    segment_ids = jax.vmap(lambda own: jnp.searchsorted(jnp.cumsum(ragged_sizes(own, DOCS, LEN, LEN // 2, 2)), jnp.arange(LEN), side="right"))(jax.random.split(key_list[1], SEQS)).reshape((SEQS, LEN)).astype(jnp.int32)
    cotangent = bell_draw_with(key_list[2], (SEQS, LEN, D), 1.0, 6.0, ((0, 4), (1, 2)), (0, 2, 4, 2.0))
    qkv_weight = bell_draw(key_list[3], (D, 3, D), D ** -0.5, 0.1875, ((0, 4), (2, 4)), jnp.float32)
    qv_bias = bell_draw(key_list[4], (2, D), 0.5, 3.0, ((1, 16),), jnp.float32)
    out_weight = bell_draw(key_list[5], (D, D), (D // 8) ** -0.5, 0.5, ((0, 4), (1, 4)), jnp.float32)
    out_bias = bell_draw(key_list[6], (D,), 0.5, 3.0, ((0, 4),), jnp.float32)
    norm1_gain = jnp.clip(1.0 + 0.18 * jax.random.normal(key_list[7], (D,), jnp.float32), 0.1, 1.9)
    norm1_shift = bell_draw(key_list[8], (D,), 0.5, 3.0, ((0, 4),), jnp.float32)
    fc_weight = bell_draw(key_list[9], (D, FF), D ** -0.5, 0.1875, ((0, 4), (1, 4)), jnp.float32)
    fc_bias = bell_draw(key_list[10], (FF,), 0.5, 3.0, ((0, 16),), jnp.float32)
    proj_weight = bell_draw(key_list[11], (FF, D), FF ** -0.5, 0.09375, ((0, 4), (1, 4)), jnp.float32)
    proj_bias = bell_draw(key_list[12], (D,), 0.5, 3.0, ((0, 4),), jnp.float32)
    norm2_gain = jnp.clip(1.0 + 0.18 * jax.random.normal(key_list[13], (D,), jnp.float32), 0.1, 1.9)
    norm2_shift = bell_draw(key_list[14], (D,), 0.5, 3.0, ((0, 4),), jnp.float32)
    return {"block_input": block_input, "segment_ids": segment_ids, "cotangent": cotangent, "qkv_weight": qkv_weight, "qv_bias": qv_bias, "out_weight": out_weight, "out_bias": out_bias, "norm1_gain": norm1_gain, "norm1_shift": norm1_shift, "fc_weight": fc_weight, "fc_bias": fc_bias, "proj_weight": proj_weight, "proj_bias": proj_bias, "norm2_gain": norm2_gain, "norm2_shift": norm2_shift}


@jax.custom_vjp
def low(v):
    return lax.optimization_barrier(v.astype(jnp.bfloat16)).astype(jnp.float32)

@jax.custom_vjp
def low_back(v):
    return v

def low_keep(v):
    return (low(v), None)

def low_pass(kept, grad):
    return (grad,)

def back_keep(v):
    return (v, None)

def back_low(kept, grad):
    return (low(grad),)
low.defvjp(low_keep, low_pass)
low_back.defvjp(back_keep, back_low)
epsilon = 1e-05
highest = lax.Precision.HIGHEST

def layer_norm(values, gain, shift):
    centred = values - lax.optimization_barrier(jnp.mean(values, axis=-1, keepdims=True))
    spread = lax.optimization_barrier(jnp.mean(centred * centred, axis=-1, keepdims=True))
    return centred * lax.rsqrt(spread + epsilon) * gain + shift

def forward(inputs, seg_row, qkv_weight, qv_bias, out_weight, out_bias, norm1_gain, norm1_shift, fc_weight, fc_bias, proj_weight, proj_bias, norm2_gain, norm2_shift):
    normed_first = low(layer_norm(inputs, low(norm1_gain), low(norm1_shift)))
    projected = jnp.einsum('rd,dce->rce', normed_first, low(qkv_weight), precision=highest)
    bias_pair = low(qv_bias)
    queries = low(low_back(projected[:, 0] + bias_pair[0]))
    key_rows = low(low_back(projected[:, 1]))
    value_rows = low(low_back(projected[:, 2] + bias_pair[1]))
    query_heads = queries.reshape(LEN, H, HD)
    key_heads = key_rows.reshape(LEN, H, HD)
    value_heads = value_rows.reshape(LEN, H, HD)
    scores = jnp.einsum('qhe,khe->hqk', query_heads, key_heads, precision=highest) * HD ** (-0.5)
    scores = low_back(scores)
    places = jnp.arange(LEN)
    allowed = (places[None, :] <= places[:, None]) & (seg_row[:, None] == seg_row[None, :])
    masked = jnp.where(allowed[None], scores, -1e+30)
    attn_probs = jax.nn.softmax(masked, axis=-1)
    attended = jnp.einsum('hqk,khe->qhe', low(attn_probs), value_heads, precision=highest)
    attended = low(low_back(attended.reshape(LEN, D)))
    branch = jnp.dot(attended, low(out_weight), precision=highest) + low(out_bias)
    middle = inputs + low_back(branch)
    normed_second = low(layer_norm(middle, low(norm2_gain), low(norm2_shift)))
    pre_act = low_back(jnp.dot(normed_second, low(fc_weight), precision=highest) + low(fc_bias))
    act_low = low(jax.nn.gelu(pre_act, approximate=True))
    feed = jnp.dot(act_low, low(proj_weight), precision=highest) + low(proj_bias)
    return middle + low_back(feed)

def reference(block_input, segment_ids, cotangent, qkv_weight, qv_bias, out_weight, out_bias, norm1_gain, norm1_shift, fc_weight, fc_bias, proj_weight, proj_bias, norm2_gain, norm2_shift):
    params = (qkv_weight, qv_bias, out_weight, out_bias, norm1_gain, norm1_shift, fc_weight, fc_bias, proj_weight, proj_bias, norm2_gain, norm2_shift)

    def one_sequence(carry, packed):
        seq_input, seg_row, seq_cot = packed

        def apply_block(inputs, *weights):
            return forward(inputs, seg_row, *weights)
        result, pull = jax.vjp(apply_block, seq_input.astype(jnp.float32), *params)
        grads = pull(seq_cot.astype(jnp.float32))
        summed = tuple((total + grad for total, grad in zip(carry, grads[1:])))
        return (summed, (result.astype(jnp.bfloat16), grads[0].astype(jnp.bfloat16)))
    start = tuple((jnp.zeros_like(weight) for weight in params))
    totals, (outputs, in_grads) = lax.scan(one_sequence, start, (block_input, segment_ids, cotangent))
    return (outputs, in_grads, totals[0], totals[1], totals[2], totals[3], totals[4], totals[5], totals[6], totals[7], totals[8], totals[9], totals[10], totals[11])
```

```python
import functools

import jax
import jax.numpy as jnp
from jax import lax
from jax.experimental import pallas as pl
from jax.experimental.pallas import tpu as pltpu
from jax.sharding import PartitionSpec as P

HD = 64


epsilon = 1e-05


def layer_norm(values, gain, shift):
    centred = values - jnp.mean(values, axis=-1, keepdims=True)
    spread = jnp.mean(centred * centred, axis=-1, keepdims=True)
    return centred * lax.rsqrt(spread + epsilon) * gain + shift


def gelu_act(values):
    return jax.nn.gelu(values, approximate=True)


def on_device(
    block_input,
    segment_ids,
    cotangent,
    qkv_weight,
    qv_bias,
    out_weight,
    out_bias,
    norm1_gain,
    norm1_shift,
    fc_weight,
    fc_bias,
    proj_weight,
    proj_bias,
    norm2_gain,
    norm2_shift,
):
    half = jnp.bfloat16
    single = jnp.float32
    seqs_here, rows_seq, model_width = block_input.shape
    row_count = seqs_here * rows_seq
    shard_index = lax.axis_index("ctx")
    scale_factor = HD ** (-0.5)
    (
        wqkv_low,
        bqv_low,
        wout_low,
        bout_low,
        gain1_low,
        shift1_low,
        wfc_low,
        bfc_low,
        wproj_low,
        bproj_low,
        gain2_low,
        shift2_low,
    ) = (
        lax.all_gather(qkv_weight.astype(half), "fsdp", axis=0, tiled=True),
        lax.all_gather(qv_bias.astype(half), "fsdp", axis=1, tiled=True),
        lax.all_gather(out_weight.astype(half), "fsdp", axis=1, tiled=True),
        lax.all_gather(out_bias.astype(half), "fsdp", axis=0, tiled=True),
        lax.all_gather(norm1_gain.astype(half), "fsdp", axis=0, tiled=True),
        lax.all_gather(norm1_shift.astype(half), "fsdp", axis=0, tiled=True),
        lax.all_gather(fc_weight.astype(half), "fsdp", axis=0, tiled=True),
        lax.all_gather(fc_bias.astype(half), "fsdp", axis=0, tiled=True),
        lax.all_gather(proj_weight.astype(half), "fsdp", axis=1, tiled=True),
        lax.all_gather(proj_bias.astype(half), "fsdp", axis=0, tiled=True),
        lax.all_gather(norm2_gain.astype(half), "fsdp", axis=0, tiled=True),
        lax.all_gather(norm2_shift.astype(half), "fsdp", axis=0, tiled=True),
    )
    gain_first = gain1_low.astype(single)
    shift_first = shift1_low.astype(single)
    gain_second = gain2_low.astype(single)
    shift_second = shift2_low.astype(single)
    inputs = block_input.reshape(row_count, model_width).astype(single)
    normed_first = layer_norm(inputs, gain_first, shift_first).astype(half)
    projected = jnp.einsum("rd,dce->rce", normed_first, wqkv_low, preferred_element_type=single)
    bias_pair = bqv_low.astype(single)
    queries = (projected[:, 0] + bias_pair[0]).astype(half)
    key_rows = projected[:, 1].astype(half)
    value_rows = (projected[:, 2] + bias_pair[1]).astype(half)
    local_width = queries.shape[1]
    head_count = local_width // HD
    keys_all, values_all = (
        lax.all_gather(
            key_rows.reshape(seqs_here, rows_seq, local_width), "ctx", axis=1, tiled=True
        ),
        lax.all_gather(
            value_rows.reshape(seqs_here, rows_seq, local_width), "ctx", axis=1, tiled=True
        ),
    )
    length = keys_all.shape[1]
    query_pos = shard_index * rows_seq + jnp.arange(rows_seq)
    key_pos = jnp.arange(length)
    seg_query = lax.dynamic_slice_in_dim(segment_ids, shard_index * rows_seq, rows_seq, 1)
    query_heads = queries.reshape(seqs_here, rows_seq, head_count, HD)
    key_heads = keys_all.reshape(seqs_here, length, head_count, HD)
    value_heads = values_all.reshape(seqs_here, length, head_count, HD)

    def masked_scores(query_blk, key_blk, seg_row, seg_here):
        raw = (
            jnp.einsum("qhe,khe->hqk", query_blk, key_blk, preferred_element_type=single)
            * scale_factor
        )
        allowed = (key_pos[None, :] <= query_pos[:, None]) & (seg_here[:, None] == seg_row[None, :])
        return jnp.where(allowed[None], raw, -1e30)

    def attend(packed):
        query_blk, key_blk, value_blk, seg_row, seg_here = packed
        masked = masked_scores(query_blk, key_blk, seg_row, seg_here)
        row_max = jnp.max(masked, axis=-1, keepdims=True)
        expo = jnp.exp(masked - row_max)
        row_total = jnp.sum(expo, axis=-1, keepdims=True)
        probs_low = (expo / row_total).astype(half)
        attended = jnp.einsum("hqk,khe->qhe", probs_low, value_blk, preferred_element_type=single)
        return (attended.astype(half), row_max + jnp.log(row_total))

    attended, log_total = lax.map(
        attend, (query_heads, key_heads, value_heads, segment_ids, seg_query)
    )
    attended_rows = attended.reshape(row_count, local_width)
    attn_partial = jnp.dot(attended_rows, wout_low, preferred_element_type=single)
    attn_total = lax.psum(attn_partial.astype(jnp.bfloat16), "tp").astype(jnp.float32)
    middle = inputs + attn_total + bout_low.astype(single)
    normed_second = layer_norm(middle, gain_second, shift_second).astype(half)
    pre_act = jnp.dot(normed_second, wfc_low, preferred_element_type=single) + bfc_low.astype(
        single
    )
    act_low = gelu_act(pre_act).astype(half)
    mlp_total = lax.psum(
        jnp.dot(act_low, wproj_low, preferred_element_type=single).astype(jnp.bfloat16), "tp"
    ).astype(jnp.float32)
    out_rows = (middle + mlp_total + bproj_low.astype(single)).astype(half)
    wqkv_use, wout_use, wfc_use, wproj_use = (
        lax.all_gather(qkv_weight.astype(half), "fsdp", axis=0, tiled=True),
        lax.all_gather(out_weight.astype(half), "fsdp", axis=1, tiled=True),
        lax.all_gather(fc_weight.astype(half), "fsdp", axis=0, tiled=True),
        lax.all_gather(proj_weight.astype(half), "fsdp", axis=1, tiled=True),
    )
    grad_out = cotangent.reshape(row_count, model_width).astype(single)
    grad_out_low = cotangent.reshape(row_count, model_width)
    grad_bproj = jnp.sum(grad_out_low, axis=0, dtype=single)
    grad_wproj = jnp.einsum("rf,rd->fd", act_low, grad_out_low, preferred_element_type=single)
    grad_act = jnp.einsum("rd,fd->rf", grad_out_low, wproj_use, preferred_element_type=single)
    gelu_unused, gelu_pull = jax.vjp(gelu_act, pre_act)
    grad_pre = gelu_pull(grad_act)[0].astype(half)
    grad_bfc = jnp.sum(grad_pre, axis=0, dtype=single)
    grad_wfc = jnp.einsum("rd,rf->df", normed_second, grad_pre, preferred_element_type=single)
    norm2_partial = jnp.einsum("rf,df->rd", grad_pre, wfc_use, preferred_element_type=single)
    grad_norm2 = lax.psum(norm2_partial.astype(jnp.bfloat16), "tp").astype(jnp.float32)
    norm_unused, second_pull = jax.vjp(layer_norm, middle, gain_second, shift_second)
    grad_mid_ln, grad_gain2, grad_shift2 = second_pull(grad_norm2)
    grad_middle = grad_out + grad_mid_ln
    grad_mid_low = grad_middle.astype(half)
    grad_bout = jnp.sum(grad_mid_low, axis=0, dtype=single)
    grad_wout = jnp.einsum("rk,rd->kd", attended_rows, grad_mid_low, preferred_element_type=single)
    grad_att = jnp.einsum(
        "rd,kd->rk", grad_mid_low, wout_use, preferred_element_type=single
    ).astype(half)
    grad_att_heads = grad_att.reshape(seqs_here, rows_seq, head_count, HD)

    def attend_back(packed):
        query_blk, key_blk, value_blk, seg_row, seg_here, log_blk, grad_blk = packed
        masked = masked_scores(query_blk, key_blk, seg_row, seg_here)
        attn_probs = jnp.exp(masked - log_blk)
        probs_low = attn_probs.astype(half)
        grad_value = jnp.einsum("hqk,qhe->khe", probs_low, grad_blk, preferred_element_type=single)
        grad_probs = jnp.einsum("qhe,khe->hqk", grad_blk, value_blk, preferred_element_type=single)
        row_delta = jnp.sum(grad_probs * attn_probs, axis=-1, keepdims=True)
        grad_scores = (attn_probs * (grad_probs - row_delta)).astype(half)
        grad_query = (
            jnp.einsum("hqk,khe->qhe", grad_scores, key_blk, preferred_element_type=single)
            * scale_factor
        )
        grad_key = (
            jnp.einsum("hqk,qhe->khe", grad_scores, query_blk, preferred_element_type=single)
            * scale_factor
        )
        return (grad_query.astype(half), grad_key, grad_value)

    grad_query, grad_key, grad_value = lax.map(
        attend_back,
        (query_heads, key_heads, value_heads, segment_ids, seg_query, log_total, grad_att_heads),
    )
    grad_key, grad_value = (
        lax.psum_scatter(
            grad_key.reshape(seqs_here, length, local_width).astype(jnp.bfloat16),
            "ctx",
            scatter_dimension=1,
            tiled=True,
        ).astype(jnp.float32),
        lax.psum_scatter(
            grad_value.reshape(seqs_here, length, local_width).astype(jnp.bfloat16),
            "ctx",
            scatter_dimension=1,
            tiled=True,
        ).astype(jnp.float32),
    )
    grad_query = grad_query.reshape(row_count, local_width)
    grad_key = grad_key.reshape(row_count, local_width).astype(half)
    grad_value = grad_value.reshape(row_count, local_width).astype(half)
    grad_qkv = jnp.stack([grad_query, grad_key, grad_value], axis=1)
    grad_bqv = jnp.stack(
        [jnp.sum(grad_query, axis=0, dtype=single), jnp.sum(grad_value, axis=0, dtype=single)]
    )
    grad_wqkv = jnp.einsum("rd,rce->dce", normed_first, grad_qkv, preferred_element_type=single)
    norm1_partial = jnp.einsum("rce,dce->rd", grad_qkv, wqkv_use, preferred_element_type=single)
    grad_norm1 = lax.psum(norm1_partial.astype(jnp.bfloat16), "tp").astype(jnp.float32)
    first_unused, first_pull = jax.vjp(layer_norm, inputs, gain_first, shift_first)
    grad_in_ln, grad_gain1, grad_shift1 = first_pull(grad_norm1)
    input_rows = (grad_middle + grad_in_ln).astype(half)
    block_output = out_rows.reshape(block_input.shape)
    input_grad = input_rows.reshape(block_input.shape)
    (
        sum_wqkv,
        sum_bqv,
        sum_wout,
        sum_bout,
        sum_gain1,
        sum_shift1,
        sum_wfc,
        sum_bfc,
        sum_wproj,
        sum_bproj,
        sum_gain2,
        sum_shift2,
    ) = (
        lax.psum_scatter(grad_wqkv, ("fsdp", "ctx"), scatter_dimension=0, tiled=True),
        lax.psum_scatter(grad_bqv, ("fsdp", "ctx"), scatter_dimension=1, tiled=True),
        lax.psum_scatter(grad_wout, ("fsdp", "ctx"), scatter_dimension=1, tiled=True),
        lax.psum_scatter(grad_bout, ("fsdp", "ctx"), scatter_dimension=0, tiled=True),
        lax.psum_scatter(grad_gain1, ("fsdp", "ctx"), scatter_dimension=0, tiled=True),
        lax.psum_scatter(grad_shift1, ("fsdp", "ctx"), scatter_dimension=0, tiled=True),
        lax.psum_scatter(grad_wfc, ("fsdp", "ctx"), scatter_dimension=0, tiled=True),
        lax.psum_scatter(grad_bfc, ("fsdp", "ctx"), scatter_dimension=0, tiled=True),
        lax.psum_scatter(grad_wproj, ("fsdp", "ctx"), scatter_dimension=1, tiled=True),
        lax.psum_scatter(grad_bproj, ("fsdp", "ctx"), scatter_dimension=0, tiled=True),
        lax.psum_scatter(grad_gain2, ("fsdp", "ctx"), scatter_dimension=0, tiled=True),
        lax.psum_scatter(grad_shift2, ("fsdp", "ctx"), scatter_dimension=0, tiled=True),
    )
    (
        final_wqkv,
        final_bqv,
        final_wout,
        final_bout,
        final_gain1,
        final_shift1,
        final_wfc,
        final_bfc,
        final_wproj,
        final_bproj,
        final_gain2,
        final_shift2,
    ) = (
        lax.all_gather(sum_wqkv.astype(jnp.bfloat16), "ctx", axis=0, tiled=True).astype(
            sum_wqkv.dtype
        ),
        lax.all_gather(sum_bqv.astype(jnp.bfloat16), "ctx", axis=1, tiled=True).astype(
            sum_bqv.dtype
        ),
        lax.all_gather(sum_wout.astype(jnp.bfloat16), "ctx", axis=1, tiled=True).astype(
            sum_wout.dtype
        ),
        lax.all_gather(sum_bout.astype(jnp.bfloat16), "ctx", axis=0, tiled=True).astype(
            sum_bout.dtype
        ),
        lax.all_gather(sum_gain1.astype(jnp.bfloat16), "ctx", axis=0, tiled=True).astype(
            sum_gain1.dtype
        ),
        lax.all_gather(sum_shift1.astype(jnp.bfloat16), "ctx", axis=0, tiled=True).astype(
            sum_shift1.dtype
        ),
        lax.all_gather(sum_wfc.astype(jnp.bfloat16), "ctx", axis=0, tiled=True).astype(
            sum_wfc.dtype
        ),
        lax.all_gather(sum_bfc.astype(jnp.bfloat16), "ctx", axis=0, tiled=True).astype(
            sum_bfc.dtype
        ),
        lax.all_gather(sum_wproj.astype(jnp.bfloat16), "ctx", axis=1, tiled=True).astype(
            sum_wproj.dtype
        ),
        lax.all_gather(sum_bproj.astype(jnp.bfloat16), "ctx", axis=0, tiled=True).astype(
            sum_bproj.dtype
        ),
        lax.all_gather(sum_gain2.astype(jnp.bfloat16), "ctx", axis=0, tiled=True).astype(
            sum_gain2.dtype
        ),
        lax.all_gather(sum_shift2.astype(jnp.bfloat16), "ctx", axis=0, tiled=True).astype(
            sum_shift2.dtype
        ),
    )
    return (
        block_output,
        input_grad,
        final_wqkv,
        final_bqv,
        final_wout,
        final_bout,
        final_gain1,
        final_shift1,
        final_wfc,
        final_bfc,
        final_wproj,
        final_bproj,
        final_gain2,
        final_shift2,
    )


MESH = pl.DeviceIdType.MESH


def dot_nn(left, right):
    return lax.dot_general(
        left, right, (((1,), (0,)), ((), ())), preferred_element_type=jnp.float32
    )


def dot_nt(left, right):
    return lax.dot_general(
        left, right, (((1,), (1,)), ((), ())), preferred_element_type=jnp.float32
    )


def by_rows(rows, step, body):
    def one(index, carry):
        body(pl.multiple_of(index * step, step))
        return carry

    lax.fori_loop(0, rows // step, one, 0)


def norm_parts(values):
    centred = values - jnp.mean(values, axis=-1, keepdims=True)
    spread = jnp.mean(centred * centred, axis=-1, keepdims=True)
    return centred, lax.rsqrt(spread + epsilon)


def norm_back(values, incoming, gain):
    centred, rate = norm_parts(values)
    hat = centred * rate
    scaled = incoming * gain
    by_value = rate * (
        scaled
        - jnp.mean(scaled, axis=-1, keepdims=True)
        - hat * jnp.mean(scaled * hat, axis=-1, keepdims=True)
    )
    return (
        by_value,
        jnp.sum(incoming * hat, axis=0, keepdims=True),
        jnp.sum(incoming, axis=0, keepdims=True),
    )


def block_kernel(
    nz,
    x_in,
    dy_in,
    seg_row,
    seg_col,
    wqkv_in,
    wout_in,
    wfc_in,
    wproj_in,
    vec_in,
    out_ref,
    grad_ref,
    gqkv_ref,
    gout_ref,
    gfc_ref,
    gproj_ref,
    gvec_ref,
    xr,
    dyb,
    nf,
    wq,
    wo,
    wf,
    wp,
    vec,
    full,
    fcb,
    qb,
    kb,
    vb,
    p0,
    p1,
    p2,
    p3,
    ao,
    ax,
    srs,
    rrs,
    own,
    mid,
    ns,
    gm,
    act,
    gp,
    turned,
    gsq,
    gso,
    gsf,
    gsp,
    grq,
    gro,
    grf,
    grp,
    xq,
    xo,
    xf,
    xp_,
    gt,
    gts,
    dkb,
    dvb,
    dqkv,
    dx,
    wide,
    wide2,
    dsb,
    gmid,
    sv,
    svall,
    s2,
    s2r,
    send_sem,
    recv_sem,
):
    half = jnp.bfloat16
    single = jnp.float32
    z = lax.axis_index("fsdp")
    x = lax.axis_index("ctx")
    t = lax.axis_index("tp")
    y = t // 2
    c = t % 2
    quarter = x_in.shape[0] // 2
    block = quarter // 2
    width = x_in.shape[1]
    dz = width // nz
    fch = wf.shape[3]
    ec = qb.shape[1]
    length = qb.shape[0]
    probs = (p0, p1, p2, p3)
    sib = (z, x, y * 2 + 1 - c)
    ynb = (z, x, (1 - y) * 2 + c)
    xnb = (z, 1 - x, t)
    dia = (z, 1 - x, (1 - y) * 2 + c)
    started = []

    def send(src, dst, dev):
        slot = len(started)
        copy = pltpu.make_async_remote_copy(
            src_ref=src,
            dst_ref=dst,
            send_sem=send_sem.at[slot],
            recv_sem=recv_sem.at[slot],
            device_id=dev,
            device_id_type=MESH,
        )
        copy.start()
        started.append(copy)
        return copy

    def arrived(copies):
        for copy in copies:
            copy.wait_recv()

    def zdev(step):
        return ((z + step) % nz, x, t)

    peers = [(z, px, pt) for px in (x, 1 - x) for pt in (t, sib[2], ynb[2], (1 - y) * 2 + 1 - c)][
        1:
    ]
    for step in range(1, nz):
        peers += [((z + step) % nz, x, t), ((z + step) % nz, x, sib[2])]
    barrier = pltpu.get_barrier_semaphore()
    for dev in peers:
        pl.semaphore_signal(barrier, inc=1, device_id=dev, device_id_type=MESH)

    by_rows(
        dz,
        64,
        lambda r: [
            wq.__setitem__(
                (c, z, pl.ds(r, 64), pl.ds(j * ec, ec)),
                wqkv_in[
                    pl.ds(r, 64), pl.ds(pl.multiple_of(j * 2 * ec + x * ec, ec), ec)
                ].astype(half),
            )
            for j in range(3)
        ]
        and None,
    )
    by_rows(
        ec,
        64,
        lambda r: wo.__setitem__(
            (c, z, pl.ds(r, 64)), wout_in[pl.ds(pl.multiple_of(x * ec + r, 64), 64)].astype(half)
        ),
    )
    by_rows(
        dz,
        64,
        lambda r: wf.__setitem__(
            (c, z, pl.ds(r, 64)),
            wfc_in[pl.ds(r, 64), pl.ds(pl.multiple_of(x * fch, fch), fch)].astype(half),
        ),
    )
    by_rows(
        fch,
        64,
        lambda r: wp.__setitem__(
            (c, z, pl.ds(r, 64)), wproj_in[pl.ds(pl.multiple_of(x * fch + r, 64), 64)].astype(half)
        ),
    )
    vec[c, z] = vec_in[...].astype(half).astype(single)
    pl.semaphore_wait(barrier, len(peers))

    x_copy = send(x_in.at[pl.ds(c * quarter, quarter)], xr.at[c], xnb)
    vec_copies = [send(vec.at[c, z], vec.at[c, z], sib)]
    for step in range(1, nz):
        for dev_t in (t, sib[2]):
            vec_copies.append(send(vec.at[c, z], vec.at[c, z], ((z + step) % nz, x, dev_t)))
    weight_z = []
    weight_sib = []
    for wide_ref in (wq, wo, wf, wp):
        weight_z.append(
            [send(wide_ref.at[c, z], wide_ref.at[c, z], zdev(step)) for step in range(1, nz)]
        )
    for wide_ref in (wq, wo, wf, wp):
        weight_sib.append([send(wide_ref.at[c, z], wide_ref.at[c, z], sib)])

    def weight_forward(which):
        wide_ref = (wq, wo, wf, wp)[which]
        for step, copy in zip(range(1, nz), weight_z[which]):
            copy.wait_recv()
            came = (z + nz - step) % nz
            weight_sib[which].append(send(wide_ref.at[c, came], wide_ref.at[c, came], sib))

    dy_copy = send(dy_in.at[pl.ds(c * quarter, quarter)], dyb.at[c, x], xnb)
    for s in range(2):
        dyb[s, x] = dy_in[s * quarter : (s + 1) * quarter]

    arrived(vec_copies)
    for piece in range(nz):
        full[:, piece * dz : (piece + 1) * dz] = vec[c, piece]
    pieces = nz // 2
    for h in range(2):
        for k in range(pieces):
            fcb[h : h + 1, k * dz : (k + 1) * dz] = vec[h, x * pieces + k][6:7]
    lane = lax.broadcasted_iota(jnp.int32, (1, ec), 1)
    low_lane = lane < HD
    first_piece = vec[c, x * pieces][7:8, 0:ec]
    next_piece = vec[c, x * pieces + 1][7:8, 0:ec]
    q_bias = jnp.where(low_lane, first_piece, pltpu.roll(next_piece, HD, 1))
    v_bias = jnp.where(low_lane, pltpu.roll(first_piece, HD, 1), next_piece)
    out_bias = full[0:1]
    gain1, shift1 = full[1:2], full[2:3]
    gain2, shift2 = full[3:4], full[4:5]
    proj_bias = full[5:6]

    def first_norm(src, dst):
        def rows(r):
            centred, rate = norm_parts(src[pl.ds(r, 32)].astype(single))
            dst[pl.ds(r, 32)] = (centred * rate * gain1 + shift1).astype(half)

        by_rows(quarter, 32, rows)

    for s in range(2):
        first_norm(x_in.at[pl.ds(s * quarter, quarter)], nf.at[x, s])
    x_copy.wait_recv()
    x_fwd = send(xr.at[c], xr.at[c], sib)
    first_norm(xr.at[c], nf.at[1 - x, c])
    x_fwd.wait_recv()
    first_norm(xr.at[1 - c], nf.at[1 - x, 1 - c])

    arrived([])
    weight_forward(0)
    for xi in range(2):
        for ci in range(2):
            rows_nf = nf[xi, ci]
            proj = dot_nn(rows_nf, wq[c].reshape(width, 3 * ec))
            at = pl.ds((xi * 2 + ci) * quarter, quarter)
            qb[at] = (proj[:, 0:ec] + q_bias).astype(half)
            kb[at] = proj[:, ec : 2 * ec].astype(half)
            vb[at] = (proj[:, 2 * ec :] + v_bias).astype(half)

    dy_copy.wait_recv()
    dy_fwd = send(dyb.at[c, 1 - x], dyb.at[c, 1 - x], sib)

    head_lane = lax.broadcasted_iota(jnp.int32, (1, ec), 1) // HD
    n_blocks = length // quarter
    heads = ec // HD

    def only(values, h):
        return jnp.where(head_lane == h, values, jnp.zeros_like(values))

    for i in range(n_blocks):
        j0 = max(0, i - 2)
        span = (i + 1 - j0) * quarter
        keys = pl.ds(j0 * quarter, span)
        total = None
        for h in range(heads):
            q_h = only(qb[pl.ds(i * quarter, quarter)], h) * jnp.asarray(HD**-0.5, half)
            wide[:, 0:span] = dot_nt(q_h, kb[keys])

            def soft(r, h=h, i=i, j0=j0, span=span):
                scores = wide[pl.ds(r, 32), 0:span]
                q_at = i * quarter + r + lax.broadcasted_iota(jnp.int32, (32, span), 0)
                k_at = j0 * quarter + lax.broadcasted_iota(jnp.int32, (32, span), 1)
                seg_q = seg_col[pl.ds(pl.multiple_of(i * quarter + r, 32), 32)]
                seg_k = seg_row[:, j0 * quarter : j0 * quarter + span]
                allowed = (k_at <= q_at) & (seg_q == seg_k)
                masked = jnp.where(allowed, scores, -1e30)
                expo = jnp.exp(masked - jnp.max(masked, axis=-1, keepdims=True))
                share = expo / jnp.sum(expo, axis=-1, keepdims=True)
                probs[i][h, pl.ds(r, 32)] = share.astype(half)

            by_rows(quarter, 32, soft)
            part = dot_nn(probs[i][h], only(vb[keys], h))
            total = part if total is None else total + part
        ao[i // 2, i % 2] = total.astype(half)

    att_copy = send(ao.at[:, 1 - c], ax.at[c], sib)
    ax[c] = ao[:, c]
    weight_forward(1)
    arrived(weight_sib[1])
    att_copy.wait_recv()

    def spread_sum(k, part):
        copies = []
        for turn, xt in ((0, 1 - x), (1, x)):

            def columns(piece, carry, turn=turn, xt=xt):
                value = part(xt, piece)
                at = pl.ds(pl.multiple_of(piece * dz, dz), dz)
                for yi in range(2):
                    rows = value[yi * block : (yi + 1) * block]
                    srs[k, turn, yi, :, at] = rows.astype(half)
                    if turn:
                        own[k % 2, yi, :, at] = rows
                return carry

            lax.fori_loop(0, nz, columns, 0)
            if turn == 0:
                copies.append(send(srs.at[k, 0, 1 - y], rrs.at[k, 0], dia))
                copies.append(send(srs.at[k, 0, y], rrs.at[k, 1], xnb))
            else:
                copies.append(send(srs.at[k, 1, 1 - y], rrs.at[k, 2], ynb))
        return copies

    def summed(k, at):
        value = own[k % 2, y, at]
        for slot in range(3):
            value = value + rrs[k, slot, at].astype(single)
        return value

    def attention_out(xt, piece):
        return dot_nn(ax[0, xt], wo[0, piece]) + dot_nn(ax[1, xt], wo[1, piece])

    copies = spread_sum(0, attention_out)

    dy_fwd.wait_recv()
    arrived(copies)

    my_x = x_in.at[pl.ds(pl.multiple_of(c * quarter + y * block, block), block)]

    def middle_rows(r):
        at = pl.ds(r, 16)
        value = my_x[at].astype(single) + (summed(0, at) + out_bias)
        mid[at] = value
        centred, rate = norm_parts(value)
        ns[c, x, y, at] = (centred * rate * gain2 + shift2).astype(half)

    by_rows(block, 16, middle_rows)

    def plane_gather(buf):
        mine = buf.at[c, x, y]
        return [
            send(mine, mine, dia),
            send(mine, mine, xnb),
            send(mine, mine, ynb),
            send(mine, mine, sib),
        ]

    copies = plane_gather(ns)
    weight_forward(2)
    arrived(weight_sib[2])
    weight_forward(3)
    arrived(weight_sib[3])

    ns_sib = [copies[3]]

    def hidden(xt):
        rows_ns = ns[c, xt].reshape(quarter, width)
        for h in range(2):
            wide[:, 0:fch] = dot_nn(rows_ns, wf[h].reshape(width, fch))
            grad = None
            for piece in range(nz):
                part = dot_nt(
                    dyb[c, xt, :, piece * dz : (piece + 1) * dz],
                    wp[h, piece],
                )
                grad = part if grad is None else grad + part
            wide2[:, 0:fch] = grad

            def rows(r, h=h):
                value = wide[pl.ds(r, 32), 0:fch] + fcb[h : h + 1]
                root = 0.7978845608028654
                square = value * value
                inner = jnp.tanh(root * (value + 0.044715 * (square * value)))
                lift = 0.5 * (1.0 + inner)
                slope = lift + 0.5 * value * (1.0 - inner * inner) * (
                    root * (1.0 + 3.0 * 0.044715 * square)
                )
                at = pl.ds(pl.multiple_of(xt * quarter + r, 32), 32)
                act[c, h, at] = (value * lift).astype(half)
                gp[c, h, at] = (wide2[pl.ds(r, 32), 0:fch] * slope).astype(half)

            by_rows(quarter, 32, rows)

    copies[2].wait_recv()
    ns_sib.append(send(ns.at[c, x, 1 - y], ns.at[c, x, 1 - y], sib))
    hidden(x)
    copies[1].wait_recv()
    ns_sib.append(send(ns.at[c, 1 - x, y], ns.at[c, 1 - x, y], sib))
    copies[0].wait_recv()
    ns_sib.append(send(ns.at[c, 1 - x, 1 - y], ns.at[c, 1 - x, 1 - y], sib))
    hidden(1 - x)

    act_copy = send(act.at[c, 1 - c], act.at[c, 1 - c], sib)
    gp_copy = send(gp.at[c, 1 - c], gp.at[c, 1 - c], sib)

    def norm2_part(xt, piece):
        at = pl.ds(pl.multiple_of(xt * quarter, quarter), quarter)
        return dot_nt(gp[c, 0, at], wf[0, piece]) + dot_nt(gp[c, 1, at], wf[1, piece])

    copies = spread_sum(1, norm2_part)

    def weight_grad(left, right_at, out, home):
        def one(step, carry):
            piece = (z + step) % nz
            at = pl.ds(pl.multiple_of(piece * dz, dz), dz)
            out[piece] = dot_nn(turned[0:left], right_at(at)).astype(half)
            return carry

        lax.fori_loop(0, nz, one, 0)
        return [
            send(out.at[(z + step) % nz], home.at[z], zdev(step)) for step in range(1, nz)
        ]

    def turn_rows(src, left, column):
        turned[0:left, pl.ds(pl.multiple_of(column, quarter), quarter)] = src.T

    act_copy.wait_recv()
    for s in range(2):
        for k in range(2):
            turn_rows(
                act[s, c, k * quarter : (k + 1) * quarter], fch, (s * 2 + k) * quarter
            )
    proj_z = weight_grad(
        fch, lambda at: dyb[:, :, :, at].reshape(length, dz), gsp, grp
    )

    gp_copy.wait_recv()
    arrived(ns_sib)
    for s in range(2):
        for k in range(2):
            turn_rows(gp[s, c, k * quarter : (k + 1) * quarter], fch, (s * 2 + k) * quarter)
    fc_z = weight_grad(fch, lambda at: ns[:, :, :, :, at].reshape(length, dz), gsf, grf)

    sv[...] = jnp.zeros_like(sv)
    for s in range(2):
        sv[6:7, 0:fch] += jnp.sum(gp[s, c].astype(single), axis=0, keepdims=True)

    arrived(copies)
    my_dy = dyb.at[c, x, pl.ds(pl.multiple_of(y * block, block), block)]

    def middle_back(r):
        at = pl.ds(r, 16)
        grad_rows = my_dy[at].astype(single)
        by_value, gain_part, shift_part = norm_back(mid[at], summed(1, at), gain2)
        grad = grad_rows + by_value
        gmid[at] = grad
        low = grad.astype(half)
        gm[c, x, y, at] = low
        sv[3:4] += gain_part
        sv[4:5] += shift_part
        sv[0:1] += jnp.sum(low.astype(single), axis=0, keepdims=True)
        sv[5:6] += jnp.sum(grad_rows, axis=0, keepdims=True)

    by_rows(block, 16, middle_back)

    copies = plane_gather(gm)
    gm_sib = [copies[3]]

    def grad_attended(xt):
        at = pl.ds(pl.multiple_of(xt * quarter, quarter), quarter)
        rows_gm = gm[c, xt].reshape(quarter, width)
        for mine in (0, 1):
            h = c if mine else 1 - c
            total = None
            for piece in range(nz):
                part = dot_nt(rows_gm[:, piece * dz : (piece + 1) * dz], wo[h, piece])
                total = part if total is None else total + part
            if mine:
                gt[c, at] = total.astype(half)
            else:
                gts[at] = total.astype(half)

    copies[2].wait_recv()
    gm_sib.append(send(gm.at[c, x, 1 - y], gm.at[c, x, 1 - y], sib))
    grad_attended(x)
    copies[1].wait_recv()
    gm_sib.append(send(gm.at[c, 1 - x, y], gm.at[c, 1 - x, y], sib))
    copies[0].wait_recv()
    gm_sib.append(send(gm.at[c, 1 - x, 1 - y], gm.at[c, 1 - x, 1 - y], sib))
    grad_attended(1 - x)
    gt_copy = send(gts, gt.at[c], sib)

    def feed_part(xt, piece):
        at = pl.ds(pl.multiple_of(xt * quarter, quarter), quarter)
        return dot_nn(act[c, 0, at], wp[0, piece]) + dot_nn(act[c, 1, at], wp[1, piece])

    feed_copies = spread_sum(2, feed_part)
    gt_copy.wait_recv()

    dkb[...] = jnp.zeros_like(dkb)
    dvb[...] = jnp.zeros_like(dvb)
    for i in range(n_blocks):
        j0 = max(0, i - 2)
        span = (i + 1 - j0) * quarter
        keys = pl.ds(j0 * quarter, span)
        total = None
        for h in range(heads):
            ga = only(gt[i % 2, (i // 2) * quarter : (i // 2 + 1) * quarter], h)
            wide[:, 0:span] = dot_nt(ga, vb[keys])

            def back(r, h=h, i=i, span=span):
                grad_p = wide[pl.ds(r, 32), 0:span]
                share = probs[i][h, pl.ds(r, 32)].astype(single)
                delta = jnp.sum(grad_p * share, axis=-1, keepdims=True)
                dsb[pl.ds(r, 32), 0:span] = (share * (grad_p - delta)).astype(half)

            by_rows(quarter, 32, back)
            grad_s = dsb[:, 0:span]
            part = dot_nn(grad_s, only(kb[keys], h))
            total = part if total is None else total + part
            dkb[keys] += dot_nn(grad_s.T, only(qb[pl.ds(i * quarter, quarter)], h))
            dvb[keys] += dot_nn(probs[i][h].T, ga)
        dqkv[i // 2, i % 2, :, 0:ec] = (total * HD**-0.5).astype(half)
    for i in range(n_blocks):
        at = pl.ds(i * quarter, quarter)
        dqkv[i // 2, i % 2, :, ec : 2 * ec] = (dkb[at] * HD**-0.5).astype(half)
        dqkv[i // 2, i % 2, :, 2 * ec :] = dvb[at].astype(half)

    dx_copy = send(dqkv.at[:, 1 - c], dx.at[c], sib)
    dx[c] = dqkv[:, c]
    for i in range(n_blocks):
        turn_rows(dqkv[i // 2, i % 2], 3 * ec, i * quarter)
    qkv_z = weight_grad(
        3 * ec, lambda at: nf[:, :, :, at].reshape(length, dz), gsq, grq
    )
    arrived(weight_sib[0])
    dx_copy.wait_recv()

    def norm1_part(xt, piece):
        return dot_nt(dx[0, xt], wq[0, piece]) + dot_nt(dx[1, xt], wq[1, piece])

    copies = spread_sum(3, norm1_part)

    arrived(gm_sib)
    for s in range(2):
        for k in range(2):
            turn_rows(ao[k, s], ec, (s * 2 + k) * quarter)
    out_z = weight_grad(ec, lambda at: gm[:, :, :, :, at].reshape(length, dz), gso, gro)

    sv[7:8, 0:ec] = jnp.sum(
        dqkv[:, :, :, 0:ec].astype(single).reshape(length, ec), axis=0, keepdims=True
    )
    sv[7:8, ec : 2 * ec] = jnp.sum(
        dqkv[:, :, :, 2 * ec :].astype(single).reshape(length, ec), axis=0, keepdims=True
    )

    arrived(feed_copies)
    my_rows = pl.multiple_of(c * quarter + y * block, block)

    def out_rows(r):
        at = pl.ds(r, 16)
        value = mid[at] + (summed(2, at) + proj_bias)
        out_ref[pl.ds(pl.multiple_of(my_rows + r, 16), 16)] = value.astype(half)

    by_rows(block, 16, out_rows)
    mine = out_ref.at[pl.ds(my_rows, block)]
    out_y = send(mine, mine, ynb)
    out_s = [send(mine, mine, sib)]

    def plane_sum(copies, out, home):
        arrived(copies)
        value = out[z].astype(single)
        for step in range(1, nz):
            value = value + home[(z + step) % nz].astype(single)
        return value.astype(half)

    xp_[x] = plane_sum(proj_z, gsp, grp)
    proj_x = send(xp_.at[x], xp_.at[x], xnb)
    xf[x] = plane_sum(fc_z, gsf, grf)
    fc_x = send(xf.at[x], xf.at[x], xnb)

    theirs = out_ref.at[pl.ds(pl.multiple_of(c * quarter + (1 - y) * block, block), block)]
    out_y.wait_recv()
    out_s.append(send(theirs, theirs, sib))

    arrived(copies)

    def first_back(r):
        at = pl.ds(r, 16)
        by_value, gain_part, shift_part = norm_back(
            my_x[at].astype(single), summed(3, at), gain1
        )
        grad_ref[pl.ds(pl.multiple_of(my_rows + r, 16), 16)] = (gmid[at] + by_value).astype(half)
        sv[1:2] += gain_part
        sv[2:3] += shift_part

    by_rows(block, 16, first_back)
    mine_g = grad_ref.at[pl.ds(my_rows, block)]
    grad_y = send(mine_g, mine_g, ynb)
    grad_s_ = [send(mine_g, mine_g, sib)]

    my_place = x * 4 + t
    svall[my_place] = sv[...]
    sv_copies = [send(sv, svall.at[my_place], dev) for dev in peers[0:7]]
    theirs_g = grad_ref.at[pl.ds(pl.multiple_of(c * quarter + (1 - y) * block, block), block)]
    grad_y.wait_recv()
    grad_s_.append(send(theirs_g, theirs_g, sib))

    xq[x] = plane_sum(qkv_z, gsq, grq)
    qkv_x = send(xq.at[x], xq.at[x], xnb)
    arrived(sv_copies)
    lines = svall[0]
    for place in range(1, 8):
        lines = lines + svall[place]
    for piece in range(nz):
        s2[piece, 0:6] = lines[0:6, piece * dz : (piece + 1) * dz]
        from_x = piece // pieces
        at = (piece % pieces) * dz
        s2[piece, 6:8] = svall[from_x * 4 + t, 6:8, at : at + dz]
        s2[piece, 7:8] = svall[from_x * 4 + t, 7:8, 0:dz]
    s2r[z] = s2[z]
    s2_copies = [
        send(s2.at[(z + step) % nz], s2r.at[z], zdev(step)) for step in range(1, nz)
    ]
    xo[x] = plane_sum(out_z, gso, gro)
    out_x = send(xo.at[x], xo.at[x], xnb)

    arrived([proj_x])
    for side in range(2):
        gproj_ref[side * fch : (side + 1) * fch] = xp_[side].astype(single)
    arrived([fc_x])
    for side in range(2):
        gfc_ref[:, side * fch : (side + 1) * fch] = xf[side].astype(single).T
    arrived([qkv_x])
    for side in range(2):
        tall = xq[side].astype(single).T
        for j in range(3):
            gqkv_ref[:, (j * 2 + side) * ec : (j * 2 + side + 1) * ec] = tall[
                :, j * ec : (j + 1) * ec
            ]
    arrived([out_x])
    for side in range(2):
        gout_ref[side * ec : (side + 1) * ec] = xo[side].astype(single)
    arrived(s2_copies)
    small = s2r[0]
    for piece in range(1, nz):
        small = small + s2r[piece]
    gvec_ref[0:7] = small[0:7]
    q_line, v_line = small[7:8, 0:ec], small[7:8, ec : 2 * ec]
    even = jnp.where(low_lane, q_line, pltpu.roll(v_line, HD, 1))
    odd = jnp.where(low_lane, pltpu.roll(q_line, HD, 1), v_line)
    gvec_ref[7:8, 0:ec] = jnp.where(z % pieces == 0, even, odd)
    gvec_ref[7:8, ec:dz] = jnp.zeros((1, dz - ec), single)
    arrived(out_s)
    arrived(grad_s_)
    for copy in started:
        copy.wait_send()


def plane_block(
    nz,
    block_input,
    segment_ids,
    cotangent,
    qkv_weight,
    qv_bias,
    out_weight,
    out_bias,
    norm1_gain,
    norm1_shift,
    fc_weight,
    fc_bias,
    proj_weight,
    proj_bias,
    norm2_gain,
    norm2_shift,
):
    half = jnp.bfloat16
    single = jnp.float32
    _, rows, width = block_input.shape
    length = segment_ids.shape[1]
    dz = qkv_weight.shape[0]
    ec = qkv_weight.shape[2] // 2
    fch = fc_weight.shape[1] // 2
    quarter, block = rows // 2, rows // 4
    pair = jnp.pad(qv_bias.reshape(1, -1), ((0, 0), (0, dz - qv_bias.size)))
    lines = jnp.concatenate(
        [
            line.reshape(1, dz)
            for line in (
                out_bias,
                norm1_gain,
                norm1_shift,
                norm2_gain,
                norm2_shift,
                proj_bias,
                fc_bias,
            )
        ]
        + [pair],
        axis=0,
    )
    vmem = pltpu.VMEM
    spans = [(i + 1 - max(0, i - 2)) * quarter for i in range(4)]
    heads = ec // HD
    scratch = [
        vmem((2, quarter, width), half),
        vmem((2, 2, quarter, width), half),
        vmem((2, 2, quarter, width), half),
        vmem((2, nz, dz, 3 * ec), half),
        vmem((2, nz, ec, dz), half),
        vmem((2, nz, dz, fch), half),
        vmem((2, nz, fch, dz), half),
        vmem((2, nz, 8, dz), single),
        vmem((8, width), single),
        vmem((2, fch), single),
        vmem((length, ec), half),
        vmem((length, ec), half),
        vmem((length, ec), half),
    ]
    scratch += [vmem((heads, quarter, span), half) for span in spans]
    scratch += [
        vmem((2, 2, quarter, ec), half),
        vmem((2, 2, quarter, ec), half),
        vmem((4, 2, 2, block, width), half),
        vmem((4, 3, block, width), half),
        vmem((2, 2, block, width), single),
        vmem((block, width), single),
        vmem((2, 2, 2, block, width), half),
        vmem((2, 2, 2, block, width), half),
        vmem((2, 2, rows, fch), half),
        vmem((2, 2, rows, fch), half),
        vmem((fch, length), half),
    ]
    for _ in range(2):
        scratch += [
            vmem((nz, 3 * ec, dz), half),
            vmem((nz, ec, dz), half),
            vmem((nz, fch, dz), half),
            vmem((nz, fch, dz), half),
        ]
    scratch += [
        vmem((2, 3 * ec, dz), half),
        vmem((2, ec, dz), half),
        vmem((2, fch, dz), half),
        vmem((2, fch, dz), half),
        vmem((2, rows, ec), half),
        vmem((rows, ec), half),
        vmem((length, ec), single),
        vmem((length, ec), single),
        vmem((2, 2, quarter, 3 * ec), half),
        vmem((2, 2, quarter, 3 * ec), half),
        vmem((quarter, 3 * quarter), single),
        vmem((quarter, fch), single),
        vmem((quarter, 3 * quarter), half),
        vmem((block, width), single),
        vmem((8, width), single),
        vmem((8, 8, width), single),
        vmem((nz, 8, dz), single),
        vmem((nz, 8, dz), single),
        pltpu.SemaphoreType.DMA((160,)),
        pltpu.SemaphoreType.DMA((160,)),
    ]
    whole = pl.BlockSpec(memory_space=pltpu.VMEM)
    outs = pl.pallas_call(
        functools.partial(block_kernel, nz),
        out_shape=(
            jax.ShapeDtypeStruct((rows, width), half),
            jax.ShapeDtypeStruct((rows, width), half),
            jax.ShapeDtypeStruct((dz, 6 * ec), single),
            jax.ShapeDtypeStruct((2 * ec, dz), single),
            jax.ShapeDtypeStruct((dz, 2 * fch), single),
            jax.ShapeDtypeStruct((2 * fch, dz), single),
            jax.ShapeDtypeStruct((8, dz), single),
        ),
        in_specs=[whole] * 9,
        out_specs=(whole,) * 7,
        scratch_shapes=scratch,
        compiler_params=pltpu.CompilerParams(
            collective_id=0, has_side_effects=True, vmem_limit_bytes=67043328
        ),
        name="residual_block",
    )(
        block_input.reshape(rows, width),
        cotangent.reshape(rows, width),
        segment_ids,
        segment_ids.reshape(length, 1),
        qkv_weight.reshape(dz, 6 * ec),
        out_weight,
        fc_weight,
        proj_weight,
        lines,
    )
    out, grad, gqkv, gout, gfc, gproj, gvec = outs
    return (
        out.reshape(block_input.shape),
        grad.reshape(block_input.shape),
        gqkv.reshape(qkv_weight.shape),
        gvec[7, : qv_bias.size].reshape(qv_bias.shape),
        gout,
        gvec[0],
        gvec[1],
        gvec[2],
        gfc,
        gvec[6],
        gproj,
        gvec[5],
        gvec[3],
        gvec[4],
    )


def device_program(mesh):
    planes = mesh.shape["fsdp"]

    def program(block_input, *others):
        seqs_here, rows, width = block_input.shape
        one_kernel = (
            seqs_here == 1
            and mesh.shape["ctx"] == 2
            and mesh.shape["tp"] == 4
            and planes == 4
            and width // planes == 256
        )
        if one_kernel:
            return plane_block(planes, block_input, *others)
        return on_device(block_input, *others)

    return program


def solution(mesh):
    return jax.shard_map(
        device_program(mesh),
        mesh=mesh,
        in_specs=(
            P("fsdp", "ctx", None),
            P("fsdp", None),
            P("fsdp", "ctx", None),
            P("fsdp", None, "tp"),
            P(None, ("tp", "fsdp")),
            P("tp", "fsdp"),
            P("fsdp"),
            P("fsdp"),
            P("fsdp"),
            P("fsdp", "tp"),
            P(("tp", "fsdp")),
            P("tp", "fsdp"),
            P("fsdp"),
            P("fsdp"),
            P("fsdp"),
        ),
        out_specs=(
            P("fsdp", "ctx", None),
            P("fsdp", "ctx", None),
            P("fsdp", None, "tp"),
            P(None, ("tp", "fsdp")),
            P("tp", "fsdp"),
            P("fsdp"),
            P("fsdp"),
            P("fsdp"),
            P("fsdp", "tp"),
            P(("tp", "fsdp")),
            P("tp", "fsdp"),
            P("fsdp"),
            P("fsdp"),
            P("fsdp"),
        ),
        check_vma=False,
    )
```

```python
import functools

import jax
import jax.numpy as jnp
from jax import lax
from jax.experimental import pallas as pl
from jax.experimental.pallas import tpu as pltpu
from jax.sharding import PartitionSpec as P

HD = 64


epsilon = 1e-05


def layer_norm(values, gain, shift):
    centred = values - jnp.mean(values, axis=-1, keepdims=True)
    spread = jnp.mean(centred * centred, axis=-1, keepdims=True)
    return centred * lax.rsqrt(spread + epsilon) * gain + shift


def gelu_act(values):
    return jax.nn.gelu(values, approximate=True)


def on_device(
    block_input,
    segment_ids,
    cotangent,
    qkv_weight,
    qv_bias,
    out_weight,
    out_bias,
    norm1_gain,
    norm1_shift,
    fc_weight,
    fc_bias,
    proj_weight,
    proj_bias,
    norm2_gain,
    norm2_shift,
):
    half = jnp.bfloat16
    single = jnp.float32
    seqs_here, rows_seq, model_width = block_input.shape
    row_count = seqs_here * rows_seq
    shard_index = lax.axis_index("ctx")
    scale_factor = HD ** (-0.5)
    (
        wqkv_low,
        bqv_low,
        wout_low,
        bout_low,
        gain1_low,
        shift1_low,
        wfc_low,
        bfc_low,
        wproj_low,
        bproj_low,
        gain2_low,
        shift2_low,
    ) = (
        lax.all_gather(qkv_weight.astype(half), "fsdp", axis=0, tiled=True),
        lax.all_gather(qv_bias.astype(half), "fsdp", axis=1, tiled=True),
        lax.all_gather(out_weight.astype(half), "fsdp", axis=1, tiled=True),
        lax.all_gather(out_bias.astype(half), "fsdp", axis=0, tiled=True),
        lax.all_gather(norm1_gain.astype(half), "fsdp", axis=0, tiled=True),
        lax.all_gather(norm1_shift.astype(half), "fsdp", axis=0, tiled=True),
        lax.all_gather(fc_weight.astype(half), "fsdp", axis=0, tiled=True),
        lax.all_gather(fc_bias.astype(half), "fsdp", axis=0, tiled=True),
        lax.all_gather(proj_weight.astype(half), "fsdp", axis=1, tiled=True),
        lax.all_gather(proj_bias.astype(half), "fsdp", axis=0, tiled=True),
        lax.all_gather(norm2_gain.astype(half), "fsdp", axis=0, tiled=True),
        lax.all_gather(norm2_shift.astype(half), "fsdp", axis=0, tiled=True),
    )
    gain_first = gain1_low.astype(single)
    shift_first = shift1_low.astype(single)
    gain_second = gain2_low.astype(single)
    shift_second = shift2_low.astype(single)
    inputs = block_input.reshape(row_count, model_width).astype(single)
    normed_first = layer_norm(inputs, gain_first, shift_first).astype(half)
    projected = jnp.einsum("rd,dce->rce", normed_first, wqkv_low, preferred_element_type=single)
    bias_pair = bqv_low.astype(single)
    queries = (projected[:, 0] + bias_pair[0]).astype(half)
    key_rows = projected[:, 1].astype(half)
    value_rows = (projected[:, 2] + bias_pair[1]).astype(half)
    local_width = queries.shape[1]
    head_count = local_width // HD
    keys_all, values_all = (
        lax.all_gather(
            key_rows.reshape(seqs_here, rows_seq, local_width), "ctx", axis=1, tiled=True
        ),
        lax.all_gather(
            value_rows.reshape(seqs_here, rows_seq, local_width), "ctx", axis=1, tiled=True
        ),
    )
    length = keys_all.shape[1]
    query_pos = shard_index * rows_seq + jnp.arange(rows_seq)
    key_pos = jnp.arange(length)
    seg_query = lax.dynamic_slice_in_dim(segment_ids, shard_index * rows_seq, rows_seq, 1)
    query_heads = queries.reshape(seqs_here, rows_seq, head_count, HD)
    key_heads = keys_all.reshape(seqs_here, length, head_count, HD)
    value_heads = values_all.reshape(seqs_here, length, head_count, HD)

    def masked_scores(query_blk, key_blk, seg_row, seg_here):
        raw = (
            jnp.einsum("qhe,khe->hqk", query_blk, key_blk, preferred_element_type=single)
            * scale_factor
        )
        allowed = (key_pos[None, :] <= query_pos[:, None]) & (seg_here[:, None] == seg_row[None, :])
        return jnp.where(allowed[None], raw, -1e30)

    def attend(packed):
        query_blk, key_blk, value_blk, seg_row, seg_here = packed
        masked = masked_scores(query_blk, key_blk, seg_row, seg_here)
        row_max = jnp.max(masked, axis=-1, keepdims=True)
        expo = jnp.exp(masked - row_max)
        row_total = jnp.sum(expo, axis=-1, keepdims=True)
        probs_low = (expo / row_total).astype(half)
        attended = jnp.einsum("hqk,khe->qhe", probs_low, value_blk, preferred_element_type=single)
        return (attended.astype(half), row_max + jnp.log(row_total))

    attended, log_total = lax.map(
        attend, (query_heads, key_heads, value_heads, segment_ids, seg_query)
    )
    attended_rows = attended.reshape(row_count, local_width)
    attn_partial = jnp.dot(attended_rows, wout_low, preferred_element_type=single)
    attn_total = lax.psum(attn_partial.astype(jnp.bfloat16), "tp").astype(jnp.float32)
    middle = inputs + attn_total + bout_low.astype(single)
    normed_second = layer_norm(middle, gain_second, shift_second).astype(half)
    pre_act = jnp.dot(normed_second, wfc_low, preferred_element_type=single) + bfc_low.astype(
        single
    )
    act_low = gelu_act(pre_act).astype(half)
    mlp_total = lax.psum(
        jnp.dot(act_low, wproj_low, preferred_element_type=single).astype(jnp.bfloat16), "tp"
    ).astype(jnp.float32)
    out_rows = (middle + mlp_total + bproj_low.astype(single)).astype(half)
    wqkv_use, wout_use, wfc_use, wproj_use = (
        lax.all_gather(qkv_weight.astype(half), "fsdp", axis=0, tiled=True),
        lax.all_gather(out_weight.astype(half), "fsdp", axis=1, tiled=True),
        lax.all_gather(fc_weight.astype(half), "fsdp", axis=0, tiled=True),
        lax.all_gather(proj_weight.astype(half), "fsdp", axis=1, tiled=True),
    )
    grad_out = cotangent.reshape(row_count, model_width).astype(single)
    grad_out_low = cotangent.reshape(row_count, model_width)
    grad_bproj = jnp.sum(grad_out_low, axis=0, dtype=single)
    grad_wproj = jnp.einsum("rf,rd->fd", act_low, grad_out_low, preferred_element_type=single)
    grad_act = jnp.einsum("rd,fd->rf", grad_out_low, wproj_use, preferred_element_type=single)
    gelu_unused, gelu_pull = jax.vjp(gelu_act, pre_act)
    grad_pre = gelu_pull(grad_act)[0].astype(half)
    grad_bfc = jnp.sum(grad_pre, axis=0, dtype=single)
    grad_wfc = jnp.einsum("rd,rf->df", normed_second, grad_pre, preferred_element_type=single)
    norm2_partial = jnp.einsum("rf,df->rd", grad_pre, wfc_use, preferred_element_type=single)
    grad_norm2 = lax.psum(norm2_partial.astype(jnp.bfloat16), "tp").astype(jnp.float32)
    norm_unused, second_pull = jax.vjp(layer_norm, middle, gain_second, shift_second)
    grad_mid_ln, grad_gain2, grad_shift2 = second_pull(grad_norm2)
    grad_middle = grad_out + grad_mid_ln
    grad_mid_low = grad_middle.astype(half)
    grad_bout = jnp.sum(grad_mid_low, axis=0, dtype=single)
    grad_wout = jnp.einsum("rk,rd->kd", attended_rows, grad_mid_low, preferred_element_type=single)
    grad_att = jnp.einsum(
        "rd,kd->rk", grad_mid_low, wout_use, preferred_element_type=single
    ).astype(half)
    grad_att_heads = grad_att.reshape(seqs_here, rows_seq, head_count, HD)

    def attend_back(packed):
        query_blk, key_blk, value_blk, seg_row, seg_here, log_blk, grad_blk = packed
        masked = masked_scores(query_blk, key_blk, seg_row, seg_here)
        attn_probs = jnp.exp(masked - log_blk)
        probs_low = attn_probs.astype(half)
        grad_value = jnp.einsum("hqk,qhe->khe", probs_low, grad_blk, preferred_element_type=single)
        grad_probs = jnp.einsum("qhe,khe->hqk", grad_blk, value_blk, preferred_element_type=single)
        row_delta = jnp.sum(grad_probs * attn_probs, axis=-1, keepdims=True)
        grad_scores = (attn_probs * (grad_probs - row_delta)).astype(half)
        grad_query = (
            jnp.einsum("hqk,khe->qhe", grad_scores, key_blk, preferred_element_type=single)
            * scale_factor
        )
        grad_key = (
            jnp.einsum("hqk,qhe->khe", grad_scores, query_blk, preferred_element_type=single)
            * scale_factor
        )
        return (grad_query.astype(half), grad_key, grad_value)

    grad_query, grad_key, grad_value = lax.map(
        attend_back,
        (query_heads, key_heads, value_heads, segment_ids, seg_query, log_total, grad_att_heads),
    )
    grad_key, grad_value = (
        lax.psum_scatter(
            grad_key.reshape(seqs_here, length, local_width).astype(jnp.bfloat16),
            "ctx",
            scatter_dimension=1,
            tiled=True,
        ).astype(jnp.float32),
        lax.psum_scatter(
            grad_value.reshape(seqs_here, length, local_width).astype(jnp.bfloat16),
            "ctx",
            scatter_dimension=1,
            tiled=True,
        ).astype(jnp.float32),
    )
    grad_query = grad_query.reshape(row_count, local_width)
    grad_key = grad_key.reshape(row_count, local_width).astype(half)
    grad_value = grad_value.reshape(row_count, local_width).astype(half)
    grad_qkv = jnp.stack([grad_query, grad_key, grad_value], axis=1)
    grad_bqv = jnp.stack(
        [jnp.sum(grad_query, axis=0, dtype=single), jnp.sum(grad_value, axis=0, dtype=single)]
    )
    grad_wqkv = jnp.einsum("rd,rce->dce", normed_first, grad_qkv, preferred_element_type=single)
    norm1_partial = jnp.einsum("rce,dce->rd", grad_qkv, wqkv_use, preferred_element_type=single)
    grad_norm1 = lax.psum(norm1_partial.astype(jnp.bfloat16), "tp").astype(jnp.float32)
    first_unused, first_pull = jax.vjp(layer_norm, inputs, gain_first, shift_first)
    grad_in_ln, grad_gain1, grad_shift1 = first_pull(grad_norm1)
    input_rows = (grad_middle + grad_in_ln).astype(half)
    block_output = out_rows.reshape(block_input.shape)
    input_grad = input_rows.reshape(block_input.shape)
    (
        sum_wqkv,
        sum_bqv,
        sum_wout,
        sum_bout,
        sum_gain1,
        sum_shift1,
        sum_wfc,
        sum_bfc,
        sum_wproj,
        sum_bproj,
        sum_gain2,
        sum_shift2,
    ) = (
        lax.psum_scatter(grad_wqkv, ("fsdp", "ctx"), scatter_dimension=0, tiled=True),
        lax.psum_scatter(grad_bqv, ("fsdp", "ctx"), scatter_dimension=1, tiled=True),
        lax.psum_scatter(grad_wout, ("fsdp", "ctx"), scatter_dimension=1, tiled=True),
        lax.psum_scatter(grad_bout, ("fsdp", "ctx"), scatter_dimension=0, tiled=True),
        lax.psum_scatter(grad_gain1, ("fsdp", "ctx"), scatter_dimension=0, tiled=True),
        lax.psum_scatter(grad_shift1, ("fsdp", "ctx"), scatter_dimension=0, tiled=True),
        lax.psum_scatter(grad_wfc, ("fsdp", "ctx"), scatter_dimension=0, tiled=True),
        lax.psum_scatter(grad_bfc, ("fsdp", "ctx"), scatter_dimension=0, tiled=True),
        lax.psum_scatter(grad_wproj, ("fsdp", "ctx"), scatter_dimension=1, tiled=True),
        lax.psum_scatter(grad_bproj, ("fsdp", "ctx"), scatter_dimension=0, tiled=True),
        lax.psum_scatter(grad_gain2, ("fsdp", "ctx"), scatter_dimension=0, tiled=True),
        lax.psum_scatter(grad_shift2, ("fsdp", "ctx"), scatter_dimension=0, tiled=True),
    )
    (
        final_wqkv,
        final_bqv,
        final_wout,
        final_bout,
        final_gain1,
        final_shift1,
        final_wfc,
        final_bfc,
        final_wproj,
        final_bproj,
        final_gain2,
        final_shift2,
    ) = (
        lax.all_gather(sum_wqkv.astype(jnp.bfloat16), "ctx", axis=0, tiled=True).astype(
            sum_wqkv.dtype
        ),
        lax.all_gather(sum_bqv.astype(jnp.bfloat16), "ctx", axis=1, tiled=True).astype(
            sum_bqv.dtype
        ),
        lax.all_gather(sum_wout.astype(jnp.bfloat16), "ctx", axis=1, tiled=True).astype(
            sum_wout.dtype
        ),
        lax.all_gather(sum_bout.astype(jnp.bfloat16), "ctx", axis=0, tiled=True).astype(
            sum_bout.dtype
        ),
        lax.all_gather(sum_gain1.astype(jnp.bfloat16), "ctx", axis=0, tiled=True).astype(
            sum_gain1.dtype
        ),
        lax.all_gather(sum_shift1.astype(jnp.bfloat16), "ctx", axis=0, tiled=True).astype(
            sum_shift1.dtype
        ),
        lax.all_gather(sum_wfc.astype(jnp.bfloat16), "ctx", axis=0, tiled=True).astype(
            sum_wfc.dtype
        ),
        lax.all_gather(sum_bfc.astype(jnp.bfloat16), "ctx", axis=0, tiled=True).astype(
            sum_bfc.dtype
        ),
        lax.all_gather(sum_wproj.astype(jnp.bfloat16), "ctx", axis=1, tiled=True).astype(
            sum_wproj.dtype
        ),
        lax.all_gather(sum_bproj.astype(jnp.bfloat16), "ctx", axis=0, tiled=True).astype(
            sum_bproj.dtype
        ),
        lax.all_gather(sum_gain2.astype(jnp.bfloat16), "ctx", axis=0, tiled=True).astype(
            sum_gain2.dtype
        ),
        lax.all_gather(sum_shift2.astype(jnp.bfloat16), "ctx", axis=0, tiled=True).astype(
            sum_shift2.dtype
        ),
    )
    return (
        block_output,
        input_grad,
        final_wqkv,
        final_bqv,
        final_wout,
        final_bout,
        final_gain1,
        final_shift1,
        final_wfc,
        final_bfc,
        final_wproj,
        final_bproj,
        final_gain2,
        final_shift2,
    )


MESH = pl.DeviceIdType.MESH


def dot_nn(left, right):
    return lax.dot_general(
        left, right, (((1,), (0,)), ((), ())), preferred_element_type=jnp.float32
    )


def dot_nt(left, right):
    return lax.dot_general(
        left, right, (((1,), (1,)), ((), ())), preferred_element_type=jnp.float32
    )


def by_rows(rows, step, body):
    def one(index, carry):
        body(pl.multiple_of(index * step, step))
        return carry

    lax.fori_loop(0, rows // step, one, 0)


def norm_parts(values):
    centred = values - jnp.mean(values, axis=-1, keepdims=True)
    spread = jnp.mean(centred * centred, axis=-1, keepdims=True)
    return centred, lax.rsqrt(spread + epsilon)


def norm_back(values, incoming, gain):
    centred, rate = norm_parts(values)
    hat = centred * rate
    scaled = incoming * gain
    by_value = rate * (
        scaled
        - jnp.mean(scaled, axis=-1, keepdims=True)
        - hat * jnp.mean(scaled * hat, axis=-1, keepdims=True)
    )
    return (
        by_value,
        jnp.sum(incoming * hat, axis=0, keepdims=True),
        jnp.sum(incoming, axis=0, keepdims=True),
    )


class Partly:
    def __init__(self, copy, sends, receives):
        self.copy, self.sends, self.receives = copy, sends, receives

    def start(self):
        self.copy.start()

    def wait_recv(self):
        pl.when(self.receives)(self.copy.wait_recv)

    def wait_send(self):
        pl.when(self.sends)(self.copy.wait_send)


def block_kernel(
    nz,
    x_in,
    dy_in,
    seg_row,
    wqkv_in,
    wout_in,
    wfc_in,
    wproj_in,
    bout_in,
    gain1_in,
    shift1_in,
    gain2_in,
    shift2_in,
    bproj_in,
    bfc_in,
    bqv_in,
    out_hbm,
    grad_hbm,
    gqkv_hbm,
    gout_hbm,
    gfc_hbm,
    gproj_hbm,
    gvec_ref,
    stq,
    sto,
    stf,
    stp,
    xl,
    xr,
    dyb,
    nf,
    wq,
    wo,
    wf,
    wp,
    vec,
    full,
    fcb,
    qb,
    kb,
    vb,
    p0,
    p1,
    p2,
    p3,
    segc,
    ao,
    ax,
    srs,
    rrs,
    own,
    mid,
    ns,
    gm,
    act,
    gp,
    turned,
    gsq,
    gso,
    gsf,
    gsp,
    grq,
    gro,
    grf,
    grp,
    glf,
    glp,
    accum,
    xq,
    xo,
    xf,
    xp_,
    gtt,
    gt,
    dkb,
    dvb,
    dqkv,
    dx,
    wide,
    wide_b,
    wide2,
    dsb,
    outv,
    gradv,
    gmid,
    sv,
    svall,
    s2,
    s2r,
    send_sem,
    recv_sem,
    local_sem,
):
    half = jnp.bfloat16
    single = jnp.float32
    z = lax.axis_index("fsdp")
    x = lax.axis_index("ctx")
    t = lax.axis_index("tp")
    y = t // 2
    c = t % 2
    quarter = xl.shape[0] // 2
    block = quarter // 2
    width = xl.shape[1]
    dz = width // nz
    fch = wf.shape[3]
    ec = qb.shape[1]
    length = qb.shape[0]
    probs = (p0, p1, p2, p3)
    sib = (z, x, y * 2 + 1 - c)
    ynb = (z, x, (1 - y) * 2 + c)
    xnb = (z, 1 - x, t)
    dia = (z, 1 - x, (1 - y) * 2 + c)
    started = []

    def send(src, dst, dev):
        slot = len(started)
        copy = pltpu.make_async_remote_copy(
            src_ref=src,
            dst_ref=dst,
            send_sem=send_sem.at[slot],
            recv_sem=recv_sem.at[slot],
            device_id=dev,
            device_id_type=MESH,
        )
        copy.start()
        started.append(copy)
        return copy

    def arrived(copies):
        for copy in copies:
            copy.wait_recv()

    def send_if(src, dst, dev, sends, receives, start=True):
        slot = len(started)
        copy = pltpu.make_async_remote_copy(
            src_ref=src,
            dst_ref=dst,
            send_sem=send_sem.at[slot],
            recv_sem=recv_sem.at[slot],
            device_id=dev,
            device_id_type=MESH,
        )
        some = Partly(copy, sends, receives)
        if start:
            pl.when(sends)(copy.start)
        started.append(some)
        return some

    fetched = []

    def fetch(src, dst):
        copy = pltpu.make_async_copy(src, dst, local_sem.at[len(fetched)])
        copy.start()
        fetched.append(copy)
        return copy

    def zdev(step):
        return ((z + step) % nz, x, t)

    right, left = zdev(1), zdev(nz - 1)

    peers = [(z, px, pt) for px in (x, 1 - x) for pt in (t, sib[2], ynb[2], (1 - y) * 2 + 1 - c)][
        1:
    ]
    for step in range(1, nz):
        peers += [((z + step) % nz, x, t), ((z + step) % nz, x, sib[2])]
    barrier = pltpu.get_barrier_semaphore()
    for dev in peers:
        pl.semaphore_signal(barrier, inc=1, device_id=dev, device_id_type=MESH)

    my_e = pl.ds(pl.multiple_of(x * ec, ec), ec)
    my_f = pl.ds(pl.multiple_of(x * fch, fch), fch)
    stage_q = [
        fetch(wqkv_in.at[j, :, my_e], stq.at[:, j * ec : (j + 1) * ec]) for j in range(3)
    ]
    stage_x = fetch(x_in, xl)
    stage_o = fetch(wout_in.at[my_e], sto)
    stage_f = fetch(wfc_in.at[:, my_f], stf)
    stage_p = fetch(wproj_in.at[my_f], stp)
    stage_dy = [
        fetch(dy_in.at[pl.ds(s * quarter, quarter)], dyb.at[s, x]) for s in range(2)
    ]

    def weight_at(which, h, plane):
        if which == 0:
            return wq.at[plane, :, pl.ds(pl.multiple_of(h * 3 * ec, ec), 3 * ec)]
        if which == 1:
            return wo.at[plane, pl.ds(pl.multiple_of(h * ec, ec), ec)]
        return (wf, wp)[which - 2].at[h, plane]

    def rounded(src, dst, rows):
        def some(r):
            dst[pl.ds(r, 64)] = src[pl.ds(r, 64)].astype(half)

        by_rows(rows, 64, some)

    lines = [[], [], [], []]
    weight_sib = [[], [], [], []]

    def line_start(which):
        mine = weight_at(which, c, z)
        lines[which].append(
            (
                send_if(mine, mine, right, z < nz - 1, z >= 1),
                send_if(mine, mine, left, z >= 1, z < nz - 1),
            )
        )

    def line_pass(which, step):
        from_left, from_right = lines[which][step - 1]
        lower = weight_at(which, c, (z + nz - step) % nz)
        upper = weight_at(which, c, (z + step) % nz)
        from_left.wait_recv()
        if step < nz - 1:
            to_right = send_if(
                lower, lower, right, (z >= step) & (z < nz - 1), z >= step + 1
            )
        weight_sib[which].append(send_if(lower, lower, sib, z >= step, z >= step))
        from_right.wait_recv()
        if step < nz - 1:
            to_left = send_if(
                upper, upper, left, (z + step < nz) & (z >= 1), z + step + 1 < nz
            )
            lines[which].append((to_right, to_left))
        weight_sib[which].append(send_if(upper, upper, sib, z + step < nz, z + step < nz))

    def to_sibling(which):
        mine = weight_at(which, c, z)
        weight_sib[which].append(send(mine, mine, sib))

    for copy in stage_q:
        copy.wait()
    rounded(stq, weight_at(0, c, z), dz)
    for row, line in enumerate(
        (bout_in, gain1_in, shift1_in, gain2_in, shift2_in, bproj_in, bfc_in)
    ):
        vec[c, z, row : row + 1] = line[...].astype(half).astype(single)
    pair = bqv_in.shape[1]
    vec[c, z, 7:8, 0:pair] = bqv_in[0:1].astype(half).astype(single)
    vec[c, z, 7:8, pair : 2 * pair] = bqv_in[1:2].astype(half).astype(single)
    vec[c, z, 7:8, 2 * pair :] = jnp.zeros((1, dz - 2 * pair), single)
    stage_x.wait()
    pl.semaphore_wait(barrier, len(peers))

    line_start(0)
    x_copy = send(xl.at[pl.ds(pl.multiple_of(c * quarter, quarter), quarter)], xr.at[c], xnb)
    vec_copies = [send(vec.at[c, z], vec.at[c, z], sib)]
    for step in range(1, nz):
        for dev_t in (t, sib[2]):
            vec_copies.append(send(vec.at[c, z], vec.at[c, z], ((z + step) % nz, x, dev_t)))
    stage_o.wait()
    rounded(sto, weight_at(1, c, z), ec)
    line_start(1)
    to_sibling(0)
    to_sibling(1)
    for copy in stage_dy:
        copy.wait()
    stage_f.wait()
    rounded(stf, weight_at(2, c, z), dz)
    stage_p.wait()
    rounded(stp, weight_at(3, c, z), fch)

    arrived(vec_copies)
    for piece in range(nz):
        full[:, piece * dz : (piece + 1) * dz] = vec[c, piece]
    pieces = nz // 2
    for h in range(2):
        for k in range(pieces):
            fcb[h : h + 1, k * dz : (k + 1) * dz] = vec[h, x * pieces + k][6:7]
    lane = lax.broadcasted_iota(jnp.int32, (1, ec), 1)
    low_lane = lane < HD
    first_piece = vec[c, x * pieces][7:8, 0:ec]
    next_piece = vec[c, x * pieces + 1][7:8, 0:ec]
    q_bias = jnp.where(low_lane, first_piece, pltpu.roll(next_piece, HD, 1))
    v_bias = jnp.where(low_lane, pltpu.roll(first_piece, HD, 1), next_piece)
    out_bias = full[0:1]
    gain1, shift1 = full[1:2], full[2:3]
    gain2, shift2 = full[3:4], full[4:5]
    proj_bias = full[5:6]

    def first_norm(src, dst):
        def rows(r):
            centred, rate = norm_parts(src[pl.ds(r, 64)].astype(single))
            dst[pl.ds(r, 64)] = (centred * rate * gain1 + shift1).astype(half)

        by_rows(quarter, 64, rows)

    for s in range(2):
        first_norm(xl.at[pl.ds(s * quarter, quarter)], nf.at[x, s])
    line_pass(0, 1)
    line_pass(1, 1)
    x_copy.wait_recv()
    x_fwd = send(xr.at[c], xr.at[c], sib)
    dy_copy = send(dyb.at[c, x], dyb.at[c, x], xnb)
    first_norm(xr.at[c], nf.at[1 - x, c])
    line_pass(0, 2)
    line_pass(1, 2)
    line_start(2)
    line_start(3)
    to_sibling(2)
    to_sibling(3)
    x_fwd.wait_recv()
    first_norm(xr.at[1 - c], nf.at[1 - x, 1 - c])
    for i in range(length // quarter):
        line = seg_row[:, i * quarter : (i + 1) * quarter].astype(single)
        segc[i * quarter : (i + 1) * quarter] = jnp.broadcast_to(line, (128, quarter)).T
    for step in range(3, nz):
        line_pass(0, step)
        line_pass(1, step)

    my_qkv = pl.ds(pl.multiple_of(c * 3 * ec, ec), 3 * ec)
    for xi in range(2):
        for ci in range(2):
            proj = dot_nn(nf[xi, ci], wq[:, :, my_qkv].reshape(width, 3 * ec))
            at = pl.ds((xi * 2 + ci) * quarter, quarter)
            qb[at] = (proj[:, 0:ec] + q_bias).astype(half)
            kb[at] = proj[:, ec : 2 * ec].astype(half)
            vb[at] = (proj[:, 2 * ec :] + v_bias).astype(half)
    dy_copy.wait_recv()
    dy_fwd = send(dyb.at[c, 1 - x], dyb.at[c, 1 - x], sib)

    head_lane = lax.broadcasted_iota(jnp.int32, (1, ec), 1) // HD
    n_blocks = length // quarter
    heads = ec // HD

    def only(values, h):
        return jnp.where(head_lane == h, values, jnp.zeros_like(values))

    for i in range(n_blocks):
        j0 = max(0, i - 2)
        span = (i + 1 - j0) * quarter
        keys = pl.ds(j0 * quarter, span)
        scores = (wide, wide_b)
        for h in range(heads):
            q_h = only(qb[pl.ds(i * quarter, quarter)], h) * jnp.asarray(HD**-0.5, half)
            scores[h][:, 0:span] = dot_nt(q_h, kb[keys])

        def soft(r, i=i, j0=j0, span=span):
            q_at = i * quarter + r + lax.broadcasted_iota(jnp.int32, (64, span), 0)
            k_at = j0 * quarter + lax.broadcasted_iota(jnp.int32, (64, span), 1)
            seg_q = segc[pl.ds(pl.multiple_of(i * quarter + r, 64), 64)]
            seg_k = seg_row[:, j0 * quarter : j0 * quarter + span].astype(single)
            same = jnp.concatenate([seg_q] * (span // 128), axis=1) == seg_k
            allowed = (k_at <= q_at) & same
            for h in range(heads):
                masked = jnp.where(allowed, scores[h][pl.ds(r, 64), 0:span], -1e30)
                expo = jnp.exp(masked - jnp.max(masked, axis=-1, keepdims=True))
                share = expo * (1.0 / jnp.sum(expo, axis=-1, keepdims=True))
                probs[i][h, pl.ds(r, 64)] = share.astype(half)

        by_rows(quarter, 64, soft)
        total = None
        for h in range(heads):
            part = dot_nn(probs[i][h], only(vb[keys], h))
            total = part if total is None else total + part
        ao[i // 2, i % 2] = total.astype(half)

    my_ax = pl.ds(pl.multiple_of(c * ec, ec), ec)
    att_copy = send(ao.at[:, 1 - c], ax.at[:, :, my_ax], sib)
    ax[:, :, my_ax] = ao[:, c]
    arrived(weight_sib[1])
    att_copy.wait_recv()

    def spread_sum(k, part):
        copies = []
        for turn, xt in ((0, 1 - x), (1, x)):

            def columns(piece, carry, turn=turn, xt=xt):
                value = part(xt, piece)
                at = pl.ds(pl.multiple_of(piece * dz, dz), dz)
                for yi in range(2):
                    rows = value[yi * block : (yi + 1) * block]
                    srs[k, turn, yi, :, at] = rows.astype(half)
                    if turn:
                        own[k % 2, yi, :, at] = rows
                return carry

            lax.fori_loop(0, nz, columns, 0)
            if turn == 0:
                copies.append(send(srs.at[k, 0, 1 - y], rrs.at[k, 0], dia))
                copies.append(send(srs.at[k, 0, y], rrs.at[k, 1], xnb))
            else:
                copies.append(send(srs.at[k, 1, 1 - y], rrs.at[k, 2], ynb))
        return copies

    def summed(k, at):
        value = own[k % 2, y, at]
        for slot in range(3):
            value = value + rrs[k, slot, at].astype(single)
        return value

    def attention_out(xt, piece):
        return dot_nn(ax[xt], wo[piece])

    copies = spread_sum(0, attention_out)

    line_pass(2, 1)
    line_pass(3, 1)
    dy_fwd.wait_recv()
    arrived(copies)

    my_x = xl.at[pl.ds(pl.multiple_of(c * quarter + y * block, block), block)]

    def middle_rows(r):
        at = pl.ds(r, 16)
        value = my_x[at].astype(single) + (summed(0, at) + out_bias)
        mid[at] = value
        centred, rate = norm_parts(value)
        ns[c, x, y, at] = (centred * rate * gain2 + shift2).astype(half)

    by_rows(block, 16, middle_rows)

    def plane_gather(buf):
        mine = buf.at[c, x, y]
        return [
            send(mine, mine, dia),
            send(mine, mine, xnb),
            send(mine, mine, ynb),
            send(mine, mine, sib),
        ]

    copies = plane_gather(ns)
    for step in range(2, nz):
        line_pass(2, step)
        line_pass(3, step)
    arrived(weight_sib[2])
    arrived(weight_sib[3])

    ns_sib = [copies[3]]

    def hidden(xt):
        rows_ns = ns[c, xt].reshape(quarter, width)
        for h in range(2):
            wide[:, 0:fch] = dot_nn(rows_ns, wf[h].reshape(width, fch))
            grad = None
            for piece in range(nz):
                part = dot_nt(
                    dyb[c, xt, :, piece * dz : (piece + 1) * dz],
                    wp[h, piece],
                )
                grad = part if grad is None else grad + part
            wide2[:, 0:fch] = grad

            def rows(r, h=h):
                value = wide[pl.ds(r, 32), 0:fch] + fcb[h : h + 1]
                root = 0.7978845608028654
                square = value * value
                inner = jnp.tanh(root * (value + 0.044715 * (square * value)))
                lift = 0.5 * (1.0 + inner)
                slope = lift + 0.5 * value * (1.0 - inner * inner) * (
                    root * (1.0 + 3.0 * 0.044715 * square)
                )
                at = pl.ds(pl.multiple_of(xt * quarter + r, 32), 32)
                act[c, h, at] = (value * lift).astype(half)
                gp[c, h, at] = (wide2[pl.ds(r, 32), 0:fch] * slope).astype(half)

            by_rows(quarter, 32, rows)

    copies[2].wait_recv()
    ns_sib.append(send(ns.at[c, x, 1 - y], ns.at[c, x, 1 - y], sib))
    hidden(x)
    copies[1].wait_recv()
    ns_sib.append(send(ns.at[c, 1 - x, y], ns.at[c, 1 - x, y], sib))
    copies[0].wait_recv()
    ns_sib.append(send(ns.at[c, 1 - x, 1 - y], ns.at[c, 1 - x, 1 - y], sib))
    hidden(1 - x)

    act_copy = send(act.at[c, 1 - c], act.at[c, 1 - c], sib)
    gp_copy = send(gp.at[c, 1 - c], gp.at[c, 1 - c], sib)

    def norm2_part(xt, piece):
        at = pl.ds(pl.multiple_of(xt * quarter, quarter), quarter)
        return dot_nt(gp[c, 0, at], wf[0, piece]) + dot_nt(gp[c, 1, at], wf[1, piece])

    copies = spread_sum(1, norm2_part)

    def weight_grad(left, right_at, out):
        def one(step, carry):
            piece = (z + step) % nz
            at = pl.ds(pl.multiple_of(piece * dz, dz), dz)
            out[piece] = dot_nn(turned[0:left], right_at(at)).astype(half)
            return carry

        lax.fori_loop(0, nz, one, 0)

    def direct_sum(out, home):
        return [
            send(out.at[(z + step) % nz], home.at[z], zdev(step)) for step in range(1, nz)
        ]

    def line_sum(out, up, down):
        rights, lefts = {}, {}
        for k in range(nz - 1, 0, -1):
            upper, lower = (z + k) % nz, (z + nz - k) % nz
            rights[k] = send_if(
                out.at[upper],
                up.at[upper],
                right,
                z + k < nz,
                (z >= 1) & (z - 1 + k < nz),
                start=False,
            )
            lefts[k] = send_if(
                out.at[lower],
                down.at[lower],
                left,
                z >= k,
                (z < nz - 1) & (z + 1 >= k),
                start=False,
            )
            pl.when((z == 0) & (z + k < nz))(rights[k].start)
            pl.when((z == nz - 1) & (z >= k))(lefts[k].start)
        return out, up, down, rights, lefts

    def line_add(line, j):
        out, up, down, rights, lefts = line
        upper, lower = (z + j) % nz, (z + nz - j) % nz

        @pl.when((z >= 1) & (z + j < nz))
        def _():
            rights[j + 1].copy.wait_recv()
            out[upper] = (out[upper].astype(single) + up[upper].astype(single)).astype(half)
            rights[j].start()

        @pl.when((z < nz - 1) & (z >= j))
        def _():
            lefts[j + 1].copy.wait_recv()
            out[lower] = (out[lower].astype(single) + down[lower].astype(single)).astype(half)
            lefts[j].start()

    def line_end(line):
        out, up, down, rights, lefts = line
        accum[...] = out[z].astype(single)

        @pl.when(z >= 1)
        def _():
            rights[1].copy.wait_recv()
            accum[...] += up[z].astype(single)

        @pl.when(z < nz - 1)
        def _():
            lefts[1].copy.wait_recv()
            accum[...] += down[z].astype(single)

    def turn_rows(src, left, column):
        turned[0:left, pl.ds(pl.multiple_of(column, quarter), quarter)] = src.T

    act_copy.wait_recv()
    for s in range(2):
        for k in range(2):
            turn_rows(
                act[s, c, k * quarter : (k + 1) * quarter], fch, (s * 2 + k) * quarter
            )
    weight_grad(fch, lambda at: dyb[:, :, :, at].reshape(length, dz), gsp)
    proj_z = line_sum(gsp, grp, glp)

    gp_copy.wait_recv()
    arrived(ns_sib)
    for s in range(2):
        for k in range(2):
            turn_rows(gp[s, c, k * quarter : (k + 1) * quarter], fch, (s * 2 + k) * quarter)
    weight_grad(fch, lambda at: ns[:, :, :, :, at].reshape(length, dz), gsf)
    fc_z = line_sum(gsf, grf, glf)

    sv[...] = jnp.zeros_like(sv)
    for s in range(2):
        sv[6:7, 0:fch] += jnp.sum(gp[s, c].astype(single), axis=0, keepdims=True)

    arrived(copies)
    my_dy = dyb.at[c, x, pl.ds(pl.multiple_of(y * block, block), block)]

    def middle_back(r):
        at = pl.ds(r, 16)
        grad_rows = my_dy[at].astype(single)
        by_value, gain_part, shift_part = norm_back(mid[at], summed(1, at), gain2)
        grad = grad_rows + by_value
        gmid[at] = grad
        low = grad.astype(half)
        gm[c, x, y, at] = low
        sv[3:4] += gain_part
        sv[4:5] += shift_part
        sv[0:1] += jnp.sum(low.astype(single), axis=0, keepdims=True)
        sv[5:6] += jnp.sum(grad_rows, axis=0, keepdims=True)

    by_rows(block, 16, middle_back)

    copies = plane_gather(gm)
    gm_sib = [copies[3]]
    for j in range(nz - 2, 0, -1):
        line_add(proj_z, j)

    def grad_attended(xt):
        at = pl.ds(pl.multiple_of(xt * quarter, quarter), quarter)
        rows_gm = gm[c, xt].reshape(quarter, width)
        total = None
        for piece in range(nz):
            part = dot_nt(rows_gm[:, piece * dz : (piece + 1) * dz], wo[piece])
            total = part if total is None else total + part
        for h in range(2):
            gtt[h, at] = total[:, h * ec : (h + 1) * ec].astype(half)

    copies[2].wait_recv()
    gm_sib.append(send(gm.at[c, x, 1 - y], gm.at[c, x, 1 - y], sib))
    grad_attended(x)
    copies[1].wait_recv()
    gm_sib.append(send(gm.at[c, 1 - x, y], gm.at[c, 1 - x, y], sib))
    copies[0].wait_recv()
    gm_sib.append(send(gm.at[c, 1 - x, 1 - y], gm.at[c, 1 - x, 1 - y], sib))
    grad_attended(1 - x)
    gt_copy = send(gtt.at[1 - c], gt.at[c], sib)
    gt[c] = gtt[c]
    arrived(gm_sib)
    for s in range(2):
        for k in range(2):
            turn_rows(ao[k, s], ec, (s * 2 + k) * quarter)
    weight_grad(ec, lambda at: gm[:, :, :, :, at].reshape(length, dz), gso)
    out_z = direct_sum(gso, gro)
    line_add(fc_z, nz - 2)
    line_end(proj_z)
    xp_[x] = accum[...].astype(half)
    proj_x = send(xp_.at[x], xp_.at[x], xnb)

    def feed_part(xt, piece):
        at = pl.ds(pl.multiple_of(xt * quarter, quarter), quarter)
        return dot_nn(act[c, 0, at], wp[0, piece]) + dot_nn(act[c, 1, at], wp[1, piece])

    feed_copies = spread_sum(2, feed_part)
    gt_copy.wait_recv()

    dkb[...] = jnp.zeros_like(dkb)
    dvb[...] = jnp.zeros_like(dvb)
    for i in range(n_blocks):
        j0 = max(0, i - 2)
        span = (i + 1 - j0) * quarter
        keys = pl.ds(j0 * quarter, span)
        grads = (wide, wide_b)
        ga = [
            only(gt[i % 2, (i // 2) * quarter : (i // 2 + 1) * quarter], h) for h in range(heads)
        ]
        for h in range(heads):
            grads[h][:, 0:span] = dot_nt(ga[h], vb[keys])

        def back(r, i=i, span=span):
            for h in range(heads):
                grad_p = grads[h][pl.ds(r, 64), 0:span]
                share = probs[i][h, pl.ds(r, 64)].astype(single)
                delta = jnp.sum(grad_p * share, axis=-1, keepdims=True)
                dsb[h, pl.ds(r, 64), 0:span] = (share * (grad_p - delta)).astype(half)

        by_rows(quarter, 64, back)
        total = None
        for h in range(heads):
            grad_s = dsb[h, :, 0:span]
            part = dot_nn(grad_s, only(kb[keys], h))
            total = part if total is None else total + part
            dkb[keys] += dot_nn(grad_s.T, only(qb[pl.ds(i * quarter, quarter)], h))
            dvb[keys] += dot_nn(probs[i][h].T, ga[h])
        dqkv[i // 2, i % 2, :, 0:ec] = (total * HD**-0.5).astype(half)
    for i in range(n_blocks):
        at = pl.ds(i * quarter, quarter)
        dqkv[i // 2, i % 2, :, ec : 2 * ec] = (dkb[at] * HD**-0.5).astype(half)
        dqkv[i // 2, i % 2, :, 2 * ec :] = dvb[at].astype(half)

    my_dx = pl.ds(pl.multiple_of(c * 3 * ec, ec), 3 * ec)
    dx_copy = send(dqkv.at[:, 1 - c], dx.at[:, :, my_dx], sib)
    dx[:, :, my_dx] = dqkv[:, c]
    for i in range(n_blocks):
        turn_rows(dqkv[i // 2, i % 2], 3 * ec, i * quarter)
    weight_grad(3 * ec, lambda at: nf[:, :, :, at].reshape(length, dz), gsq)
    qkv_z = direct_sum(gsq, grq)
    arrived(weight_sib[0])
    dx_copy.wait_recv()

    def norm1_part(xt, piece):
        return dot_nt(dx[xt], wq[piece])

    copies = spread_sum(3, norm1_part)
    for j in range(nz - 3, 0, -1):
        line_add(fc_z, j)

    sv[7:8, 0:ec] = jnp.sum(
        dqkv[:, :, :, 0:ec].astype(single).reshape(length, ec), axis=0, keepdims=True
    )
    sv[7:8, ec : 2 * ec] = jnp.sum(
        dqkv[:, :, :, 2 * ec :].astype(single).reshape(length, ec), axis=0, keepdims=True
    )

    arrived(feed_copies)
    my_rows = pl.multiple_of(c * quarter + y * block, block)

    def out_rows(r):
        at = pl.ds(r, 16)
        value = mid[at] + (summed(2, at) + proj_bias)
        outv[pl.ds(pl.multiple_of(my_rows + r, 16), 16)] = value.astype(half)

    by_rows(block, 16, out_rows)
    mine = outv.at[pl.ds(my_rows, block)]
    out_y = send(mine, mine, ynb)
    out_s = [send(mine, mine, sib)]

    def plane_sum(copies, out, home):
        arrived(copies)
        value = out[z].astype(single)
        for step in range(1, nz):
            value = value + home[(z + step) % nz].astype(single)
        return value

    line_end(fc_z)
    xf[x] = accum[...].T.astype(half)
    fc_x = send(xf.at[x], xf.at[x], xnb)
    xo[x] = plane_sum(out_z, gso, gro).astype(half)
    out_x = send(xo.at[x], xo.at[x], xnb)
    proj_x.wait_recv()
    final = [fetch(xp_, gproj_hbm)]

    theirs = outv.at[pl.ds(pl.multiple_of(c * quarter + (1 - y) * block, block), block)]
    out_y.wait_recv()
    out_s.append(send(theirs, theirs, sib))

    arrived(out_s)
    final.append(fetch(outv, out_hbm))
    arrived(copies)

    def first_back(r):
        at = pl.ds(r, 16)
        by_value, gain_part, shift_part = norm_back(
            my_x[at].astype(single), summed(3, at), gain1
        )
        gradv[pl.ds(pl.multiple_of(my_rows + r, 16), 16)] = (gmid[at] + by_value).astype(half)
        sv[1:2] += gain_part
        sv[2:3] += shift_part

    by_rows(block, 16, first_back)
    mine_g = gradv.at[pl.ds(my_rows, block)]
    grad_y = send(mine_g, mine_g, ynb)
    grad_s_ = [send(mine_g, mine_g, sib)]

    my_place = x * 4 + t
    svall[my_place] = sv[...]
    sv_copies = [send(sv, svall.at[my_place], dev) for dev in peers[0:7]]
    theirs_g = gradv.at[pl.ds(pl.multiple_of(c * quarter + (1 - y) * block, block), block)]
    xq[x] = plane_sum(qkv_z, gsq, grq).T.astype(half)
    qkv_x = send(xq.at[x], xq.at[x], xnb)
    grad_y.wait_recv()
    grad_s_.append(send(theirs_g, theirs_g, sib))

    arrived(sv_copies)
    total = svall[0]
    for place in range(1, 8):
        total = total + svall[place]
    for piece in range(nz):
        s2[piece, 0:6] = total[0:6, piece * dz : (piece + 1) * dz]
        from_x = piece // pieces
        at = (piece % pieces) * dz
        s2[piece, 6:7] = svall[from_x * 4 + t, 6:7, at : at + dz]
        s2[piece, 7:8] = svall[from_x * 4 + t, 7:8, 0:dz]
    s2r[z] = s2[z]
    s2_copies = [
        send(s2.at[(z + step) % nz], s2r.at[z], zdev(step)) for step in range(1, nz)
    ]
    arrived([fc_x])
    final.append(fetch(xf, gfc_hbm))
    arrived([out_x])
    final.append(fetch(xo, gout_hbm))
    arrived(grad_s_)
    final.append(fetch(gradv, grad_hbm))
    arrived(s2_copies)
    small = s2r[0]
    for piece in range(1, nz):
        small = small + s2r[piece]
    gvec_ref[0:7] = small[0:7]
    q_line, v_line = small[7:8, 0:ec], small[7:8, ec : 2 * ec]
    even = jnp.where(low_lane, q_line, pltpu.roll(v_line, HD, 1))
    odd = jnp.where(low_lane, pltpu.roll(q_line, HD, 1), v_line)
    gvec_ref[7:8, 0:ec] = jnp.where(z % pieces == 0, even, odd)
    gvec_ref[7:8, ec:dz] = jnp.zeros((1, dz - ec), single)
    arrived([qkv_x])
    final.append(fetch(xq, gqkv_hbm))
    for copy in final:
        copy.wait()
    for copy in started:
        copy.wait_send()


def finish_kernel(
    out,
    grad,
    gqkv,
    gout,
    gfc,
    gproj,
    gvec,
    out_ref,
    grad_ref,
    gqkv_ref,
    gout_ref,
    gfc_ref,
    gproj_ref,
    gqv_ref,
    *line_refs,
):
    single = jnp.float32
    out_ref[...] = out[...]
    grad_ref[...] = grad[...]
    ec = gqkv_ref.shape[2]
    for j in range(3):
        gqkv_ref[j] = gqkv[0, :, j * ec : (j + 1) * ec].astype(single)
    gout_ref[...] = gout[0].astype(single)
    gfc_ref[...] = gfc[0].astype(single)
    gproj_ref[...] = gproj[0].astype(single)
    pair = gqv_ref.shape[1]
    gqv_ref[0:1] = gvec[7:8, 0:pair]
    gqv_ref[1:2] = gvec[7:8, pair : 2 * pair]
    for row, ref in enumerate(line_refs):
        ref[...] = gvec[row : row + 1]


def plane_block(
    nz,
    block_input,
    segment_ids,
    cotangent,
    qkv_weight,
    qv_bias,
    out_weight,
    out_bias,
    norm1_gain,
    norm1_shift,
    fc_weight,
    fc_bias,
    proj_weight,
    proj_bias,
    norm2_gain,
    norm2_shift,
):
    half = jnp.bfloat16
    single = jnp.float32
    _, rows, width = block_input.shape
    length = segment_ids.shape[1]
    dz = qkv_weight.shape[0]
    ec = qkv_weight.shape[2] // 2
    fch = fc_weight.shape[1] // 2
    quarter, block = rows // 2, rows // 4
    vmem = pltpu.VMEM
    spans = [(i + 1 - max(0, i - 2)) * quarter for i in range(4)]
    heads = ec // HD
    scratch = [
        vmem((dz, 3 * ec), single),
        vmem((ec, dz), single),
        vmem((dz, fch), single),
        vmem((fch, dz), single),
        vmem((rows, width), half),
        vmem((2, quarter, width), half),
        vmem((2, 2, quarter, width), half),
        vmem((2, 2, quarter, width), half),
        vmem((nz, dz, 6 * ec), half),
        vmem((nz, 2 * ec, dz), half),
        vmem((2, nz, dz, fch), half),
        vmem((2, nz, fch, dz), half),
        vmem((2, nz, 8, dz), single),
        vmem((8, width), single),
        vmem((2, fch), single),
        vmem((length, ec), half),
        vmem((length, ec), half),
        vmem((length, ec), half),
    ]
    scratch += [vmem((heads, quarter, span), half) for span in spans]
    scratch += [
        vmem((length, 128), single),
        vmem((2, 2, quarter, ec), half),
        vmem((2, quarter, 2 * ec), half),
        vmem((4, 2, 2, block, width), half),
        vmem((4, 3, block, width), half),
        vmem((2, 2, block, width), single),
        vmem((block, width), single),
        vmem((2, 2, 2, block, width), half),
        vmem((2, 2, 2, block, width), half),
        vmem((2, 2, rows, fch), half),
        vmem((2, 2, rows, fch), half),
        vmem((fch, length), half),
    ]
    for _ in range(2):
        scratch += [
            vmem((nz, 3 * ec, dz), half),
            vmem((nz, ec, dz), half),
            vmem((nz, fch, dz), half),
            vmem((nz, fch, dz), half),
        ]
    scratch += [
        vmem((nz, fch, dz), half),
        vmem((nz, fch, dz), half),
        vmem((fch, dz), single),
        vmem((2, dz, 3 * ec), half),
        vmem((2, ec, dz), half),
        vmem((2, dz, fch), half),
        vmem((2, fch, dz), half),
        vmem((2, rows, ec), half),
        vmem((2, rows, ec), half),
        vmem((length, ec), single),
        vmem((length, ec), single),
        vmem((2, 2, quarter, 3 * ec), half),
        vmem((2, quarter, 6 * ec), half),
        vmem((quarter, 3 * quarter), single),
        vmem((quarter, 3 * quarter), single),
        vmem((quarter, fch), single),
        vmem((2, quarter, 3 * quarter), half),
        vmem((rows, width), half),
        vmem((rows, width), half),
        vmem((block, width), single),
        vmem((8, width), single),
        vmem((8, 8, width), single),
        vmem((nz, 8, dz), single),
        vmem((nz, 8, dz), single),
        pltpu.SemaphoreType.DMA((180,)),
        pltpu.SemaphoreType.DMA((180,)),
        pltpu.SemaphoreType.DMA((20,)),
    ]
    whole = pl.BlockSpec(memory_space=pltpu.VMEM)
    there = pl.BlockSpec(memory_space=pl.ANY)
    middle = pl.pallas_call(
        functools.partial(block_kernel, nz),
        out_shape=(
            jax.ShapeDtypeStruct((rows, width), half),
            jax.ShapeDtypeStruct((rows, width), half),
            jax.ShapeDtypeStruct((2, dz, 3 * ec), half),
            jax.ShapeDtypeStruct((2, ec, dz), half),
            jax.ShapeDtypeStruct((2, dz, fch), half),
            jax.ShapeDtypeStruct((2, fch, dz), half),
            jax.ShapeDtypeStruct((8, dz), single),
        ),
        in_specs=[there] * 2 + [whole] + [there] * 4 + [whole] * 8,
        out_specs=(there,) * 6 + (whole,),
        scratch_shapes=scratch,
        compiler_params=pltpu.CompilerParams(
            collective_id=0, has_side_effects=True, vmem_limit_bytes=67043328
        ),
        name="residual_block",
    )(
        block_input.reshape(rows, width),
        cotangent.reshape(rows, width),
        segment_ids,
        qkv_weight.transpose(1, 0, 2),
        out_weight,
        fc_weight,
        proj_weight,
        out_bias.reshape(1, dz),
        norm1_gain.reshape(1, dz),
        norm1_shift.reshape(1, dz),
        norm2_gain.reshape(1, dz),
        norm2_shift.reshape(1, dz),
        proj_bias.reshape(1, dz),
        fc_bias.reshape(1, dz),
        qv_bias,
    )

    def halves(shape, axis):
        return pl.BlockSpec(
            shape, lambda side: tuple(side if k == axis else 0 for k in range(len(shape)))
        )

    line = pl.BlockSpec((1, dz), lambda side: (0, 0))
    outs = pl.pallas_call(
        finish_kernel,
        grid=(2,),
        out_shape=(
            jax.ShapeDtypeStruct((rows, width), half),
            jax.ShapeDtypeStruct((rows, width), half),
            jax.ShapeDtypeStruct((3, dz, 2 * ec), single),
            jax.ShapeDtypeStruct((2 * ec, dz), single),
            jax.ShapeDtypeStruct((dz, 2 * fch), single),
            jax.ShapeDtypeStruct((2 * fch, dz), single),
            jax.ShapeDtypeStruct(qv_bias.shape, single),
        )
        + (jax.ShapeDtypeStruct((1, dz), single),) * 7,
        in_specs=[
            halves((quarter, width), 0),
            halves((quarter, width), 0),
            halves((1, dz, 3 * ec), 0),
            halves((1, ec, dz), 0),
            halves((1, dz, fch), 0),
            halves((1, fch, dz), 0),
            pl.BlockSpec((8, dz), lambda side: (0, 0)),
        ],
        out_specs=(
            halves((quarter, width), 0),
            halves((quarter, width), 0),
            halves((3, dz, ec), 2),
            halves((ec, dz), 0),
            halves((dz, fch), 1),
            halves((fch, dz), 0),
            pl.BlockSpec(qv_bias.shape, lambda side: (0, 0)),
        )
        + (line,) * 7,
        name="finish",
    )(*middle)
    out, grad, gqkv, gout, gfc, gproj, gqv = outs[:7]
    gbout, ggain1, gshift1, ggain2, gshift2, gbproj, gbfc = [
        value.reshape(dz) for value in outs[7:]
    ]
    return (
        out.reshape(block_input.shape),
        grad.reshape(block_input.shape),
        gqkv.transpose(1, 0, 2),
        gqv,
        gout,
        gbout,
        ggain1,
        gshift1,
        gfc,
        gbfc,
        gproj,
        gbproj,
        ggain2,
        gshift2,
    )


def device_program(mesh):
    planes = mesh.shape["fsdp"]

    def program(block_input, *others):
        seqs_here, rows, width = block_input.shape
        one_kernel = (
            seqs_here == 1
            and mesh.shape["ctx"] == 2
            and mesh.shape["tp"] == 4
            and planes == 4
            and width // planes == 256
        )
        if one_kernel:
            return plane_block(planes, block_input, *others)
        return on_device(block_input, *others)

    return program


def solution(mesh):
    return jax.shard_map(
        device_program(mesh),
        mesh=mesh,
        in_specs=(
            P("fsdp", "ctx", None),
            P("fsdp", None),
            P("fsdp", "ctx", None),
            P("fsdp", None, "tp"),
            P(None, ("tp", "fsdp")),
            P("tp", "fsdp"),
            P("fsdp"),
            P("fsdp"),
            P("fsdp"),
            P("fsdp", "tp"),
            P(("tp", "fsdp")),
            P("tp", "fsdp"),
            P("fsdp"),
            P("fsdp"),
            P("fsdp"),
        ),
        out_specs=(
            P("fsdp", "ctx", None),
            P("fsdp", "ctx", None),
            P("fsdp", None, "tp"),
            P(None, ("tp", "fsdp")),
            P("tp", "fsdp"),
            P("fsdp"),
            P("fsdp"),
            P("fsdp"),
            P("fsdp", "tp"),
            P(("tp", "fsdp")),
            P("tp", "fsdp"),
            P("fsdp"),
            P("fsdp"),
            P("fsdp"),
        ),
        check_vma=False,
    )
```

```python
import functools

import jax
import jax.numpy as jnp
from jax import lax
from jax.experimental import pallas as pl
from jax.experimental.pallas import tpu as pltpu
from jax.sharding import PartitionSpec as P

HD = 64


epsilon = 1e-05


def layer_norm(values, gain, shift):
    centred = values - jnp.mean(values, axis=-1, keepdims=True)
    spread = jnp.mean(centred * centred, axis=-1, keepdims=True)
    return centred * lax.rsqrt(spread + epsilon) * gain + shift


def gelu_act(values):
    return jax.nn.gelu(values, approximate=True)


def on_device(
    block_input,
    segment_ids,
    cotangent,
    qkv_weight,
    qv_bias,
    out_weight,
    out_bias,
    norm1_gain,
    norm1_shift,
    fc_weight,
    fc_bias,
    proj_weight,
    proj_bias,
    norm2_gain,
    norm2_shift,
):
    half = jnp.bfloat16
    single = jnp.float32
    seqs_here, rows_seq, model_width = block_input.shape
    row_count = seqs_here * rows_seq
    shard_index = lax.axis_index("ctx")
    scale_factor = HD ** (-0.5)
    (
        wqkv_low,
        bqv_low,
        wout_low,
        bout_low,
        gain1_low,
        shift1_low,
        wfc_low,
        bfc_low,
        wproj_low,
        bproj_low,
        gain2_low,
        shift2_low,
    ) = (
        lax.all_gather(qkv_weight.astype(half), "fsdp", axis=0, tiled=True),
        lax.all_gather(qv_bias.astype(half), "fsdp", axis=1, tiled=True),
        lax.all_gather(out_weight.astype(half), "fsdp", axis=1, tiled=True),
        lax.all_gather(out_bias.astype(half), "fsdp", axis=0, tiled=True),
        lax.all_gather(norm1_gain.astype(half), "fsdp", axis=0, tiled=True),
        lax.all_gather(norm1_shift.astype(half), "fsdp", axis=0, tiled=True),
        lax.all_gather(fc_weight.astype(half), "fsdp", axis=0, tiled=True),
        lax.all_gather(fc_bias.astype(half), "fsdp", axis=0, tiled=True),
        lax.all_gather(proj_weight.astype(half), "fsdp", axis=1, tiled=True),
        lax.all_gather(proj_bias.astype(half), "fsdp", axis=0, tiled=True),
        lax.all_gather(norm2_gain.astype(half), "fsdp", axis=0, tiled=True),
        lax.all_gather(norm2_shift.astype(half), "fsdp", axis=0, tiled=True),
    )
    gain_first = gain1_low.astype(single)
    shift_first = shift1_low.astype(single)
    gain_second = gain2_low.astype(single)
    shift_second = shift2_low.astype(single)
    inputs = block_input.reshape(row_count, model_width).astype(single)
    normed_first = layer_norm(inputs, gain_first, shift_first).astype(half)
    projected = jnp.einsum("rd,dce->rce", normed_first, wqkv_low, preferred_element_type=single)
    bias_pair = bqv_low.astype(single)
    queries = (projected[:, 0] + bias_pair[0]).astype(half)
    key_rows = projected[:, 1].astype(half)
    value_rows = (projected[:, 2] + bias_pair[1]).astype(half)
    local_width = queries.shape[1]
    head_count = local_width // HD
    keys_all, values_all = (
        lax.all_gather(
            key_rows.reshape(seqs_here, rows_seq, local_width), "ctx", axis=1, tiled=True
        ),
        lax.all_gather(
            value_rows.reshape(seqs_here, rows_seq, local_width), "ctx", axis=1, tiled=True
        ),
    )
    length = keys_all.shape[1]
    query_pos = shard_index * rows_seq + jnp.arange(rows_seq)
    key_pos = jnp.arange(length)
    seg_query = lax.dynamic_slice_in_dim(segment_ids, shard_index * rows_seq, rows_seq, 1)
    query_heads = queries.reshape(seqs_here, rows_seq, head_count, HD)
    key_heads = keys_all.reshape(seqs_here, length, head_count, HD)
    value_heads = values_all.reshape(seqs_here, length, head_count, HD)

    def masked_scores(query_blk, key_blk, seg_row, seg_here):
        raw = (
            jnp.einsum("qhe,khe->hqk", query_blk, key_blk, preferred_element_type=single)
            * scale_factor
        )
        allowed = (key_pos[None, :] <= query_pos[:, None]) & (seg_here[:, None] == seg_row[None, :])
        return jnp.where(allowed[None], raw, -1e30)

    def attend(packed):
        query_blk, key_blk, value_blk, seg_row, seg_here = packed
        masked = masked_scores(query_blk, key_blk, seg_row, seg_here)
        row_max = jnp.max(masked, axis=-1, keepdims=True)
        expo = jnp.exp(masked - row_max)
        row_total = jnp.sum(expo, axis=-1, keepdims=True)
        probs_low = (expo / row_total).astype(half)
        attended = jnp.einsum("hqk,khe->qhe", probs_low, value_blk, preferred_element_type=single)
        return (attended.astype(half), row_max + jnp.log(row_total))

    attended, log_total = lax.map(
        attend, (query_heads, key_heads, value_heads, segment_ids, seg_query)
    )
    attended_rows = attended.reshape(row_count, local_width)
    attn_partial = jnp.dot(attended_rows, wout_low, preferred_element_type=single)
    attn_total = lax.psum(attn_partial.astype(jnp.bfloat16), "tp").astype(jnp.float32)
    middle = inputs + attn_total + bout_low.astype(single)
    normed_second = layer_norm(middle, gain_second, shift_second).astype(half)
    pre_act = jnp.dot(normed_second, wfc_low, preferred_element_type=single) + bfc_low.astype(
        single
    )
    act_low = gelu_act(pre_act).astype(half)
    mlp_total = lax.psum(
        jnp.dot(act_low, wproj_low, preferred_element_type=single).astype(jnp.bfloat16), "tp"
    ).astype(jnp.float32)
    out_rows = (middle + mlp_total + bproj_low.astype(single)).astype(half)
    wqkv_use, wout_use, wfc_use, wproj_use = (
        lax.all_gather(qkv_weight.astype(half), "fsdp", axis=0, tiled=True),
        lax.all_gather(out_weight.astype(half), "fsdp", axis=1, tiled=True),
        lax.all_gather(fc_weight.astype(half), "fsdp", axis=0, tiled=True),
        lax.all_gather(proj_weight.astype(half), "fsdp", axis=1, tiled=True),
    )
    grad_out = cotangent.reshape(row_count, model_width).astype(single)
    grad_out_low = cotangent.reshape(row_count, model_width)
    grad_bproj = jnp.sum(grad_out_low, axis=0, dtype=single)
    grad_wproj = jnp.einsum("rf,rd->fd", act_low, grad_out_low, preferred_element_type=single)
    grad_act = jnp.einsum("rd,fd->rf", grad_out_low, wproj_use, preferred_element_type=single)
    gelu_unused, gelu_pull = jax.vjp(gelu_act, pre_act)
    grad_pre = gelu_pull(grad_act)[0].astype(half)
    grad_bfc = jnp.sum(grad_pre, axis=0, dtype=single)
    grad_wfc = jnp.einsum("rd,rf->df", normed_second, grad_pre, preferred_element_type=single)
    norm2_partial = jnp.einsum("rf,df->rd", grad_pre, wfc_use, preferred_element_type=single)
    grad_norm2 = lax.psum(norm2_partial.astype(jnp.bfloat16), "tp").astype(jnp.float32)
    norm_unused, second_pull = jax.vjp(layer_norm, middle, gain_second, shift_second)
    grad_mid_ln, grad_gain2, grad_shift2 = second_pull(grad_norm2)
    grad_middle = grad_out + grad_mid_ln
    grad_mid_low = grad_middle.astype(half)
    grad_bout = jnp.sum(grad_mid_low, axis=0, dtype=single)
    grad_wout = jnp.einsum("rk,rd->kd", attended_rows, grad_mid_low, preferred_element_type=single)
    grad_att = jnp.einsum(
        "rd,kd->rk", grad_mid_low, wout_use, preferred_element_type=single
    ).astype(half)
    grad_att_heads = grad_att.reshape(seqs_here, rows_seq, head_count, HD)

    def attend_back(packed):
        query_blk, key_blk, value_blk, seg_row, seg_here, log_blk, grad_blk = packed
        masked = masked_scores(query_blk, key_blk, seg_row, seg_here)
        attn_probs = jnp.exp(masked - log_blk)
        probs_low = attn_probs.astype(half)
        grad_value = jnp.einsum("hqk,qhe->khe", probs_low, grad_blk, preferred_element_type=single)
        grad_probs = jnp.einsum("qhe,khe->hqk", grad_blk, value_blk, preferred_element_type=single)
        row_delta = jnp.sum(grad_probs * attn_probs, axis=-1, keepdims=True)
        grad_scores = (attn_probs * (grad_probs - row_delta)).astype(half)
        grad_query = (
            jnp.einsum("hqk,khe->qhe", grad_scores, key_blk, preferred_element_type=single)
            * scale_factor
        )
        grad_key = (
            jnp.einsum("hqk,qhe->khe", grad_scores, query_blk, preferred_element_type=single)
            * scale_factor
        )
        return (grad_query.astype(half), grad_key, grad_value)

    grad_query, grad_key, grad_value = lax.map(
        attend_back,
        (query_heads, key_heads, value_heads, segment_ids, seg_query, log_total, grad_att_heads),
    )
    grad_key, grad_value = (
        lax.psum_scatter(
            grad_key.reshape(seqs_here, length, local_width).astype(jnp.bfloat16),
            "ctx",
            scatter_dimension=1,
            tiled=True,
        ).astype(jnp.float32),
        lax.psum_scatter(
            grad_value.reshape(seqs_here, length, local_width).astype(jnp.bfloat16),
            "ctx",
            scatter_dimension=1,
            tiled=True,
        ).astype(jnp.float32),
    )
    grad_query = grad_query.reshape(row_count, local_width)
    grad_key = grad_key.reshape(row_count, local_width).astype(half)
    grad_value = grad_value.reshape(row_count, local_width).astype(half)
    grad_qkv = jnp.stack([grad_query, grad_key, grad_value], axis=1)
    grad_bqv = jnp.stack(
        [jnp.sum(grad_query, axis=0, dtype=single), jnp.sum(grad_value, axis=0, dtype=single)]
    )
    grad_wqkv = jnp.einsum("rd,rce->dce", normed_first, grad_qkv, preferred_element_type=single)
    norm1_partial = jnp.einsum("rce,dce->rd", grad_qkv, wqkv_use, preferred_element_type=single)
    grad_norm1 = lax.psum(norm1_partial.astype(jnp.bfloat16), "tp").astype(jnp.float32)
    first_unused, first_pull = jax.vjp(layer_norm, inputs, gain_first, shift_first)
    grad_in_ln, grad_gain1, grad_shift1 = first_pull(grad_norm1)
    input_rows = (grad_middle + grad_in_ln).astype(half)
    block_output = out_rows.reshape(block_input.shape)
    input_grad = input_rows.reshape(block_input.shape)
    (
        sum_wqkv,
        sum_bqv,
        sum_wout,
        sum_bout,
        sum_gain1,
        sum_shift1,
        sum_wfc,
        sum_bfc,
        sum_wproj,
        sum_bproj,
        sum_gain2,
        sum_shift2,
    ) = (
        lax.psum_scatter(grad_wqkv, ("fsdp", "ctx"), scatter_dimension=0, tiled=True),
        lax.psum_scatter(grad_bqv, ("fsdp", "ctx"), scatter_dimension=1, tiled=True),
        lax.psum_scatter(grad_wout, ("fsdp", "ctx"), scatter_dimension=1, tiled=True),
        lax.psum_scatter(grad_bout, ("fsdp", "ctx"), scatter_dimension=0, tiled=True),
        lax.psum_scatter(grad_gain1, ("fsdp", "ctx"), scatter_dimension=0, tiled=True),
        lax.psum_scatter(grad_shift1, ("fsdp", "ctx"), scatter_dimension=0, tiled=True),
        lax.psum_scatter(grad_wfc, ("fsdp", "ctx"), scatter_dimension=0, tiled=True),
        lax.psum_scatter(grad_bfc, ("fsdp", "ctx"), scatter_dimension=0, tiled=True),
        lax.psum_scatter(grad_wproj, ("fsdp", "ctx"), scatter_dimension=1, tiled=True),
        lax.psum_scatter(grad_bproj, ("fsdp", "ctx"), scatter_dimension=0, tiled=True),
        lax.psum_scatter(grad_gain2, ("fsdp", "ctx"), scatter_dimension=0, tiled=True),
        lax.psum_scatter(grad_shift2, ("fsdp", "ctx"), scatter_dimension=0, tiled=True),
    )
    (
        final_wqkv,
        final_bqv,
        final_wout,
        final_bout,
        final_gain1,
        final_shift1,
        final_wfc,
        final_bfc,
        final_wproj,
        final_bproj,
        final_gain2,
        final_shift2,
    ) = (
        lax.all_gather(sum_wqkv.astype(jnp.bfloat16), "ctx", axis=0, tiled=True).astype(
            sum_wqkv.dtype
        ),
        lax.all_gather(sum_bqv.astype(jnp.bfloat16), "ctx", axis=1, tiled=True).astype(
            sum_bqv.dtype
        ),
        lax.all_gather(sum_wout.astype(jnp.bfloat16), "ctx", axis=1, tiled=True).astype(
            sum_wout.dtype
        ),
        lax.all_gather(sum_bout.astype(jnp.bfloat16), "ctx", axis=0, tiled=True).astype(
            sum_bout.dtype
        ),
        lax.all_gather(sum_gain1.astype(jnp.bfloat16), "ctx", axis=0, tiled=True).astype(
            sum_gain1.dtype
        ),
        lax.all_gather(sum_shift1.astype(jnp.bfloat16), "ctx", axis=0, tiled=True).astype(
            sum_shift1.dtype
        ),
        lax.all_gather(sum_wfc.astype(jnp.bfloat16), "ctx", axis=0, tiled=True).astype(
            sum_wfc.dtype
        ),
        lax.all_gather(sum_bfc.astype(jnp.bfloat16), "ctx", axis=0, tiled=True).astype(
            sum_bfc.dtype
        ),
        lax.all_gather(sum_wproj.astype(jnp.bfloat16), "ctx", axis=1, tiled=True).astype(
            sum_wproj.dtype
        ),
        lax.all_gather(sum_bproj.astype(jnp.bfloat16), "ctx", axis=0, tiled=True).astype(
            sum_bproj.dtype
        ),
        lax.all_gather(sum_gain2.astype(jnp.bfloat16), "ctx", axis=0, tiled=True).astype(
            sum_gain2.dtype
        ),
        lax.all_gather(sum_shift2.astype(jnp.bfloat16), "ctx", axis=0, tiled=True).astype(
            sum_shift2.dtype
        ),
    )
    return (
        block_output,
        input_grad,
        final_wqkv,
        final_bqv,
        final_wout,
        final_bout,
        final_gain1,
        final_shift1,
        final_wfc,
        final_bfc,
        final_wproj,
        final_bproj,
        final_gain2,
        final_shift2,
    )


MESH = pl.DeviceIdType.MESH


def dot_nn(left, right):
    return lax.dot_general(
        left, right, (((1,), (0,)), ((), ())), preferred_element_type=jnp.float32
    )


def dot_nt(left, right):
    return lax.dot_general(
        left, right, (((1,), (1,)), ((), ())), preferred_element_type=jnp.float32
    )


def by_rows(rows, step, body):
    def one(index, carry):
        body(pl.multiple_of(index * step, step))
        return carry

    lax.fori_loop(0, rows // step, one, 0)


def norm_parts(values):
    centred = values - jnp.mean(values, axis=-1, keepdims=True)
    spread = jnp.mean(centred * centred, axis=-1, keepdims=True)
    return centred, lax.rsqrt(spread + epsilon)


def norm_back(values, incoming, gain):
    centred, rate = norm_parts(values)
    hat = centred * rate
    scaled = incoming * gain
    by_value = rate * (
        scaled
        - jnp.mean(scaled, axis=-1, keepdims=True)
        - hat * jnp.mean(scaled * hat, axis=-1, keepdims=True)
    )
    return (
        by_value,
        jnp.sum(incoming * hat, axis=0, keepdims=True),
        jnp.sum(incoming, axis=0, keepdims=True),
    )


class Partly:
    def __init__(self, copy, sends, receives):
        self.copy, self.sends, self.receives = copy, sends, receives

    def start(self):
        self.copy.start()

    def wait_recv(self):
        pl.when(self.receives)(self.copy.wait_recv)

    def wait_send(self):
        pl.when(self.sends)(self.copy.wait_send)


def block_kernel(
    nz,
    x_in,
    dy_in,
    seg_row,
    wqkv_in,
    wout_in,
    wfc_in,
    wproj_in,
    bout_in,
    gain1_in,
    shift1_in,
    gain2_in,
    shift2_in,
    bproj_in,
    bfc_in,
    bqv_in,
    out_hbm,
    grad_hbm,
    gqkv_hbm,
    gout_hbm,
    gfc_hbm,
    gproj_hbm,
    gvec_ref,
    stq,
    sto,
    stf,
    stp,
    xl,
    xr,
    dyb,
    nf,
    wq,
    wo,
    wf,
    wp,
    vec,
    full,
    fcb,
    qb,
    kb,
    vb,
    p0,
    p1,
    p2,
    p3,
    segc,
    ao,
    ax,
    srs,
    rrs,
    own,
    mid,
    ns,
    gm,
    act,
    gp,
    turned,
    gsq,
    gso,
    gsf,
    gsp,
    grq,
    gro,
    grf,
    grp,
    glf,
    glp,
    accum,
    xq,
    xo,
    xf,
    xp_,
    gtt,
    gt,
    dkb,
    dvb,
    dqkv,
    dx,
    wide,
    wide_b,
    slope,
    dsb,
    outv,
    gradv,
    gmid,
    sv,
    svall,
    late,
    lateall,
    l2,
    l2r,
    s2,
    s2r,
    send_sem,
    recv_sem,
    local_sem,
):
    half = jnp.bfloat16
    single = jnp.float32
    z = lax.axis_index("fsdp")
    x = lax.axis_index("ctx")
    t = lax.axis_index("tp")
    y = t // 2
    c = t % 2
    quarter = xl.shape[0] // 2
    block = quarter // 2
    width = xl.shape[1]
    dz = width // nz
    fch = wf.shape[3]
    ec = qb.shape[1]
    length = qb.shape[0]
    probs = (p0, p1, p2, p3)
    sib = (z, x, y * 2 + 1 - c)
    ynb = (z, x, (1 - y) * 2 + c)
    xnb = (z, 1 - x, t)
    dia = (z, 1 - x, (1 - y) * 2 + c)
    started = []

    def send(src, dst, dev):
        slot = len(started)
        copy = pltpu.make_async_remote_copy(
            src_ref=src,
            dst_ref=dst,
            send_sem=send_sem.at[slot],
            recv_sem=recv_sem.at[slot],
            device_id=dev,
            device_id_type=MESH,
        )
        copy.start()
        started.append(copy)
        return copy

    def arrived(copies):
        for copy in copies:
            copy.wait_recv()

    def send_if(src, dst, dev, sends, receives, start=True):
        slot = len(started)
        copy = pltpu.make_async_remote_copy(
            src_ref=src,
            dst_ref=dst,
            send_sem=send_sem.at[slot],
            recv_sem=recv_sem.at[slot],
            device_id=dev,
            device_id_type=MESH,
        )
        some = Partly(copy, sends, receives)
        if start:
            pl.when(sends)(copy.start)
        started.append(some)
        return some

    fetched = []

    def fetch(src, dst):
        copy = pltpu.make_async_copy(src, dst, local_sem.at[len(fetched)])
        copy.start()
        fetched.append(copy)
        return copy

    def zdev(step):
        return ((z + step) % nz, x, t)

    right, left = zdev(1), zdev(nz - 1)

    peers = [(z, px, pt) for px in (x, 1 - x) for pt in (t, sib[2], ynb[2], (1 - y) * 2 + 1 - c)][
        1:
    ]
    for step in range(1, nz):
        peers += [((z + step) % nz, x, t), ((z + step) % nz, x, sib[2])]
    barrier = pltpu.get_barrier_semaphore()
    for dev in peers:
        pl.semaphore_signal(barrier, inc=1, device_id=dev, device_id_type=MESH)

    my_e = pl.ds(pl.multiple_of(x * ec, ec), ec)
    my_f = pl.ds(pl.multiple_of(x * fch, fch), fch)
    stage_q = [
        fetch(wqkv_in.at[j, :, my_e], stq.at[:, j * ec : (j + 1) * ec]) for j in range(3)
    ]
    stage_x = fetch(x_in, xl)
    stage_o = fetch(wout_in.at[my_e], sto)
    stage_f = fetch(wfc_in.at[:, my_f], stf)
    stage_p = fetch(wproj_in.at[my_f], stp)
    stage_dy = [
        fetch(dy_in.at[pl.ds(s * quarter, quarter)], dyb.at[s, x]) for s in range(2)
    ]

    def weight_at(which, h, plane):
        if which == 0:
            return wq.at[plane, :, pl.ds(pl.multiple_of(h * 3 * ec, ec), 3 * ec)]
        if which == 1:
            return wo.at[plane, pl.ds(pl.multiple_of(h * ec, ec), ec)]
        if which == 2:
            return wf.at[h, plane]
        part = fch // 2
        return wp.at[h, plane, (which - 3) * part : (which - 2) * part]

    def rounded(src, dst, rows):
        def some(r):
            dst[pl.ds(r, 64)] = src[pl.ds(r, 64)].astype(half)

        by_rows(rows, 64, some)

    lines = [[], [], [], [], []]
    weight_sib = [[], [], [], [], []]

    def line_start(which):
        mine = weight_at(which, c, z)
        lines[which].append(
            (
                send_if(mine, mine, right, z < nz - 1, z >= 1),
                send_if(mine, mine, left, z >= 1, z < nz - 1),
            )
        )

    def line_pass(which, step):
        from_left, from_right = lines[which][step - 1]
        lower = weight_at(which, c, (z + nz - step) % nz)
        upper = weight_at(which, c, (z + step) % nz)
        from_left.wait_recv()
        if step < nz - 1:
            to_right = send_if(
                lower, lower, right, (z >= step) & (z < nz - 1), z >= step + 1
            )
        weight_sib[which].append(send_if(lower, lower, sib, z >= step, z >= step))
        from_right.wait_recv()
        if step < nz - 1:
            to_left = send_if(
                upper, upper, left, (z + step < nz) & (z >= 1), z + step + 1 < nz
            )
            lines[which].append((to_right, to_left))
        weight_sib[which].append(send_if(upper, upper, sib, z + step < nz, z + step < nz))

    def to_sibling(which):
        mine = weight_at(which, c, z)
        weight_sib[which].append(send(mine, mine, sib))

    for copy in stage_q:
        copy.wait()
    rounded(stq, weight_at(0, c, z), dz)
    for row, line in enumerate(
        (bout_in, gain1_in, shift1_in, gain2_in, shift2_in, bproj_in, bfc_in)
    ):
        vec[c, z, row : row + 1] = line[...].astype(half).astype(single)
    pair = bqv_in.shape[1]
    vec[c, z, 7:8, 0:pair] = bqv_in[0:1].astype(half).astype(single)
    vec[c, z, 7:8, pair : 2 * pair] = bqv_in[1:2].astype(half).astype(single)
    vec[c, z, 7:8, 2 * pair :] = jnp.zeros((1, dz - 2 * pair), single)
    pl.semaphore_wait(barrier, len(peers))

    line_start(0)
    stage_x.wait()
    x_copy = send(xl.at[pl.ds(pl.multiple_of(c * quarter, quarter), quarter)], xr.at[c], xnb)
    vec_copies = [send(vec.at[c, z], vec.at[c, z], sib)]
    for step in range(1, nz):
        for dev_t in (t, sib[2]):
            vec_copies.append(send(vec.at[c, z], vec.at[c, z], ((z + step) % nz, x, dev_t)))
    stage_o.wait()
    rounded(sto, weight_at(1, c, z), ec)
    line_start(1)
    to_sibling(0)
    to_sibling(1)
    for copy in stage_dy:
        copy.wait()
    stage_f.wait()
    rounded(stf, weight_at(2, c, z), dz)
    stage_p.wait()
    rounded(stp, wp.at[c, z], fch)

    arrived(vec_copies)
    for piece in range(nz):
        full[:, piece * dz : (piece + 1) * dz] = vec[c, piece]
    pieces = nz // 2
    for h in range(2):
        for k in range(pieces):
            fcb[h : h + 1, k * dz : (k + 1) * dz] = vec[h, x * pieces + k][6:7]
    lane = lax.broadcasted_iota(jnp.int32, (1, ec), 1)
    low_lane = lane < HD
    first_piece = vec[c, x * pieces][7:8, 0:ec]
    next_piece = vec[c, x * pieces + 1][7:8, 0:ec]
    q_bias = jnp.where(low_lane, first_piece, pltpu.roll(next_piece, HD, 1))
    v_bias = jnp.where(low_lane, pltpu.roll(first_piece, HD, 1), next_piece)
    out_bias = full[0:1]
    gain1, shift1 = full[1:2], full[2:3]
    gain2, shift2 = full[3:4], full[4:5]
    proj_bias = full[5:6]

    def first_norm(src, dst):
        def rows(r):
            centred, rate = norm_parts(src[pl.ds(r, 64)].astype(single))
            dst[pl.ds(r, 64)] = (centred * rate * gain1 + shift1).astype(half)

        by_rows(quarter, 64, rows)

    for s in range(2):
        first_norm(xl.at[pl.ds(s * quarter, quarter)], nf.at[x, s])
    line_pass(0, 1)
    line_pass(1, 1)
    x_copy.wait_recv()
    x_fwd = send(xr.at[c], xr.at[c], sib)
    dy_copy = send(dyb.at[c, x], dyb.at[c, x], xnb)
    first_norm(xr.at[c], nf.at[1 - x, c])
    line_pass(0, 2)
    line_pass(1, 2)
    line_start(2)
    line_start(3)
    to_sibling(2)
    to_sibling(3)
    to_sibling(4)
    x_fwd.wait_recv()
    first_norm(xr.at[1 - c], nf.at[1 - x, 1 - c])
    for i in range(length // quarter):
        line = seg_row[:, i * quarter : (i + 1) * quarter].astype(single)
        segc[i * quarter : (i + 1) * quarter] = jnp.broadcast_to(line, (128, quarter)).T
    for step in range(3, nz):
        line_pass(0, step)
        line_pass(1, step)

    my_qkv = pl.ds(pl.multiple_of(c * 3 * ec, ec), 3 * ec)
    for xi in range(2):
        for ci in range(2):
            proj = dot_nn(nf[xi, ci], wq[:, :, my_qkv].reshape(width, 3 * ec))
            at = pl.ds((xi * 2 + ci) * quarter, quarter)
            qb[at] = (proj[:, 0:ec] + q_bias).astype(half)
            kb[at] = proj[:, ec : 2 * ec].astype(half)
            vb[at] = (proj[:, 2 * ec :] + v_bias).astype(half)

    head_lane = lax.broadcasted_iota(jnp.int32, (1, ec), 1) // HD
    n_blocks = length // quarter
    heads = ec // HD

    def only(values, h):
        return jnp.where(head_lane == h, values, jnp.zeros_like(values))

    for i in range(n_blocks):
        j0 = max(0, i - 2)
        span = (i + 1 - j0) * quarter
        keys = pl.ds(j0 * quarter, span)
        scores = (wide, wide_b)
        for h in range(heads):
            q_h = only(qb[pl.ds(i * quarter, quarter)], h) * jnp.asarray(HD**-0.5, half)
            scores[h][:, 0:span] = dot_nt(q_h, kb[keys])

        def soft(r, i=i, j0=j0, span=span):
            q_at = i * quarter + r + lax.broadcasted_iota(jnp.int32, (64, span), 0)
            k_at = j0 * quarter + lax.broadcasted_iota(jnp.int32, (64, span), 1)
            seg_q = segc[pl.ds(pl.multiple_of(i * quarter + r, 64), 64)]
            seg_k = seg_row[:, j0 * quarter : j0 * quarter + span].astype(single)
            same = jnp.concatenate([seg_q] * (span // 128), axis=1) == seg_k
            allowed = (k_at <= q_at) & same
            for h in range(heads):
                masked = jnp.where(allowed, scores[h][pl.ds(r, 64), 0:span], -1e30)
                expo = jnp.exp(masked - jnp.max(masked, axis=-1, keepdims=True))
                share = expo * (1.0 / jnp.sum(expo, axis=-1, keepdims=True))
                probs[i][h, pl.ds(r, 64)] = share.astype(half)

        by_rows(quarter, 64, soft)
        total = None
        for h in range(heads):
            part = dot_nn(probs[i][h], only(vb[keys], h))
            total = part if total is None else total + part
        ao[i // 2, i % 2] = total.astype(half)

    my_ax = pl.ds(pl.multiple_of(c * ec, ec), ec)
    att_copy = send(ao.at[:, 1 - c], ax.at[:, :, my_ax], sib)
    ax[:, :, my_ax] = ao[:, c]
    arrived(weight_sib[1])
    att_copy.wait_recv()

    split = width // 2

    def spread_part(k, part, turn, side):
        xt = x if turn else 1 - x

        def columns(piece, carry):
            value = part(xt, side * (nz // 2) + piece)
            at = pl.ds(pl.multiple_of(piece * dz, dz), dz)
            for yi in range(2):
                rows = value[yi * block : (yi + 1) * block]
                srs[k, turn, yi, side, :, at] = rows.astype(half)
                if turn:
                    own[k, yi, side, :, at] = rows
            return carry

        lax.fori_loop(0, nz // 2, columns, 0)

    def spread_first(k):
        return [
            send(srs.at[k, 0, 1 - y, 0], rrs.at[k, 0], xnb),
            send(srs.at[k, 0, y, 0], rrs.at[k, 2], xnb),
        ]

    def spread_second(k):
        return [send(srs.at[k, 0, 1 - y, 1], rrs.at[k, 1], ynb)]

    def spread_third(k):
        return [send(srs.at[k, 1, 1 - y, 1], rrs.at[k, 5], ynb)]

    def spread_pass(k, copies):
        copies[0].wait_recv()
        srs[k, 1, 1 - y, 0] = (
            srs[k, 1, 1 - y, 0].astype(single) + rrs[k, 0].astype(single)
        ).astype(half)
        last = [send(srs.at[k, 1, 1 - y, 0], rrs.at[k, 4], ynb)]
        copies[2].wait_recv()
        srs[k, 0, y, 1] = (srs[k, 0, y, 1].astype(single) + rrs[k, 1].astype(single)).astype(half)
        last.append(send(srs.at[k, 0, y, 1], rrs.at[k, 3], xnb))
        return [copies[1], copies[3]] + last

    def spread_sum(k, part):
        spread_part(k, part, 0, 0)
        copies = spread_first(k)
        spread_part(k, part, 0, 1)
        copies += spread_second(k)
        spread_part(k, part, 1, 1)
        copies += spread_third(k)
        spread_part(k, part, 1, 0)
        return copies

    def summed(k, at):
        sides = [
            own[k, y, side, at]
            + (rrs[k, 2 + side, at].astype(single) + rrs[k, 4 + side, at].astype(single))
            for side in range(2)
        ]
        return jnp.concatenate(sides, axis=1)

    def attention_out(xt, piece):
        return dot_nn(ax[xt], wo[piece])

    copies = spread_sum(0, attention_out)
    line_pass(2, 1)
    line_start(4)
    copies = spread_pass(0, copies)
    dy_copy.wait_recv()
    dy_fwd = send(dyb.at[c, 1 - x], dyb.at[c, 1 - x], sib)
    line_pass(3, 1)
    arrived(copies)

    my_x = xl.at[pl.ds(pl.multiple_of(c * quarter + y * block, block), block)]

    def middle_rows(r):
        at = pl.ds(r, 32)
        value = my_x[at].astype(single) + (summed(0, at) + out_bias)
        mid[at] = value
        centred, rate = norm_parts(value)
        ns[c, x, y, at] = (centred * rate * gain2 + shift2).astype(half)

    lower, upper = pl.ds(0, block // 2), pl.ds(block // 2, block // 2)

    def gather_first(buf):
        return [send(buf.at[c, x, y, lower], buf.at[c, x, y, lower], xnb)]

    def gather_rest(buf):
        mine = buf.at[c, x, y]
        return [
            send(mine.at[upper], mine.at[upper], ynb),
            send(mine.at[upper], mine.at[upper], xnb),
            send(mine.at[lower], mine.at[lower], ynb),
            send(mine, mine, sib),
        ]

    def gather_pass(buf, copies):
        by_x, by_y = buf.at[c, 1 - x, y, lower], buf.at[c, x, 1 - y, upper]
        copies[0].wait_recv()
        through = [send(by_x, by_x, ynb)]
        copies[1].wait_recv()
        through.append(send(by_y, by_y, xnb))
        return through

    def halves_of_block(step, body, between):
        def low(r):
            body(r)

        by_rows(block // 2, step, low)
        first = between()

        def high(r):
            body(pl.multiple_of(r + block // 2, step))

        by_rows(block // 2, step, high)
        return first

    copies = halves_of_block(32, middle_rows, lambda: gather_first(ns))
    copies += gather_rest(ns)
    line_pass(2, 2)
    through = gather_pass(ns, copies)
    ns_sib = [copies[4]]

    def pass_block(buf, bx, by):
        return send(buf.at[c, bx, by], buf.at[c, bx, by], sib)

    line_pass(4, 1)
    copies[3].wait_recv()
    ns_sib.append(pass_block(ns, x, 1 - y))
    copies[2].wait_recv()
    ns_sib.append(pass_block(ns, 1 - x, y))
    for step in range(3, nz):
        line_pass(2, step)
    arrived(weight_sib[2])

    def hidden(xt):
        rows_ns = ns[c, xt].reshape(quarter, width)
        for h in range(2):
            wide[:, 0:fch] = dot_nn(rows_ns, wf[h].reshape(width, fch))

            def rows(r, h=h):
                value = wide[pl.ds(r, 64), 0:fch] + fcb[h : h + 1]
                root = 0.7978845608028654
                square = value * value
                inner = jnp.tanh(root * (value + 0.044715 * (square * value)))
                lift = 0.5 * (1.0 + inner)
                at = pl.ds(pl.multiple_of(xt * quarter + r, 64), 64)
                act[c, h, at] = (value * lift).astype(half)
                slope[h, at] = lift + 0.5 * value * (1.0 - inner * inner) * (
                    root * (1.0 + 3.0 * 0.044715 * square)
                )

            by_rows(quarter, 64, rows)

    def hidden_grad(xt, which):
        at = pl.ds(pl.multiple_of(xt * quarter, quarter), quarter)
        part_at = slice((which - 3) * (fch // 2), (which - 2) * (fch // 2))
        for h in range(2):
            grad = None
            for piece in range(nz):
                part = dot_nt(
                    dyb[c, xt, :, piece * dz : (piece + 1) * dz],
                    wp[h, piece, part_at],
                )
                grad = part if grad is None else grad + part
            gp[c, h, at, part_at] = (grad * slope[h, at, part_at]).astype(half)

    hidden(x)
    line_pass(3, 2)
    arrived(through)
    ns_sib.append(pass_block(ns, 1 - x, 1 - y))
    hidden(1 - x)
    act_copy = send(act.at[c, 1 - c], act.at[c, 1 - c], sib)
    line_pass(4, 2)

    def weight_grad(left, right_at, out):
        def one(step, carry):
            piece = (z + step) % nz
            at = pl.ds(pl.multiple_of(piece * dz, dz), dz)
            out[piece] = dot_nn(turned[0:left], right_at(at)).astype(half)
            return carry

        lax.fori_loop(0, nz, one, 0)

    def direct_sum(out, home):
        return [
            send(out.at[(z + step) % nz], home.at[z], zdev(step)) for step in range(1, nz)
        ]

    def line_sum(out, up, down):
        rights, lefts = {}, {}
        for k in range(nz - 1, 0, -1):
            upper, lower = (z + k) % nz, (z + nz - k) % nz
            rights[k] = send_if(
                out.at[upper],
                up.at[upper],
                right,
                z + k < nz,
                (z >= 1) & (z - 1 + k < nz),
                start=False,
            )
            lefts[k] = send_if(
                out.at[lower],
                down.at[lower],
                left,
                z >= k,
                (z < nz - 1) & (z + 1 >= k),
                start=False,
            )
            pl.when((z == 0) & (z + k < nz))(rights[k].start)
            pl.when((z == nz - 1) & (z >= k))(lefts[k].start)
        return out, up, down, rights, lefts

    def line_add(line, j):
        out, up, down, rights, lefts = line
        upper, lower = (z + j) % nz, (z + nz - j) % nz

        @pl.when((z >= 1) & (z + j < nz))
        def _():
            rights[j + 1].copy.wait_recv()
            out[upper] = (out[upper].astype(single) + up[upper].astype(single)).astype(half)
            rights[j].start()

        @pl.when((z < nz - 1) & (z >= j))
        def _():
            lefts[j + 1].copy.wait_recv()
            out[lower] = (out[lower].astype(single) + down[lower].astype(single)).astype(half)
            lefts[j].start()

    def line_end(line):
        out, up, down, rights, lefts = line
        accum[...] = out[z].astype(single)

        @pl.when(z >= 1)
        def _():
            rights[1].copy.wait_recv()
            accum[...] += up[z].astype(single)

        @pl.when(z < nz - 1)
        def _():
            lefts[1].copy.wait_recv()
            accum[...] += down[z].astype(single)

    def turn_rows(src, left, column):
        turned[0:left, pl.ds(pl.multiple_of(column, quarter), quarter)] = src.T

    dy_fwd.wait_recv()
    act_copy.wait_recv()
    for s in range(2):
        for k in range(2):
            turn_rows(act[s, c, k * quarter : (k + 1) * quarter], fch, (s * 2 + k) * quarter)
    weight_grad(fch, lambda at: dyb[:, :, :, at].reshape(length, dz), gsp)
    proj_z = line_sum(gsp, grp, glp)
    for which in (3, 4):
        for step in range(3, nz):
            line_pass(which, step)
        arrived(weight_sib[which])
        hidden_grad(1 - x, which)
        hidden_grad(x, which)
    gp_copy = send(gp.at[c, 1 - c], gp.at[c, 1 - c], sib)

    def norm2_part(xt, piece):
        at = pl.ds(pl.multiple_of(xt * quarter, quarter), quarter)
        return dot_nt(gp[c, 0, at], wf[0, piece]) + dot_nt(gp[c, 1, at], wf[1, piece])

    copies = spread_sum(1, norm2_part)
    line_add(proj_z, nz - 2)
    gp_copy.wait_recv()
    arrived(ns_sib)
    for s in range(2):
        for k in range(2):
            turn_rows(gp[s, c, k * quarter : (k + 1) * quarter], fch, (s * 2 + k) * quarter)
    copies = spread_pass(1, copies)
    weight_grad(fch, lambda at: ns[:, :, :, :, at].reshape(length, dz), gsf)
    fc_z = line_sum(gsf, grf, glf)

    def feed_part(xt, piece):
        at = pl.ds(pl.multiple_of(xt * quarter, quarter), quarter)
        return dot_nn(act[c, 0, at], wp[0, piece]) + dot_nn(act[c, 1, at], wp[1, piece])

    for turn in range(2):
        for side in range(2):
            spread_part(2, feed_part, turn, side)
    sv[...] = jnp.zeros_like(sv)
    late[...] = jnp.zeros_like(late)
    for s in range(2):
        sv[6:7, 0:fch] += jnp.sum(gp[s, c].astype(single), axis=0, keepdims=True)

    arrived(copies)
    my_dy = dyb.at[c, x, pl.ds(pl.multiple_of(y * block, block), block)]

    def middle_back(r):
        at = pl.ds(r, 32)
        grad_rows = my_dy[at].astype(single)
        by_value, gain_part, shift_part = norm_back(mid[at], summed(1, at), gain2)
        grad = grad_rows + by_value
        gmid[at] = grad
        low = grad.astype(half)
        gm[c, x, y, at] = low
        sv[3:4] += gain_part
        sv[4:5] += shift_part
        sv[0:1] += jnp.sum(low.astype(single), axis=0, keepdims=True)
        sv[5:6] += jnp.sum(grad_rows, axis=0, keepdims=True)

    copies = halves_of_block(32, middle_back, lambda: gather_first(gm))
    copies += gather_rest(gm)
    through = gather_pass(gm, copies)
    gm_sib = [copies[4]]
    for j in range(nz - 3, 0, -1):
        line_add(proj_z, j)

    def grad_attended(xt):
        at = pl.ds(pl.multiple_of(xt * quarter, quarter), quarter)
        rows_gm = gm[c, xt].reshape(quarter, width)
        total = None
        for piece in range(nz):
            part = dot_nt(rows_gm[:, piece * dz : (piece + 1) * dz], wo[piece])
            total = part if total is None else total + part
        for h in range(2):
            gtt[h, at] = total[:, h * ec : (h + 1) * ec].astype(half)

    copies[3].wait_recv()
    gm_sib.append(pass_block(gm, x, 1 - y))
    grad_attended(x)
    copies[2].wait_recv()
    gm_sib.append(pass_block(gm, 1 - x, y))
    arrived(through)
    gm_sib.append(pass_block(gm, 1 - x, 1 - y))
    grad_attended(1 - x)
    gt_copy = send(gtt.at[1 - c], gt.at[c], sib)
    gt[c] = gtt[c]
    arrived(gm_sib)
    for s in range(2):
        for k in range(2):
            turn_rows(ao[k, s], ec, (s * 2 + k) * quarter)
    weight_grad(ec, lambda at: gm[:, :, :, :, at].reshape(length, dz), gso)
    out_z = direct_sum(gso, gro)
    feed_copies = spread_first(2) + spread_second(2) + spread_third(2)
    line_add(fc_z, nz - 2)
    gt_copy.wait_recv()

    dkb[...] = jnp.zeros_like(dkb)
    dvb[...] = jnp.zeros_like(dvb)
    for i in range(n_blocks):
        j0 = max(0, i - 2)
        span = (i + 1 - j0) * quarter
        keys = pl.ds(j0 * quarter, span)
        grads = (wide, wide_b)
        ga = [
            only(gt[i % 2, (i // 2) * quarter : (i // 2 + 1) * quarter], h) for h in range(heads)
        ]
        for h in range(heads):
            grads[h][:, 0:span] = dot_nt(ga[h], vb[keys])

        def back(r, i=i, span=span):
            for h in range(heads):
                grad_p = grads[h][pl.ds(r, 64), 0:span]
                share = probs[i][h, pl.ds(r, 64)].astype(single)
                delta = jnp.sum(grad_p * share, axis=-1, keepdims=True)
                dsb[h, pl.ds(r, 64), 0:span] = (share * (grad_p - delta)).astype(half)

        by_rows(quarter, 64, back)
        total = None
        for h in range(heads):
            grad_s = dsb[h, :, 0:span]
            part = dot_nn(grad_s, only(kb[keys], h))
            total = part if total is None else total + part
            dkb[keys] += dot_nn(grad_s.T, only(qb[pl.ds(i * quarter, quarter)], h))
            dvb[keys] += dot_nn(probs[i][h].T, ga[h])
        dqkv[i // 2, i % 2, :, 0:ec] = (total * HD**-0.5).astype(half)
        if i == n_blocks - 2:
            feed_copies = spread_pass(2, feed_copies)
            line_end(proj_z)
            xp_[x] = accum[...].astype(half)
            proj_x = send(xp_.at[x], xp_.at[x], xnb)
    for i in range(n_blocks):
        at = pl.ds(i * quarter, quarter)
        dqkv[i // 2, i % 2, :, ec : 2 * ec] = (dkb[at] * HD**-0.5).astype(half)
        dqkv[i // 2, i % 2, :, 2 * ec :] = dvb[at].astype(half)

    my_dx = pl.ds(pl.multiple_of(c * 3 * ec, ec), 3 * ec)
    dx_copy = send(dqkv.at[:, 1 - c], dx.at[:, :, my_dx], sib)
    dx[:, :, my_dx] = dqkv[:, c]
    for i in range(n_blocks):
        turn_rows(dqkv[i // 2, i % 2], 3 * ec, i * quarter)
    weight_grad(3 * ec, lambda at: nf[:, :, :, at].reshape(length, dz), gsq)
    qkv_z = direct_sum(gsq, grq)
    for j in range(nz - 3, 0, -1):
        line_add(fc_z, j)
    arrived(weight_sib[0])
    dx_copy.wait_recv()

    def norm1_part(xt, piece):
        return dot_nt(dx[xt], wq[piece])

    copies = spread_sum(3, norm1_part)

    sv[7:8, 0:ec] = jnp.sum(
        dqkv[:, :, :, 0:ec].astype(single).reshape(length, ec), axis=0, keepdims=True
    )
    sv[7:8, ec : 2 * ec] = jnp.sum(
        dqkv[:, :, :, 2 * ec :].astype(single).reshape(length, ec), axis=0, keepdims=True
    )

    my_place = x * 4 + t
    svall[my_place] = sv[...]
    sv_copies = [send(sv, svall.at[my_place], dev) for dev in peers[0:7]]

    arrived(feed_copies)
    my_rows = pl.multiple_of(c * quarter + y * block, block)

    def out_rows(r):
        at = pl.ds(r, 32)
        value = mid[at] + (summed(2, at) + proj_bias)
        outv[pl.ds(pl.multiple_of(my_rows + r, 32), 32)] = value.astype(half)

    by_rows(block, 32, out_rows)
    copies = spread_pass(3, copies)
    mine = outv.at[pl.ds(my_rows, block)]
    theirs = outv.at[pl.ds(pl.multiple_of(c * quarter + (1 - y) * block, block), block)]
    out_y = send(mine, mine, ynb)
    out_s = [send(mine, mine, sib)]

    def plane_sum(copies, out, home):
        arrived(copies)
        value = out[z].astype(single)
        for step in range(1, nz):
            value = value + home[(z + step) % nz].astype(single)
        return value

    line_end(fc_z)
    xf[x] = accum[...].T.astype(half)
    fc_x = send(xf.at[x], xf.at[x], xnb)
    xo[x] = plane_sum(out_z, gso, gro).astype(half)
    out_x = send(xo.at[x], xo.at[x], xnb)
    proj_x.wait_recv()
    final = [fetch(xp_, gproj_hbm)]

    arrived(copies)

    def first_back(r):
        at = pl.ds(r, 32)
        by_value, gain_part, shift_part = norm_back(
            my_x[at].astype(single), summed(3, at), gain1
        )
        gradv[pl.ds(pl.multiple_of(my_rows + r, 32), 32)] = (gmid[at] + by_value).astype(half)
        late[0:1] += gain_part
        late[1:2] += shift_part

    def grad_rows_at(by, row):
        start = pl.multiple_of(c * quarter + by * block + row, block // 2)
        return gradv.at[pl.ds(start, block // 2)]

    def grad_send(row):
        rows = grad_rows_at(y, row)
        return [send(rows, rows, ynb), send(rows, rows, sib)]

    copies = halves_of_block(32, first_back, lambda: grad_send(0))
    lateall[my_place] = late[...]
    late_copies = [send(late, lateall.at[my_place], dev) for dev in peers[0:7]]
    copies += grad_send(block // 2)
    arrived(sv_copies)
    total = svall[0]
    for place in range(1, 8):
        total = total + svall[place]
    for piece in range(nz):
        s2[piece, 0:6] = total[0:6, piece * dz : (piece + 1) * dz]
        from_x = piece // pieces
        at = (piece % pieces) * dz
        s2[piece, 6:7] = svall[from_x * 4 + t, 6:7, at : at + dz]
        s2[piece, 7:8] = svall[from_x * 4 + t, 7:8, 0:dz]
    s2r[z] = s2[z]
    s2_copies = [
        send(s2.at[(z + step) % nz], s2r.at[z], zdev(step)) for step in range(1, nz)
    ]
    out_y.wait_recv()
    out_s.append(send(theirs, theirs, sib))
    arrived(late_copies)
    total = lateall[0]
    for place in range(1, 8):
        total = total + lateall[place]
    for piece in range(nz):
        l2[piece] = total[:, piece * dz : (piece + 1) * dz]
    l2r[z] = l2[z]
    l2_copies = [
        send(l2.at[(z + step) % nz], l2r.at[z], zdev(step)) for step in range(1, nz)
    ]
    xq[x] = plane_sum(qkv_z, gsq, grq).T.astype(half)
    qkv_x = send(xq.at[x], xq.at[x], xnb)
    grad_s_ = [copies[1], copies[3]]
    for k in range(2):
        copies[2 * k].wait_recv()
        rows = grad_rows_at(1 - y, k * (block // 2))
        grad_s_.append(send(rows, rows, sib))
    arrived(out_s)
    final.append(fetch(outv, out_hbm))
    arrived([fc_x])
    final.append(fetch(xf, gfc_hbm))
    arrived([out_x])
    final.append(fetch(xo, gout_hbm))
    arrived(grad_s_)
    final.append(fetch(gradv, grad_hbm))
    arrived(s2_copies)
    small = s2r[0]
    for piece in range(1, nz):
        small = small + s2r[piece]
    gvec_ref[0:7] = small[0:7]
    arrived(l2_copies)
    small_late = l2r[0]
    for piece in range(1, nz):
        small_late = small_late + l2r[piece]
    gvec_ref[1:3] = small_late[0:2]
    q_line, v_line = small[7:8, 0:ec], small[7:8, ec : 2 * ec]
    even = jnp.where(low_lane, q_line, pltpu.roll(v_line, HD, 1))
    odd = jnp.where(low_lane, pltpu.roll(q_line, HD, 1), v_line)
    gvec_ref[7:8, 0:ec] = jnp.where(z % pieces == 0, even, odd)
    gvec_ref[7:8, ec:dz] = jnp.zeros((1, dz - ec), single)
    arrived([qkv_x])
    final.append(fetch(xq, gqkv_hbm))
    for copy in final:
        copy.wait()
    for copy in started:
        copy.wait_send()


def finish_kernel(
    out,
    grad,
    gqkv,
    gout,
    gfc,
    gproj,
    gvec,
    out_ref,
    grad_ref,
    gqkv_ref,
    gout_ref,
    gfc_ref,
    gproj_ref,
    gqv_ref,
    *line_refs,
):
    single = jnp.float32
    out_ref[...] = out[...]
    grad_ref[...] = grad[...]
    ec = gqkv_ref.shape[2]
    for j in range(3):
        gqkv_ref[j] = gqkv[0, :, j * ec : (j + 1) * ec].astype(single)
    gout_ref[...] = gout[0].astype(single)
    gfc_ref[...] = gfc[0].astype(single)
    gproj_ref[...] = gproj[0].astype(single)
    pair = gqv_ref.shape[1]
    gqv_ref[0:1] = gvec[7:8, 0:pair]
    gqv_ref[1:2] = gvec[7:8, pair : 2 * pair]
    for row, ref in enumerate(line_refs):
        ref[...] = gvec[row : row + 1]


def plane_block(
    nz,
    block_input,
    segment_ids,
    cotangent,
    qkv_weight,
    qv_bias,
    out_weight,
    out_bias,
    norm1_gain,
    norm1_shift,
    fc_weight,
    fc_bias,
    proj_weight,
    proj_bias,
    norm2_gain,
    norm2_shift,
):
    half = jnp.bfloat16
    single = jnp.float32
    _, rows, width = block_input.shape
    length = segment_ids.shape[1]
    dz = qkv_weight.shape[0]
    ec = qkv_weight.shape[2] // 2
    fch = fc_weight.shape[1] // 2
    quarter, block = rows // 2, rows // 4
    vmem = pltpu.VMEM
    spans = [(i + 1 - max(0, i - 2)) * quarter for i in range(4)]
    heads = ec // HD
    scratch = [
        vmem((dz, 3 * ec), single),
        vmem((ec, dz), single),
        vmem((dz, fch), single),
        vmem((fch, dz), single),
        vmem((rows, width), half),
        vmem((2, quarter, width), half),
        vmem((2, 2, quarter, width), half),
        vmem((2, 2, quarter, width), half),
        vmem((nz, dz, 6 * ec), half),
        vmem((nz, 2 * ec, dz), half),
        vmem((2, nz, dz, fch), half),
        vmem((2, nz, fch, dz), half),
        vmem((2, nz, 8, dz), single),
        vmem((8, width), single),
        vmem((2, fch), single),
        vmem((length, ec), half),
        vmem((length, ec), half),
        vmem((length, ec), half),
    ]
    scratch += [vmem((heads, quarter, span), half) for span in spans]
    scratch += [
        vmem((length, 128), single),
        vmem((2, 2, quarter, ec), half),
        vmem((2, quarter, 2 * ec), half),
        vmem((4, 2, 2, 2, block, width // 2), half),
        vmem((4, 6, block, width // 2), half),
        vmem((4, 2, 2, block, width // 2), single),
        vmem((block, width), single),
        vmem((2, 2, 2, block, width), half),
        vmem((2, 2, 2, block, width), half),
        vmem((2, 2, rows, fch), half),
        vmem((2, 2, rows, fch), half),
        vmem((fch, length), half),
    ]
    for _ in range(2):
        scratch += [
            vmem((nz, 3 * ec, dz), half),
            vmem((nz, ec, dz), half),
            vmem((nz, fch, dz), half),
            vmem((nz, fch, dz), half),
        ]
    scratch += [
        vmem((nz, fch, dz), half),
        vmem((nz, fch, dz), half),
        vmem((fch, dz), single),
        vmem((2, dz, 3 * ec), half),
        vmem((2, ec, dz), half),
        vmem((2, dz, fch), half),
        vmem((2, fch, dz), half),
        vmem((2, rows, ec), half),
        vmem((2, rows, ec), half),
        vmem((length, ec), single),
        vmem((length, ec), single),
        vmem((2, 2, quarter, 3 * ec), half),
        vmem((2, quarter, 6 * ec), half),
        vmem((quarter, 3 * quarter), single),
        vmem((quarter, 3 * quarter), single),
        vmem((2, rows, fch), single),
        vmem((2, quarter, 3 * quarter), half),
        vmem((rows, width), half),
        vmem((rows, width), half),
        vmem((block, width), single),
        vmem((8, width), single),
        vmem((8, 8, width), single),
        vmem((8, width), single),
        vmem((8, 8, width), single),
        vmem((nz, 8, dz), single),
        vmem((nz, 8, dz), single),
        vmem((nz, 8, dz), single),
        vmem((nz, 8, dz), single),
        pltpu.SemaphoreType.DMA((210,)),
        pltpu.SemaphoreType.DMA((210,)),
        pltpu.SemaphoreType.DMA((20,)),
    ]
    whole = pl.BlockSpec(memory_space=pltpu.VMEM)
    there = pl.BlockSpec(memory_space=pl.ANY)
    middle = pl.pallas_call(
        functools.partial(block_kernel, nz),
        out_shape=(
            jax.ShapeDtypeStruct((rows, width), half),
            jax.ShapeDtypeStruct((rows, width), half),
            jax.ShapeDtypeStruct((2, dz, 3 * ec), half),
            jax.ShapeDtypeStruct((2, ec, dz), half),
            jax.ShapeDtypeStruct((2, dz, fch), half),
            jax.ShapeDtypeStruct((2, fch, dz), half),
            jax.ShapeDtypeStruct((8, dz), single),
        ),
        in_specs=[there] * 2 + [whole] + [there] * 4 + [whole] * 8,
        out_specs=(there,) * 6 + (whole,),
        scratch_shapes=scratch,
        compiler_params=pltpu.CompilerParams(
            collective_id=0, has_side_effects=True, vmem_limit_bytes=67043328
        ),
        name="residual_block",
    )(
        block_input.reshape(rows, width),
        cotangent.reshape(rows, width),
        segment_ids,
        qkv_weight.transpose(1, 0, 2),
        out_weight,
        fc_weight,
        proj_weight,
        out_bias.reshape(1, dz),
        norm1_gain.reshape(1, dz),
        norm1_shift.reshape(1, dz),
        norm2_gain.reshape(1, dz),
        norm2_shift.reshape(1, dz),
        proj_bias.reshape(1, dz),
        fc_bias.reshape(1, dz),
        qv_bias,
    )

    def halves(shape, axis):
        return pl.BlockSpec(
            shape, lambda side: tuple(side if k == axis else 0 for k in range(len(shape)))
        )

    line = pl.BlockSpec((1, dz), lambda side: (0, 0))
    outs = pl.pallas_call(
        finish_kernel,
        grid=(2,),
        out_shape=(
            jax.ShapeDtypeStruct((rows, width), half),
            jax.ShapeDtypeStruct((rows, width), half),
            jax.ShapeDtypeStruct((3, dz, 2 * ec), single),
            jax.ShapeDtypeStruct((2 * ec, dz), single),
            jax.ShapeDtypeStruct((dz, 2 * fch), single),
            jax.ShapeDtypeStruct((2 * fch, dz), single),
            jax.ShapeDtypeStruct(qv_bias.shape, single),
        )
        + (jax.ShapeDtypeStruct((1, dz), single),) * 7,
        in_specs=[
            halves((quarter, width), 0),
            halves((quarter, width), 0),
            halves((1, dz, 3 * ec), 0),
            halves((1, ec, dz), 0),
            halves((1, dz, fch), 0),
            halves((1, fch, dz), 0),
            pl.BlockSpec((8, dz), lambda side: (0, 0)),
        ],
        out_specs=(
            halves((quarter, width), 0),
            halves((quarter, width), 0),
            halves((3, dz, ec), 2),
            halves((ec, dz), 0),
            halves((dz, fch), 1),
            halves((fch, dz), 0),
            pl.BlockSpec(qv_bias.shape, lambda side: (0, 0)),
        )
        + (line,) * 7,
        name="finish",
    )(*middle)
    out, grad, gqkv, gout, gfc, gproj, gqv = outs[:7]
    gbout, ggain1, gshift1, ggain2, gshift2, gbproj, gbfc = [
        value.reshape(dz) for value in outs[7:]
    ]
    return (
        out.reshape(block_input.shape),
        grad.reshape(block_input.shape),
        gqkv.transpose(1, 0, 2),
        gqv,
        gout,
        gbout,
        ggain1,
        gshift1,
        gfc,
        gbfc,
        gproj,
        gbproj,
        ggain2,
        gshift2,
    )


def device_program(mesh):
    planes = mesh.shape["fsdp"]

    def program(block_input, *others):
        seqs_here, rows, width = block_input.shape
        one_kernel = (
            seqs_here == 1
            and mesh.shape["ctx"] == 2
            and mesh.shape["tp"] == 4
            and planes == 4
            and width // planes == 256
        )
        if one_kernel:
            return plane_block(planes, block_input, *others)
        return on_device(block_input, *others)

    return program


def solution(mesh):
    return jax.shard_map(
        device_program(mesh),
        mesh=mesh,
        in_specs=(
            P("fsdp", "ctx", None),
            P("fsdp", None),
            P("fsdp", "ctx", None),
            P("fsdp", None, "tp"),
            P(None, ("tp", "fsdp")),
            P("tp", "fsdp"),
            P("fsdp"),
            P("fsdp"),
            P("fsdp"),
            P("fsdp", "tp"),
            P(("tp", "fsdp")),
            P("tp", "fsdp"),
            P("fsdp"),
            P("fsdp"),
            P("fsdp"),
        ),
        out_specs=(
            P("fsdp", "ctx", None),
            P("fsdp", "ctx", None),
            P("fsdp", None, "tp"),
            P(None, ("tp", "fsdp")),
            P("tp", "fsdp"),
            P("fsdp"),
            P("fsdp"),
            P("fsdp"),
            P("fsdp", "tp"),
            P(("tp", "fsdp")),
            P("tp", "fsdp"),
            P("fsdp"),
            P("fsdp"),
            P("fsdp"),
        ),
        check_vma=False,
    )
```

```python
import functools

import jax
import jax.numpy as jnp
from jax import lax
from jax.experimental import pallas as pl
from jax.experimental.pallas import tpu as pltpu
from jax.sharding import PartitionSpec as P

HD = 64


epsilon = 1e-05


def layer_norm(values, gain, shift):
    centred = values - jnp.mean(values, axis=-1, keepdims=True)
    spread = jnp.mean(centred * centred, axis=-1, keepdims=True)
    return centred * lax.rsqrt(spread + epsilon) * gain + shift


def gelu_act(values):
    return jax.nn.gelu(values, approximate=True)


def on_device(
    block_input,
    segment_ids,
    cotangent,
    qkv_weight,
    qv_bias,
    out_weight,
    out_bias,
    norm1_gain,
    norm1_shift,
    fc_weight,
    fc_bias,
    proj_weight,
    proj_bias,
    norm2_gain,
    norm2_shift,
):
    half = jnp.bfloat16
    single = jnp.float32
    seqs_here, rows_seq, model_width = block_input.shape
    row_count = seqs_here * rows_seq
    shard_index = lax.axis_index("ctx")
    scale_factor = HD ** (-0.5)
    (
        wqkv_low,
        bqv_low,
        wout_low,
        bout_low,
        gain1_low,
        shift1_low,
        wfc_low,
        bfc_low,
        wproj_low,
        bproj_low,
        gain2_low,
        shift2_low,
    ) = (
        lax.all_gather(qkv_weight.astype(half), "fsdp", axis=0, tiled=True),
        lax.all_gather(qv_bias.astype(half), "fsdp", axis=1, tiled=True),
        lax.all_gather(out_weight.astype(half), "fsdp", axis=1, tiled=True),
        lax.all_gather(out_bias.astype(half), "fsdp", axis=0, tiled=True),
        lax.all_gather(norm1_gain.astype(half), "fsdp", axis=0, tiled=True),
        lax.all_gather(norm1_shift.astype(half), "fsdp", axis=0, tiled=True),
        lax.all_gather(fc_weight.astype(half), "fsdp", axis=0, tiled=True),
        lax.all_gather(fc_bias.astype(half), "fsdp", axis=0, tiled=True),
        lax.all_gather(proj_weight.astype(half), "fsdp", axis=1, tiled=True),
        lax.all_gather(proj_bias.astype(half), "fsdp", axis=0, tiled=True),
        lax.all_gather(norm2_gain.astype(half), "fsdp", axis=0, tiled=True),
        lax.all_gather(norm2_shift.astype(half), "fsdp", axis=0, tiled=True),
    )
    gain_first = gain1_low.astype(single)
    shift_first = shift1_low.astype(single)
    gain_second = gain2_low.astype(single)
    shift_second = shift2_low.astype(single)
    inputs = block_input.reshape(row_count, model_width).astype(single)
    normed_first = layer_norm(inputs, gain_first, shift_first).astype(half)
    projected = jnp.einsum("rd,dce->rce", normed_first, wqkv_low, preferred_element_type=single)
    bias_pair = bqv_low.astype(single)
    queries = (projected[:, 0] + bias_pair[0]).astype(half)
    key_rows = projected[:, 1].astype(half)
    value_rows = (projected[:, 2] + bias_pair[1]).astype(half)
    local_width = queries.shape[1]
    head_count = local_width // HD
    keys_all, values_all = (
        lax.all_gather(
            key_rows.reshape(seqs_here, rows_seq, local_width), "ctx", axis=1, tiled=True
        ),
        lax.all_gather(
            value_rows.reshape(seqs_here, rows_seq, local_width), "ctx", axis=1, tiled=True
        ),
    )
    length = keys_all.shape[1]
    query_pos = shard_index * rows_seq + jnp.arange(rows_seq)
    key_pos = jnp.arange(length)
    seg_query = lax.dynamic_slice_in_dim(segment_ids, shard_index * rows_seq, rows_seq, 1)
    query_heads = queries.reshape(seqs_here, rows_seq, head_count, HD)
    key_heads = keys_all.reshape(seqs_here, length, head_count, HD)
    value_heads = values_all.reshape(seqs_here, length, head_count, HD)

    def masked_scores(query_blk, key_blk, seg_row, seg_here):
        raw = (
            jnp.einsum("qhe,khe->hqk", query_blk, key_blk, preferred_element_type=single)
            * scale_factor
        )
        allowed = (key_pos[None, :] <= query_pos[:, None]) & (seg_here[:, None] == seg_row[None, :])
        return jnp.where(allowed[None], raw, -1e30)

    def attend(packed):
        query_blk, key_blk, value_blk, seg_row, seg_here = packed
        masked = masked_scores(query_blk, key_blk, seg_row, seg_here)
        row_max = jnp.max(masked, axis=-1, keepdims=True)
        expo = jnp.exp(masked - row_max)
        row_total = jnp.sum(expo, axis=-1, keepdims=True)
        probs_low = (expo / row_total).astype(half)
        attended = jnp.einsum("hqk,khe->qhe", probs_low, value_blk, preferred_element_type=single)
        return (attended.astype(half), row_max + jnp.log(row_total))

    attended, log_total = lax.map(
        attend, (query_heads, key_heads, value_heads, segment_ids, seg_query)
    )
    attended_rows = attended.reshape(row_count, local_width)
    attn_partial = jnp.dot(attended_rows, wout_low, preferred_element_type=single)
    attn_total = lax.psum(attn_partial.astype(jnp.bfloat16), "tp").astype(jnp.float32)
    middle = inputs + attn_total + bout_low.astype(single)
    normed_second = layer_norm(middle, gain_second, shift_second).astype(half)
    pre_act = jnp.dot(normed_second, wfc_low, preferred_element_type=single) + bfc_low.astype(
        single
    )
    act_low = gelu_act(pre_act).astype(half)
    mlp_total = lax.psum(
        jnp.dot(act_low, wproj_low, preferred_element_type=single).astype(jnp.bfloat16), "tp"
    ).astype(jnp.float32)
    out_rows = (middle + mlp_total + bproj_low.astype(single)).astype(half)
    wqkv_use, wout_use, wfc_use, wproj_use = (
        lax.all_gather(qkv_weight.astype(half), "fsdp", axis=0, tiled=True),
        lax.all_gather(out_weight.astype(half), "fsdp", axis=1, tiled=True),
        lax.all_gather(fc_weight.astype(half), "fsdp", axis=0, tiled=True),
        lax.all_gather(proj_weight.astype(half), "fsdp", axis=1, tiled=True),
    )
    grad_out = cotangent.reshape(row_count, model_width).astype(single)
    grad_out_low = cotangent.reshape(row_count, model_width)
    grad_bproj = jnp.sum(grad_out_low, axis=0, dtype=single)
    grad_wproj = jnp.einsum("rf,rd->fd", act_low, grad_out_low, preferred_element_type=single)
    grad_act = jnp.einsum("rd,fd->rf", grad_out_low, wproj_use, preferred_element_type=single)
    gelu_unused, gelu_pull = jax.vjp(gelu_act, pre_act)
    grad_pre = gelu_pull(grad_act)[0].astype(half)
    grad_bfc = jnp.sum(grad_pre, axis=0, dtype=single)
    grad_wfc = jnp.einsum("rd,rf->df", normed_second, grad_pre, preferred_element_type=single)
    norm2_partial = jnp.einsum("rf,df->rd", grad_pre, wfc_use, preferred_element_type=single)
    grad_norm2 = lax.psum(norm2_partial.astype(jnp.bfloat16), "tp").astype(jnp.float32)
    norm_unused, second_pull = jax.vjp(layer_norm, middle, gain_second, shift_second)
    grad_mid_ln, grad_gain2, grad_shift2 = second_pull(grad_norm2)
    grad_middle = grad_out + grad_mid_ln
    grad_mid_low = grad_middle.astype(half)
    grad_bout = jnp.sum(grad_mid_low, axis=0, dtype=single)
    grad_wout = jnp.einsum("rk,rd->kd", attended_rows, grad_mid_low, preferred_element_type=single)
    grad_att = jnp.einsum(
        "rd,kd->rk", grad_mid_low, wout_use, preferred_element_type=single
    ).astype(half)
    grad_att_heads = grad_att.reshape(seqs_here, rows_seq, head_count, HD)

    def attend_back(packed):
        query_blk, key_blk, value_blk, seg_row, seg_here, log_blk, grad_blk = packed
        masked = masked_scores(query_blk, key_blk, seg_row, seg_here)
        attn_probs = jnp.exp(masked - log_blk)
        probs_low = attn_probs.astype(half)
        grad_value = jnp.einsum("hqk,qhe->khe", probs_low, grad_blk, preferred_element_type=single)
        grad_probs = jnp.einsum("qhe,khe->hqk", grad_blk, value_blk, preferred_element_type=single)
        row_delta = jnp.sum(grad_probs * attn_probs, axis=-1, keepdims=True)
        grad_scores = (attn_probs * (grad_probs - row_delta)).astype(half)
        grad_query = (
            jnp.einsum("hqk,khe->qhe", grad_scores, key_blk, preferred_element_type=single)
            * scale_factor
        )
        grad_key = (
            jnp.einsum("hqk,qhe->khe", grad_scores, query_blk, preferred_element_type=single)
            * scale_factor
        )
        return (grad_query.astype(half), grad_key, grad_value)

    grad_query, grad_key, grad_value = lax.map(
        attend_back,
        (query_heads, key_heads, value_heads, segment_ids, seg_query, log_total, grad_att_heads),
    )
    grad_key, grad_value = (
        lax.psum_scatter(
            grad_key.reshape(seqs_here, length, local_width).astype(jnp.bfloat16),
            "ctx",
            scatter_dimension=1,
            tiled=True,
        ).astype(jnp.float32),
        lax.psum_scatter(
            grad_value.reshape(seqs_here, length, local_width).astype(jnp.bfloat16),
            "ctx",
            scatter_dimension=1,
            tiled=True,
        ).astype(jnp.float32),
    )
    grad_query = grad_query.reshape(row_count, local_width)
    grad_key = grad_key.reshape(row_count, local_width).astype(half)
    grad_value = grad_value.reshape(row_count, local_width).astype(half)
    grad_qkv = jnp.stack([grad_query, grad_key, grad_value], axis=1)
    grad_bqv = jnp.stack(
        [jnp.sum(grad_query, axis=0, dtype=single), jnp.sum(grad_value, axis=0, dtype=single)]
    )
    grad_wqkv = jnp.einsum("rd,rce->dce", normed_first, grad_qkv, preferred_element_type=single)
    norm1_partial = jnp.einsum("rce,dce->rd", grad_qkv, wqkv_use, preferred_element_type=single)
    grad_norm1 = lax.psum(norm1_partial.astype(jnp.bfloat16), "tp").astype(jnp.float32)
    first_unused, first_pull = jax.vjp(layer_norm, inputs, gain_first, shift_first)
    grad_in_ln, grad_gain1, grad_shift1 = first_pull(grad_norm1)
    input_rows = (grad_middle + grad_in_ln).astype(half)
    block_output = out_rows.reshape(block_input.shape)
    input_grad = input_rows.reshape(block_input.shape)
    (
        sum_wqkv,
        sum_bqv,
        sum_wout,
        sum_bout,
        sum_gain1,
        sum_shift1,
        sum_wfc,
        sum_bfc,
        sum_wproj,
        sum_bproj,
        sum_gain2,
        sum_shift2,
    ) = (
        lax.psum_scatter(grad_wqkv, ("fsdp", "ctx"), scatter_dimension=0, tiled=True),
        lax.psum_scatter(grad_bqv, ("fsdp", "ctx"), scatter_dimension=1, tiled=True),
        lax.psum_scatter(grad_wout, ("fsdp", "ctx"), scatter_dimension=1, tiled=True),
        lax.psum_scatter(grad_bout, ("fsdp", "ctx"), scatter_dimension=0, tiled=True),
        lax.psum_scatter(grad_gain1, ("fsdp", "ctx"), scatter_dimension=0, tiled=True),
        lax.psum_scatter(grad_shift1, ("fsdp", "ctx"), scatter_dimension=0, tiled=True),
        lax.psum_scatter(grad_wfc, ("fsdp", "ctx"), scatter_dimension=0, tiled=True),
        lax.psum_scatter(grad_bfc, ("fsdp", "ctx"), scatter_dimension=0, tiled=True),
        lax.psum_scatter(grad_wproj, ("fsdp", "ctx"), scatter_dimension=1, tiled=True),
        lax.psum_scatter(grad_bproj, ("fsdp", "ctx"), scatter_dimension=0, tiled=True),
        lax.psum_scatter(grad_gain2, ("fsdp", "ctx"), scatter_dimension=0, tiled=True),
        lax.psum_scatter(grad_shift2, ("fsdp", "ctx"), scatter_dimension=0, tiled=True),
    )
    (
        final_wqkv,
        final_bqv,
        final_wout,
        final_bout,
        final_gain1,
        final_shift1,
        final_wfc,
        final_bfc,
        final_wproj,
        final_bproj,
        final_gain2,
        final_shift2,
    ) = (
        lax.all_gather(sum_wqkv.astype(jnp.bfloat16), "ctx", axis=0, tiled=True).astype(
            sum_wqkv.dtype
        ),
        lax.all_gather(sum_bqv.astype(jnp.bfloat16), "ctx", axis=1, tiled=True).astype(
            sum_bqv.dtype
        ),
        lax.all_gather(sum_wout.astype(jnp.bfloat16), "ctx", axis=1, tiled=True).astype(
            sum_wout.dtype
        ),
        lax.all_gather(sum_bout.astype(jnp.bfloat16), "ctx", axis=0, tiled=True).astype(
            sum_bout.dtype
        ),
        lax.all_gather(sum_gain1.astype(jnp.bfloat16), "ctx", axis=0, tiled=True).astype(
            sum_gain1.dtype
        ),
        lax.all_gather(sum_shift1.astype(jnp.bfloat16), "ctx", axis=0, tiled=True).astype(
            sum_shift1.dtype
        ),
        lax.all_gather(sum_wfc.astype(jnp.bfloat16), "ctx", axis=0, tiled=True).astype(
            sum_wfc.dtype
        ),
        lax.all_gather(sum_bfc.astype(jnp.bfloat16), "ctx", axis=0, tiled=True).astype(
            sum_bfc.dtype
        ),
        lax.all_gather(sum_wproj.astype(jnp.bfloat16), "ctx", axis=1, tiled=True).astype(
            sum_wproj.dtype
        ),
        lax.all_gather(sum_bproj.astype(jnp.bfloat16), "ctx", axis=0, tiled=True).astype(
            sum_bproj.dtype
        ),
        lax.all_gather(sum_gain2.astype(jnp.bfloat16), "ctx", axis=0, tiled=True).astype(
            sum_gain2.dtype
        ),
        lax.all_gather(sum_shift2.astype(jnp.bfloat16), "ctx", axis=0, tiled=True).astype(
            sum_shift2.dtype
        ),
    )
    return (
        block_output,
        input_grad,
        final_wqkv,
        final_bqv,
        final_wout,
        final_bout,
        final_gain1,
        final_shift1,
        final_wfc,
        final_bfc,
        final_wproj,
        final_bproj,
        final_gain2,
        final_shift2,
    )


MESH = pl.DeviceIdType.MESH


def dot_nn(left, right):
    return lax.dot_general(
        left, right, (((1,), (0,)), ((), ())), preferred_element_type=jnp.float32
    )


def dot_nt(left, right):
    return lax.dot_general(
        left, right, (((1,), (1,)), ((), ())), preferred_element_type=jnp.float32
    )


def by_rows(rows, step, body):
    def one(index, carry):
        body(pl.multiple_of(index * step, step))
        return carry

    lax.fori_loop(0, rows // step, one, 0)


def norm_parts(values):
    centred = values - jnp.mean(values, axis=-1, keepdims=True)
    spread = jnp.mean(centred * centred, axis=-1, keepdims=True)
    return centred, lax.rsqrt(spread + epsilon)


def norm_back(values, incoming, gain):
    centred, rate = norm_parts(values)
    hat = centred * rate
    scaled = incoming * gain
    by_value = rate * (
        scaled
        - jnp.mean(scaled, axis=-1, keepdims=True)
        - hat * jnp.mean(scaled * hat, axis=-1, keepdims=True)
    )
    return (
        by_value,
        jnp.sum(incoming * hat, axis=0, keepdims=True),
        jnp.sum(incoming, axis=0, keepdims=True),
    )


class Partly:
    def __init__(self, copy, sends, receives):
        self.copy, self.sends, self.receives = copy, sends, receives

    def start(self):
        self.copy.start()

    def wait_recv(self):
        pl.when(self.receives)(self.copy.wait_recv)

    def wait_send(self):
        pl.when(self.sends)(self.copy.wait_send)


def block_kernel(
    nz,
    x_in,
    dy_in,
    seg_row,
    wqkv_in,
    wout_in,
    wfc_in,
    wproj_in,
    bout_in,
    gain1_in,
    shift1_in,
    gain2_in,
    shift2_in,
    bproj_in,
    bfc_in,
    bqv_in,
    out_hbm,
    grad_hbm,
    gqkv_hbm,
    gout_hbm,
    gfc_hbm,
    gproj_hbm,
    gvec_ref,
    stq,
    sto,
    stf,
    stp,
    xl,
    xr,
    dyb,
    nf,
    wq,
    wo,
    wf,
    wp,
    vec,
    full,
    fcb,
    qb,
    kb,
    vb,
    p0,
    p1,
    p2,
    p3,
    segc,
    ao,
    ax,
    srs,
    rrs,
    mid,
    ns,
    gm,
    act,
    gp,
    turned,
    gsq,
    gso,
    gsf,
    gsp,
    grq,
    gro,
    grf,
    grp,
    glq,
    glf,
    glp,
    accum,
    xq,
    xo,
    xf,
    xp_,
    gtt,
    gt,
    dkb,
    dvb,
    dqkv,
    dx,
    wide,
    wide_b,
    slope,
    dsb,
    outv,
    gradv,
    gmid,
    sv,
    svall,
    late,
    lateall,
    bqall,
    l2,
    l2r,
    s2,
    s2r,
    send_sem,
    recv_sem,
    local_sem,
):
    half = jnp.bfloat16
    single = jnp.float32
    z = lax.axis_index("fsdp")
    x = lax.axis_index("ctx")
    t = lax.axis_index("tp")
    y = t // 2
    c = t % 2
    quarter = xl.shape[0] // 2
    block = quarter // 2
    width = xl.shape[1]
    dz = width // nz
    fch = wf.shape[3]
    ec = qb.shape[1]
    length = qb.shape[0]
    probs = (p0, p1, p2, p3)
    sib = (z, x, y * 2 + 1 - c)
    ynb = (z, x, (1 - y) * 2 + c)
    xnb = (z, 1 - x, t)
    dia = (z, 1 - x, (1 - y) * 2 + c)
    started = []

    def send(src, dst, dev):
        slot = len(started)
        copy = pltpu.make_async_remote_copy(
            src_ref=src,
            dst_ref=dst,
            send_sem=send_sem.at[slot],
            recv_sem=recv_sem.at[slot],
            device_id=dev,
            device_id_type=MESH,
        )
        copy.start()
        started.append(copy)
        return copy

    def arrived(copies):
        for copy in copies:
            copy.wait_recv()

    def send_if(src, dst, dev, sends, receives, start=True):
        slot = len(started)
        copy = pltpu.make_async_remote_copy(
            src_ref=src,
            dst_ref=dst,
            send_sem=send_sem.at[slot],
            recv_sem=recv_sem.at[slot],
            device_id=dev,
            device_id_type=MESH,
        )
        some = Partly(copy, sends, receives)
        if start:
            pl.when(sends)(copy.start)
        started.append(some)
        return some

    fetched = []

    def fetch(src, dst):
        copy = pltpu.make_async_copy(src, dst, local_sem.at[len(fetched)])
        copy.start()
        fetched.append(copy)
        return copy

    def zdev(step):
        return ((z + step) % nz, x, t)

    right, left = zdev(1), zdev(nz - 1)

    peers = [(z, px, pt) for px in (x, 1 - x) for pt in (t, sib[2], ynb[2], (1 - y) * 2 + 1 - c)][
        1:
    ]
    for step in range(1, nz):
        peers += [((z + step) % nz, x, t), ((z + step) % nz, x, sib[2])]
    barrier = pltpu.get_barrier_semaphore()
    for dev in peers:
        pl.semaphore_signal(barrier, inc=1, device_id=dev, device_id_type=MESH)

    my_e = pl.ds(pl.multiple_of(x * ec, ec), ec)
    my_f = pl.ds(pl.multiple_of(x * fch, fch), fch)
    stage_q = [
        fetch(wqkv_in.at[j, :, my_e], stq.at[:, j * ec : (j + 1) * ec]) for j in range(3)
    ]
    stage_x = fetch(x_in, xl)
    stage_o = fetch(wout_in.at[my_e], sto)
    stage_f = fetch(wfc_in.at[:, my_f], stf)
    stage_p = fetch(wproj_in.at[my_f], stp)
    stage_dy = [
        fetch(dy_in.at[pl.ds(s * quarter, quarter)], dyb.at[s, x]) for s in range(2)
    ]

    def weight_at(which, h, plane):
        if which == 0:
            return wq.at[plane, :, pl.ds(pl.multiple_of(h * 3 * ec, ec), 3 * ec)]
        if which == 1:
            return wo.at[plane, pl.ds(pl.multiple_of(h * ec, ec), ec)]
        if which == 2:
            return wf.at[h, plane]
        part = fch // 2
        return wp.at[h, plane, (which - 3) * part : (which - 2) * part]

    def rounded(src, dst, rows):
        def some(r):
            dst[pl.ds(r, 64)] = src[pl.ds(r, 64)].astype(half)

        by_rows(rows, 64, some)

    lines = [[], [], [], [], []]
    weight_sib = [[], [], [], [], []]

    def line_start(which):
        mine = weight_at(which, c, z)
        lines[which].append(
            (
                send_if(mine, mine, right, z < nz - 1, z >= 1),
                send_if(mine, mine, left, z >= 1, z < nz - 1),
            )
        )

    def line_pass(which, step):
        from_left, from_right = lines[which][step - 1]
        lower = weight_at(which, c, (z + nz - step) % nz)
        upper = weight_at(which, c, (z + step) % nz)
        from_left.wait_recv()
        if step < nz - 1:
            to_right = send_if(
                lower, lower, right, (z >= step) & (z < nz - 1), z >= step + 1
            )
        weight_sib[which].append(send_if(lower, lower, sib, z >= step, z >= step))
        from_right.wait_recv()
        if step < nz - 1:
            to_left = send_if(
                upper, upper, left, (z + step < nz) & (z >= 1), z + step + 1 < nz
            )
            lines[which].append((to_right, to_left))
        weight_sib[which].append(send_if(upper, upper, sib, z + step < nz, z + step < nz))

    def to_sibling(which):
        mine = weight_at(which, c, z)
        weight_sib[which].append(send(mine, mine, sib))

    for copy in stage_q:
        copy.wait()
    rounded(stq, weight_at(0, c, z), dz)
    for row, line in enumerate(
        (bout_in, gain1_in, shift1_in, gain2_in, shift2_in, bproj_in, bfc_in)
    ):
        vec[c, z, row : row + 1] = line[...].astype(half).astype(single)
    pair = bqv_in.shape[1]
    vec[c, z, 7:8, 0:pair] = bqv_in[0:1].astype(half).astype(single)
    vec[c, z, 7:8, pair : 2 * pair] = bqv_in[1:2].astype(half).astype(single)
    vec[c, z, 7:8, 2 * pair :] = jnp.zeros((1, dz - 2 * pair), single)
    pl.semaphore_wait(barrier, len(peers))

    line_start(0)
    stage_x.wait()
    x_copy = send(xl.at[pl.ds(pl.multiple_of(c * quarter, quarter), quarter)], xr.at[c], xnb)
    vec_copies = [send(vec.at[c, z], vec.at[c, z], sib)]
    for step in range(1, nz):
        for dev_t in (t, sib[2]):
            vec_copies.append(send(vec.at[c, z], vec.at[c, z], ((z + step) % nz, x, dev_t)))
    stage_o.wait()
    rounded(sto, weight_at(1, c, z), ec)
    line_start(1)
    to_sibling(0)
    to_sibling(1)
    for copy in stage_dy:
        copy.wait()
    stage_f.wait()
    rounded(stf, weight_at(2, c, z), dz)
    stage_p.wait()
    rounded(stp, wp.at[c, z], fch)

    arrived(vec_copies)
    for piece in range(nz):
        full[:, piece * dz : (piece + 1) * dz] = vec[c, piece]
    pieces = nz // 2
    for h in range(2):
        for k in range(pieces):
            fcb[h : h + 1, k * dz : (k + 1) * dz] = vec[h, x * pieces + k][6:7]
    lane = lax.broadcasted_iota(jnp.int32, (1, ec), 1)
    low_lane = lane < HD
    first_piece = vec[c, x * pieces][7:8, 0:ec]
    next_piece = vec[c, x * pieces + 1][7:8, 0:ec]
    q_bias = jnp.where(low_lane, first_piece, pltpu.roll(next_piece, HD, 1))
    v_bias = jnp.where(low_lane, pltpu.roll(first_piece, HD, 1), next_piece)
    out_bias = full[0:1]
    gain1, shift1 = full[1:2], full[2:3]
    gain2, shift2 = full[3:4], full[4:5]
    proj_bias = full[5:6]

    def first_norm(src, dst):
        def rows(r):
            centred, rate = norm_parts(src[pl.ds(r, 64)].astype(single))
            dst[pl.ds(r, 64)] = (centred * rate * gain1 + shift1).astype(half)

        by_rows(quarter, 64, rows)

    for s in range(2):
        first_norm(xl.at[pl.ds(s * quarter, quarter)], nf.at[x, s])
    line_pass(0, 1)
    line_pass(1, 1)
    x_copy.wait_recv()
    x_fwd = send(xr.at[c], xr.at[c], sib)
    dy_copy = send(dyb.at[c, x], dyb.at[c, x], xnb)
    first_norm(xr.at[c], nf.at[1 - x, c])
    line_pass(0, 2)
    line_pass(1, 2)
    line_start(2)
    line_start(3)
    to_sibling(2)
    to_sibling(3)
    to_sibling(4)
    x_fwd.wait_recv()
    first_norm(xr.at[1 - c], nf.at[1 - x, 1 - c])
    for i in range(length // quarter):
        line = seg_row[:, i * quarter : (i + 1) * quarter].astype(single)
        segc[i * quarter : (i + 1) * quarter] = jnp.broadcast_to(line, (128, quarter)).T
    for step in range(3, nz):
        line_pass(0, step)
        line_pass(1, step)

    my_qkv = pl.ds(pl.multiple_of(c * 3 * ec, ec), 3 * ec)
    for xi in range(2):
        for ci in range(2):
            proj = dot_nn(nf[xi, ci], wq[:, :, my_qkv].reshape(width, 3 * ec))
            at = pl.ds((xi * 2 + ci) * quarter, quarter)
            qb[at] = (proj[:, 0:ec] + q_bias).astype(half)
            kb[at] = proj[:, ec : 2 * ec].astype(half)
            vb[at] = (proj[:, 2 * ec :] + v_bias).astype(half)

    head_lane = lax.broadcasted_iota(jnp.int32, (1, ec), 1) // HD
    n_blocks = length // quarter
    heads = ec // HD

    def only(values, h):
        return jnp.where(head_lane == h, values, jnp.zeros_like(values))

    for i in range(n_blocks):
        j0 = max(0, i - 2)
        span = (i + 1 - j0) * quarter
        keys = pl.ds(j0 * quarter, span)
        scores = (wide, wide_b)
        for h in range(heads):
            q_h = only(qb[pl.ds(i * quarter, quarter)], h) * jnp.asarray(HD**-0.5, half)
            scores[h][:, 0:span] = dot_nt(q_h, kb[keys])

        def soft(r, i=i, j0=j0, span=span):
            q_at = i * quarter + r + lax.broadcasted_iota(jnp.int32, (64, span), 0)
            k_at = j0 * quarter + lax.broadcasted_iota(jnp.int32, (64, span), 1)
            seg_q = segc[pl.ds(pl.multiple_of(i * quarter + r, 64), 64)]
            seg_k = seg_row[:, j0 * quarter : j0 * quarter + span].astype(single)
            same = jnp.concatenate([seg_q] * (span // 128), axis=1) == seg_k
            allowed = (k_at <= q_at) & same
            for h in range(heads):
                masked = jnp.where(allowed, scores[h][pl.ds(r, 64), 0:span], -1e30)
                expo = jnp.exp(masked - jnp.max(masked, axis=-1, keepdims=True))
                share = expo * (1.0 / jnp.sum(expo, axis=-1, keepdims=True))
                probs[i][h, pl.ds(r, 64)] = share.astype(half)

        by_rows(quarter, 64, soft)
        total = None
        for h in range(heads):
            part = dot_nn(probs[i][h], only(vb[keys], h))
            total = part if total is None else total + part
        ao[i // 2, i % 2] = total.astype(half)

    my_ax = pl.ds(pl.multiple_of(c * ec, ec), ec)
    att_copy = send(ao.at[:, 1 - c], ax.at[:, :, my_ax], sib)
    ax[:, :, my_ax] = ao[:, c]
    arrived(weight_sib[1])
    att_copy.wait_recv()

    group = block // 2

    def rows_of(ref, g):
        return jnp.concatenate(
            [ref[b * block + g * group : b * block + (g + 1) * group] for b in range(4)], axis=0
        )

    def rows_of_pair(ref, g):
        return jnp.concatenate(
            [
                ref[b // 2, (b % 2) * block + g * group : (b % 2) * block + (g + 1) * group]
                for b in range(4)
            ],
            axis=0,
        )

    def spread_part(k, g, part, side):
        for p in range(nz // 2):
            value = part(g, side * (nz // 2) + p).astype(half)
            for b in range(4):
                srs[k, g, b // 2, b % 2, side, :, p * dz : (p + 1) * dz] = value[
                    b * group : (b + 1) * group
                ]

    def spread_send(k, g, side):
        if side:
            return [
                send(srs.at[k, g, 1 - x, 1 - y, 1], rrs.at[k, g, 1], ynb),
                send(srs.at[k, g, x, 1 - y, 1], rrs.at[k, g, 5], ynb),
            ]
        return [
            send(srs.at[k, g, 1 - x, 1 - y, 0], rrs.at[k, g, 0], xnb),
            send(srs.at[k, g, 1 - x, y, 0], rrs.at[k, g, 2], xnb),
        ]

    def spread_pass(k, g, copies):
        copies[0].wait_recv()
        srs[k, g, x, 1 - y, 0] = (
            srs[k, g, x, 1 - y, 0].astype(single) + rrs[k, g, 0].astype(single)
        ).astype(half)
        last = [send(srs.at[k, g, x, 1 - y, 0], rrs.at[k, g, 4], ynb)]
        copies[2].wait_recv()
        srs[k, g, 1 - x, y, 1] = (
            srs[k, g, 1 - x, y, 1].astype(single) + rrs[k, g, 1].astype(single)
        ).astype(half)
        last.append(send(srs.at[k, g, 1 - x, y, 1], rrs.at[k, g, 3], xnb))
        return [copies[1], copies[3]] + last

    def spread_sum(k, g, part):
        copies = []
        for side in range(2):
            spread_part(k, g, part, side)
            copies += spread_send(k, g, side)
        return copies

    def summed(k, g, at):
        sides = [
            srs[k, g, x, y, side, at].astype(single)
            + rrs[k, g, 2 + side, at].astype(single)
            + rrs[k, g, 4 + side, at].astype(single)
            for side in range(2)
        ]
        return jnp.concatenate(sides, axis=1)

    def attention_out(g, piece):
        return dot_nn(rows_of_pair(ax, g), wo[piece])

    copies = [spread_sum(0, g, attention_out) for g in range(2)]
    line_pass(2, 1)
    line_start(4)
    copies = [spread_pass(0, g, copies[g]) for g in range(2)]
    dy_copy.wait_recv()
    dy_fwd = send(dyb.at[c, 1 - x], dyb.at[c, 1 - x], sib)
    line_pass(3, 1)

    my_x = xl.at[pl.ds(pl.multiple_of(c * quarter + y * block, block), block)]

    def middle_rows(g):
        def rows(r):
            at = pl.ds(pl.multiple_of(g * group + r, 32), 32)
            value = my_x[at].astype(single) + (summed(0, g, pl.ds(r, 32)) + out_bias)
            mid[at] = value
            centred, rate = norm_parts(value)
            ns[c, x, y, at] = (centred * rate * gain2 + shift2).astype(half)

        by_rows(group, 32, rows)

    def gather_rows(g, part):
        return pl.ds(g * group + part * (group // 2), group // 2)

    def gather(buf, g):
        mine = buf.at[c, x, y]
        first, last = mine.at[gather_rows(g, 0)], mine.at[gather_rows(g, 1)]
        all_rows = mine.at[pl.ds(g * group, group)]
        return [
            send(first, first, xnb),
            send(last, last, ynb),
            send(last, last, xnb),
            send(first, first, ynb),
            send(all_rows, all_rows, sib),
        ]

    def gather_pass(buf, g, copies):
        by_x = buf.at[c, 1 - x, y, gather_rows(g, 0)]
        by_y = buf.at[c, x, 1 - y, gather_rows(g, 1)]
        copies[0].wait_recv()
        through = [send(by_x, by_x, ynb)]
        copies[1].wait_recv()
        through.append(send(by_y, by_y, xnb))
        return through

    def gather_end(buf, g, copies, through):
        def on(bx, by):
            rows = buf.at[c, bx, by, pl.ds(g * group, group)]
            return send(rows, rows, sib)

        copies[3].wait_recv()
        to_sib = [copies[4], on(x, 1 - y)]
        copies[2].wait_recv()
        to_sib.append(on(1 - x, y))
        arrived(through)
        to_sib.append(on(1 - x, 1 - y))
        return to_sib

    ns_copies = []
    for g in range(2):
        arrived(copies[g])
        middle_rows(g)
        ns_copies.append(gather(ns, g))
    line_pass(2, 2)
    through = [gather_pass(ns, g, ns_copies[g]) for g in range(2)]
    line_pass(4, 1)
    ns_sib = gather_end(ns, 0, ns_copies[0], through[0])
    for step in range(3, nz):
        line_pass(2, step)
    arrived(weight_sib[2])

    def hidden(g):
        rows_ns = ns[c, :, :, g * group : (g + 1) * group].reshape(quarter, width)
        for h in range(2):
            wide[:, 0:fch] = dot_nn(rows_ns, wf[h].reshape(width, fch))

            def rows(r, h=h):
                value = wide[pl.ds(r, group), 0:fch] + fcb[h : h + 1]
                root = 0.7978845608028654
                square = value * value
                inner = jnp.tanh(root * (value + 0.044715 * (square * value)))
                lift = 0.5 * (1.0 + inner)
                at = pl.ds(pl.multiple_of(2 * r + g * group, group), group)
                act[c, h, at] = (value * lift).astype(half)
                slope[h, at] = lift + 0.5 * value * (1.0 - inner * inner) * (
                    root * (1.0 + 3.0 * 0.044715 * square)
                )

            by_rows(quarter, group, rows)

    def hidden_grad(g, which):
        part_at = slice((which - 3) * (fch // 2), (which - 2) * (fch // 2))
        rows_dy = rows_of_pair(dyb.at[c], g)
        for h in range(2):
            grad = None
            for piece in range(nz):
                part = dot_nt(
                    rows_dy[:, piece * dz : (piece + 1) * dz],
                    wp[h, piece, part_at],
                )
                grad = part if grad is None else grad + part
            for b in range(4):
                at = slice(b * block + g * group, b * block + (g + 1) * group)
                gp[c, h, at, part_at] = (
                    grad[b * group : (b + 1) * group] * slope[h, at, part_at]
                ).astype(half)

    hidden(0)
    line_pass(3, 2)
    ns_sib += gather_end(ns, 1, ns_copies[1], through[1])
    hidden(1)
    act_copy = send(act.at[c, 1 - c], act.at[c, 1 - c], sib)
    line_pass(4, 2)

    def weight_grad(left, right_at, out):
        def one(step, carry):
            piece = (z + step) % nz
            at = pl.ds(pl.multiple_of(piece * dz, dz), dz)
            out[piece] = dot_nn(turned[0:left], right_at(at)).astype(half)
            return carry

        lax.fori_loop(0, nz, one, 0)

    def direct_sum(out, home):
        return [
            send(out.at[(z + step) % nz], home.at[z], zdev(step)) for step in range(1, nz)
        ]

    def line_sum(out, home, merged):
        up2, down2 = out.at[(z + 2) % nz], out.at[(z + nz - 2) % nz]
        up1, down1 = out.at[(z + 1) % nz], out.at[(z + nz - 1) % nz]
        far_up = send_if(out.at[nz - 1], merged, right, z == 0, z == 1)
        far_down = send_if(out.at[0], merged, left, z == nz - 1, z == nz - 2)
        two_up = send_if(up2, home.at[z], zdev(2), z + 2 < nz, z >= 2, start=False)
        two_down = send_if(down2, home.at[z], zdev(nz - 2), z >= 2, z + 2 < nz, start=False)
        pl.when(z == 0)(two_up.start)
        pl.when(z == nz - 1)(two_down.start)
        one_up = send_if(up1, home.at[z], right, z < nz - 1, z >= 1)
        one_down = send_if(down1, home.at[z], left, z >= 1, z < nz - 1)
        return out, home, merged, far_up, far_down, two_up, two_down, one_up, one_down

    def line_add(line):
        out, home, merged, far_up, far_down, two_up, two_down, _, _ = line

        @pl.when(z == 1)
        def _():
            far_up.copy.wait_recv()
            out[nz - 1] = (out[nz - 1].astype(single) + merged[...].astype(single)).astype(half)
            two_up.start()

        @pl.when(z == nz - 2)
        def _():
            far_down.copy.wait_recv()
            out[0] = (out[0].astype(single) + merged[...].astype(single)).astype(half)
            two_down.start()

    def line_end(line):
        out, home, _, _, _, two_up, two_down, one_up, one_down = line
        total = accum.at[0 : out.shape[1]]
        total[...] = out[z].astype(single)
        for copy, source, there in (
            (one_up, z - 1, z >= 1),
            (one_down, z + 1, z < nz - 1),
            (two_up, z - 2, z >= 2),
            (two_down, z + 2, z + 2 < nz),
        ):

            def take(copy=copy, source=source):
                copy.copy.wait_recv()
                total[...] += home[(source + nz) % nz].astype(single)

            pl.when(there)(take)
        return total[...]

    def turn_rows(src, left, column):
        turned[0:left, pl.ds(pl.multiple_of(column, quarter), quarter)] = src.T

    dy_fwd.wait_recv()
    act_copy.wait_recv()
    for s in range(2):
        for k in range(2):
            turn_rows(act[s, c, k * quarter : (k + 1) * quarter], fch, (s * 2 + k) * quarter)
    weight_grad(fch, lambda at: dyb[:, :, :, at].reshape(length, dz), gsp)
    proj_z = line_sum(gsp, grp, glp)
    for step in range(3, nz):
        line_pass(3, step)
    arrived(weight_sib[3])
    hidden_grad(0, 3)
    hidden_grad(1, 3)
    for step in range(3, nz):
        line_pass(4, step)
    arrived(weight_sib[4])

    def norm2_part(g, piece):
        return dot_nt(rows_of(gp.at[c, 0], g), wf[0, piece]) + dot_nt(
            rows_of(gp.at[c, 1], g), wf[1, piece]
        )

    hidden_grad(0, 4)
    copies = [spread_sum(1, 0, norm2_part)]
    hidden_grad(1, 4)
    gp_copy = send(gp.at[c, 1 - c], gp.at[c, 1 - c], sib)
    copies.append(spread_sum(1, 1, norm2_part))
    copies[0] = spread_pass(1, 0, copies[0])
    line_add(proj_z)
    copies[1] = spread_pass(1, 1, copies[1])
    gp_copy.wait_recv()
    arrived(ns_sib)
    for s in range(2):
        for k in range(2):
            turn_rows(gp[s, c, k * quarter : (k + 1) * quarter], fch, (s * 2 + k) * quarter)
    weight_grad(fch, lambda at: ns[:, :, :, :, at].reshape(length, dz), gsf)
    fc_z = line_sum(gsf, grf, glf)

    sv[...] = jnp.zeros_like(sv)
    late[...] = jnp.zeros_like(late)
    my_dy = dyb.at[c, x, pl.ds(pl.multiple_of(y * block, block), block)]

    def middle_back(g):
        def rows(r):
            at = pl.ds(pl.multiple_of(g * group + r, 32), 32)
            grad_rows = my_dy[at].astype(single)
            by_value, gain_part, shift_part = norm_back(
                mid[at], summed(1, g, pl.ds(r, 32)), gain2
            )
            grad = grad_rows + by_value
            gmid[at] = grad
            low = grad.astype(half)
            gm[c, x, y, at] = low
            sv[3:4] += gain_part
            sv[4:5] += shift_part
            sv[0:1] += jnp.sum(low.astype(single), axis=0, keepdims=True)
            sv[5:6] += jnp.sum(grad_rows, axis=0, keepdims=True)

        by_rows(group, 32, rows)

    gm_copies = []
    for g in range(2):
        arrived(copies[g])
        middle_back(g)
        gm_copies.append(gather(gm, g))

    def feed_part(g, piece):
        return dot_nn(rows_of(act.at[c, 0], g), wp[0, piece]) + dot_nn(
            rows_of(act.at[c, 1], g), wp[1, piece]
        )

    for side in range(2):
        spread_part(2, 0, feed_part, side)
    through = [gather_pass(gm, g, gm_copies[g]) for g in range(2)]
    for side in range(2):
        spread_part(2, 1, feed_part, side)
    for s in range(2):
        sv[6:7, 0:fch] += jnp.sum(gp[s, c].astype(single), axis=0, keepdims=True)

    def grad_attended(g):
        rows_gm = gm[c, :, :, g * group : (g + 1) * group].reshape(quarter, width)
        total = None
        for piece in range(nz):
            part = dot_nt(rows_gm[:, piece * dz : (piece + 1) * dz], wo[piece])
            total = part if total is None else total + part
        for h in range(2):
            for b in range(4):
                gtt[h, b, g] = total[b * group : (b + 1) * group, h * ec : (h + 1) * ec].astype(
                    half
                )
        gt[c, :, g] = gtt[c, :, g]
        return send(gtt.at[1 - c, :, g], gt.at[c, :, g], sib)

    gm_sib, gt_copies = [], []
    for g in range(2):
        gm_sib += gather_end(gm, g, gm_copies[g], through[g])
        gt_copies.append(grad_attended(g))
    line_add(fc_z)
    feed_copies = [spread_send(2, g, 0) + spread_send(2, g, 1) for g in range(2)]
    my_place = x * 4 + t
    svall[my_place] = sv[...]
    sv_copies = [send(sv, svall.at[my_place], dev) for dev in peers[0:7]]
    arrived(gm_sib)
    for s in range(2):
        for k in range(2):
            turn_rows(ao[k, s], ec, (s * 2 + k) * quarter)
    weight_grad(ec, lambda at: gm[:, :, :, :, at].reshape(length, dz), gso)
    out_z = direct_sum(gso, gro)
    arrived(gt_copies)

    dkb[...] = jnp.zeros_like(dkb)
    dvb[...] = jnp.zeros_like(dvb)
    for i in range(n_blocks):
        j0 = max(0, i - 2)
        span = (i + 1 - j0) * quarter
        keys = pl.ds(j0 * quarter, span)
        grads = (wide, wide_b)
        rows_gt = gt[i % 2, (i // 2) * 2 : (i // 2) * 2 + 2].reshape(quarter, ec)
        ga = [only(rows_gt, h) for h in range(heads)]
        for h in range(heads):
            grads[h][:, 0:span] = dot_nt(ga[h], vb[keys])

        def back(r, i=i, span=span):
            for h in range(heads):
                grad_p = grads[h][pl.ds(r, 64), 0:span]
                share = probs[i][h, pl.ds(r, 64)].astype(single)
                delta = jnp.sum(grad_p * share, axis=-1, keepdims=True)
                dsb[h, pl.ds(r, 64), 0:span] = (share * (grad_p - delta)).astype(half)

        by_rows(quarter, 64, back)
        total = None
        for h in range(heads):
            grad_s = dsb[h, :, 0:span]
            part = dot_nn(grad_s, only(kb[keys], h))
            total = part if total is None else total + part
            dkb[keys] += dot_nn(grad_s.T, only(qb[pl.ds(i * quarter, quarter)], h))
            dvb[keys] += dot_nn(probs[i][h].T, ga[h])
        dqkv[i // 2, i % 2, :, 0:ec] = (total * HD**-0.5).astype(half)
        if i == n_blocks - 2:
            feed_copies = [spread_pass(2, g, feed_copies[g]) for g in range(2)]
            xp_[x] = line_end(proj_z).astype(half)
            proj_x = send(xp_.at[x], xp_.at[x], xnb)
    for i in range(n_blocks):
        at = pl.ds(i * quarter, quarter)
        dqkv[i // 2, i % 2, :, ec : 2 * ec] = (dkb[at] * HD**-0.5).astype(half)
        dqkv[i // 2, i % 2, :, 2 * ec :] = dvb[at].astype(half)

    my_dx = pl.ds(pl.multiple_of(c * 3 * ec, ec), 3 * ec)
    dx_copy = send(dqkv.at[:, 1 - c], dx.at[:, :, my_dx], sib)
    dx[:, :, my_dx] = dqkv[:, c]
    for i in range(n_blocks):
        turn_rows(dqkv[i // 2, i % 2], 3 * ec, i * quarter)
    weight_grad(3 * ec, lambda at: nf[:, :, :, at].reshape(length, dz), gsq)
    qkv_z = line_sum(gsq, grq, glq)
    arrived(weight_sib[0])
    dx_copy.wait_recv()

    def norm1_part(g, piece):
        return dot_nt(rows_of_pair(dx, g), wq[piece])

    copies = [spread_sum(3, g, norm1_part) for g in range(2)]
    line_add(qkv_z)
    copies[0] = spread_pass(3, 0, copies[0])
    copies[1] = spread_pass(3, 1, copies[1])

    for g in range(2):
        arrived(feed_copies[g])
    my_rows = pl.multiple_of(c * quarter + y * block, block)

    def out_rows(g):
        def rows(r):
            at = pl.ds(pl.multiple_of(g * group + r, 32), 32)
            value = mid[at] + (summed(2, g, pl.ds(r, 32)) + proj_bias)
            outv[pl.ds(pl.multiple_of(my_rows + g * group + r, 32), 32)] = value.astype(half)

        by_rows(group, 32, rows)

    out_rows(0)
    out_rows(1)
    mine = outv.at[pl.ds(my_rows, block)]
    theirs = outv.at[pl.ds(pl.multiple_of(c * quarter + (1 - y) * block, block), block)]
    out_y = send(mine, mine, ynb)
    out_s = [send(mine, mine, sib)]

    for k, first in enumerate((0, 2 * ec)):
        bqall[x, :, k * ec : (k + 1) * ec] = jnp.sum(
            dqkv[:, :, :, first : first + ec].astype(single).reshape(length, ec),
            axis=0,
            keepdims=True,
        )
    bq_copy = send(bqall.at[x], bqall.at[x], xnb)

    def first_back(g):
        def rows(r):
            at = pl.ds(pl.multiple_of(g * group + r, 32), 32)
            by_value, gain_part, shift_part = norm_back(
                my_x[at].astype(single), summed(3, g, pl.ds(r, 32)), gain1
            )
            gradv[pl.ds(pl.multiple_of(my_rows + g * group + r, 32), 32)] = (
                gmid[at] + by_value
            ).astype(half)
            late[0:1] += gain_part
            late[1:2] += shift_part

        by_rows(group, 32, rows)

    def grad_rows_at(by, g):
        start = pl.multiple_of(c * quarter + by * block + g * group, group)
        return gradv.at[pl.ds(start, group)]

    grad_copies = []
    for g in range(2):
        arrived(copies[g])
        first_back(g)
        if g:
            lateall[my_place] = late[...]
            late_copies = [send(late, lateall.at[my_place], dev) for dev in peers[0:7]]
        rows = grad_rows_at(y, g)
        grad_copies += [send(rows, rows, ynb), send(rows, rows, sib)]

    xf[x] = line_end(fc_z).T.astype(half)
    fc_x = send(xf.at[x], xf.at[x], xnb)
    arrived(out_z)
    value = gso[z].astype(single)
    for step in range(1, nz):
        value = value + gro[(z + step) % nz].astype(single)
    xo[x] = value.astype(half)
    out_x = send(xo.at[x], xo.at[x], xnb)
    proj_x.wait_recv()
    final = [fetch(xp_, gproj_hbm)]
    arrived(sv_copies)
    total = svall[0]
    for place in range(1, 8):
        total = total + svall[place]
    for piece in range(nz):
        s2[piece, 0:6] = total[0:6, piece * dz : (piece + 1) * dz]
        at = (piece % pieces) * dz
        s2[piece, 6:7] = svall[(piece // pieces) * 4 + t, 6:7, at : at + dz]
        s2[piece, 7:8] = jnp.zeros((1, dz), single)
    s2r[z] = s2[z]
    s2_copies = [
        send(s2.at[(z + step) % nz], s2r.at[z], zdev(step)) for step in range(1, nz)
    ]
    out_y.wait_recv()
    out_s.append(send(theirs, theirs, sib))
    bq_copy.wait_recv()
    arrived(late_copies)
    total = lateall[0]
    for place in range(1, 8):
        total = total + lateall[place]
    for piece in range(nz):
        l2[piece, 0:2] = total[:, piece * dz : (piece + 1) * dz]
        l2[piece, 2:3] = bqall[piece // pieces]
        l2[piece, 3:8] = jnp.zeros((5, dz), single)
    l2r[z] = l2[z]
    l2_copies = [
        send(l2.at[(z + step) % nz], l2r.at[z], zdev(step)) for step in range(1, nz)
    ]
    xq[x] = line_end(qkv_z).T.astype(half)
    qkv_x = send(xq.at[x], xq.at[x], xnb)
    grad_s_ = [grad_copies[1], grad_copies[3]]
    for g in range(2):
        grad_copies[2 * g].wait_recv()
        rows = grad_rows_at(1 - y, g)
        grad_s_.append(send(rows, rows, sib))
    arrived(out_s)
    final.append(fetch(outv, out_hbm))
    arrived([fc_x])
    final.append(fetch(xf, gfc_hbm))
    arrived([out_x])
    final.append(fetch(xo, gout_hbm))
    arrived(grad_s_)
    final.append(fetch(gradv, grad_hbm))
    arrived(s2_copies)
    small = s2r[0]
    for piece in range(1, nz):
        small = small + s2r[piece]
    gvec_ref[0:7] = small[0:7]
    arrived(l2_copies)
    small_late = l2r[0]
    for piece in range(1, nz):
        small_late = small_late + l2r[piece]
    gvec_ref[1:3] = small_late[0:2]
    q_line, v_line = small_late[2:3, 0:ec], small_late[2:3, ec : 2 * ec]
    even = jnp.where(low_lane, q_line, pltpu.roll(v_line, HD, 1))
    odd = jnp.where(low_lane, pltpu.roll(q_line, HD, 1), v_line)
    gvec_ref[7:8, 0:ec] = jnp.where(z % pieces == 0, even, odd)
    gvec_ref[7:8, ec:dz] = jnp.zeros((1, dz - ec), single)
    arrived([qkv_x])
    final.append(fetch(xq, gqkv_hbm))
    for copy in final:
        copy.wait()
    for copy in started:
        copy.wait_send()


def finish_kernel(
    out,
    grad,
    gqkv,
    gout,
    gfc,
    gproj,
    gvec,
    out_ref,
    grad_ref,
    gqkv_ref,
    gout_ref,
    gfc_ref,
    gproj_ref,
    gqv_ref,
    *line_refs,
):
    single = jnp.float32
    out_ref[...] = out[...]
    grad_ref[...] = grad[...]
    ec = gqkv_ref.shape[2]
    for j in range(3):
        gqkv_ref[j] = gqkv[0, :, j * ec : (j + 1) * ec].astype(single)
    gout_ref[...] = gout[0].astype(single)
    gfc_ref[...] = gfc[0].astype(single)
    gproj_ref[...] = gproj[0].astype(single)
    pair = gqv_ref.shape[1]
    gqv_ref[0:1] = gvec[7:8, 0:pair]
    gqv_ref[1:2] = gvec[7:8, pair : 2 * pair]
    for row, ref in enumerate(line_refs):
        ref[...] = gvec[row : row + 1]


def plane_block(
    nz,
    block_input,
    segment_ids,
    cotangent,
    qkv_weight,
    qv_bias,
    out_weight,
    out_bias,
    norm1_gain,
    norm1_shift,
    fc_weight,
    fc_bias,
    proj_weight,
    proj_bias,
    norm2_gain,
    norm2_shift,
):
    half = jnp.bfloat16
    single = jnp.float32
    _, rows, width = block_input.shape
    length = segment_ids.shape[1]
    dz = qkv_weight.shape[0]
    ec = qkv_weight.shape[2] // 2
    fch = fc_weight.shape[1] // 2
    quarter, block = rows // 2, rows // 4
    vmem = pltpu.VMEM
    spans = [(i + 1 - max(0, i - 2)) * quarter for i in range(4)]
    heads = ec // HD
    scratch = [
        vmem((dz, 3 * ec), single),
        vmem((ec, dz), single),
        vmem((dz, fch), single),
        vmem((fch, dz), single),
        vmem((rows, width), half),
        vmem((2, quarter, width), half),
        vmem((2, 2, quarter, width), half),
        vmem((2, 2, quarter, width), half),
        vmem((nz, dz, 6 * ec), half),
        vmem((nz, 2 * ec, dz), half),
        vmem((2, nz, dz, fch), half),
        vmem((2, nz, fch, dz), half),
        vmem((2, nz, 8, dz), single),
        vmem((8, width), single),
        vmem((2, fch), single),
        vmem((length, ec), half),
        vmem((length, ec), half),
        vmem((length, ec), half),
    ]
    scratch += [vmem((heads, quarter, span), half) for span in spans]
    scratch += [
        vmem((length, 128), single),
        vmem((2, 2, quarter, ec), half),
        vmem((2, quarter, 2 * ec), half),
        vmem((4, 2, 2, 2, 2, block // 2, width // 2), half),
        vmem((4, 2, 6, block // 2, width // 2), half),
        vmem((block, width), single),
        vmem((2, 2, 2, block, width), half),
        vmem((2, 2, 2, block, width), half),
        vmem((2, 2, rows, fch), half),
        vmem((2, 2, rows, fch), half),
        vmem((fch, length), half),
    ]
    for _ in range(2):
        scratch += [
            vmem((nz, 3 * ec, dz), half),
            vmem((nz, ec, dz), half),
            vmem((nz, fch, dz), half),
            vmem((nz, fch, dz), half),
        ]
    scratch += [
        vmem((3 * ec, dz), half),
        vmem((fch, dz), half),
        vmem((fch, dz), half),
        vmem((fch, dz), single),
        vmem((2, dz, 3 * ec), half),
        vmem((2, ec, dz), half),
        vmem((2, dz, fch), half),
        vmem((2, fch, dz), half),
        vmem((2, 4, 2, block // 2, ec), half),
        vmem((2, 4, 2, block // 2, ec), half),
        vmem((length, ec), single),
        vmem((length, ec), single),
        vmem((2, 2, quarter, 3 * ec), half),
        vmem((2, quarter, 6 * ec), half),
        vmem((quarter, 3 * quarter), single),
        vmem((quarter, 3 * quarter), single),
        vmem((2, rows, fch), single),
        vmem((2, quarter, 3 * quarter), half),
        vmem((rows, width), half),
        vmem((rows, width), half),
        vmem((block, width), single),
        vmem((8, width), single),
        vmem((8, 8, width), single),
        vmem((2, width), single),
        vmem((8, 2, width), single),
        vmem((2, 1, dz), single),
        vmem((nz, 8, dz), single),
        vmem((nz, 8, dz), single),
        vmem((nz, 8, dz), single),
        vmem((nz, 8, dz), single),
        pltpu.SemaphoreType.DMA((300,)),
        pltpu.SemaphoreType.DMA((300,)),
        pltpu.SemaphoreType.DMA((20,)),
    ]
    whole = pl.BlockSpec(memory_space=pltpu.VMEM)
    there = pl.BlockSpec(memory_space=pl.ANY)
    middle = pl.pallas_call(
        functools.partial(block_kernel, nz),
        out_shape=(
            jax.ShapeDtypeStruct((rows, width), half),
            jax.ShapeDtypeStruct((rows, width), half),
            jax.ShapeDtypeStruct((2, dz, 3 * ec), half),
            jax.ShapeDtypeStruct((2, ec, dz), half),
            jax.ShapeDtypeStruct((2, dz, fch), half),
            jax.ShapeDtypeStruct((2, fch, dz), half),
            jax.ShapeDtypeStruct((8, dz), single),
        ),
        in_specs=[there] * 2 + [whole] + [there] * 4 + [whole] * 8,
        out_specs=(there,) * 6 + (whole,),
        scratch_shapes=scratch,
        compiler_params=pltpu.CompilerParams(
            collective_id=0, has_side_effects=True, vmem_limit_bytes=67043328
        ),
        name="residual_block",
    )(
        block_input.reshape(rows, width),
        cotangent.reshape(rows, width),
        segment_ids,
        qkv_weight.transpose(1, 0, 2),
        out_weight,
        fc_weight,
        proj_weight,
        out_bias.reshape(1, dz),
        norm1_gain.reshape(1, dz),
        norm1_shift.reshape(1, dz),
        norm2_gain.reshape(1, dz),
        norm2_shift.reshape(1, dz),
        proj_bias.reshape(1, dz),
        fc_bias.reshape(1, dz),
        qv_bias,
    )

    def halves(shape, axis):
        return pl.BlockSpec(
            shape, lambda side: tuple(side if k == axis else 0 for k in range(len(shape)))
        )

    line = pl.BlockSpec((1, dz), lambda side: (0, 0))
    outs = pl.pallas_call(
        finish_kernel,
        grid=(2,),
        out_shape=(
            jax.ShapeDtypeStruct((rows, width), half),
            jax.ShapeDtypeStruct((rows, width), half),
            jax.ShapeDtypeStruct((3, dz, 2 * ec), single),
            jax.ShapeDtypeStruct((2 * ec, dz), single),
            jax.ShapeDtypeStruct((dz, 2 * fch), single),
            jax.ShapeDtypeStruct((2 * fch, dz), single),
            jax.ShapeDtypeStruct(qv_bias.shape, single),
        )
        + (jax.ShapeDtypeStruct((1, dz), single),) * 7,
        in_specs=[
            halves((quarter, width), 0),
            halves((quarter, width), 0),
            halves((1, dz, 3 * ec), 0),
            halves((1, ec, dz), 0),
            halves((1, dz, fch), 0),
            halves((1, fch, dz), 0),
            pl.BlockSpec((8, dz), lambda side: (0, 0)),
        ],
        out_specs=(
            halves((quarter, width), 0),
            halves((quarter, width), 0),
            halves((3, dz, ec), 2),
            halves((ec, dz), 0),
            halves((dz, fch), 1),
            halves((fch, dz), 0),
            pl.BlockSpec(qv_bias.shape, lambda side: (0, 0)),
        )
        + (line,) * 7,
        name="finish",
    )(*middle)
    out, grad, gqkv, gout, gfc, gproj, gqv = outs[:7]
    gbout, ggain1, gshift1, ggain2, gshift2, gbproj, gbfc = [
        value.reshape(dz) for value in outs[7:]
    ]
    return (
        out.reshape(block_input.shape),
        grad.reshape(block_input.shape),
        gqkv.transpose(1, 0, 2),
        gqv,
        gout,
        gbout,
        ggain1,
        gshift1,
        gfc,
        gbfc,
        gproj,
        gbproj,
        ggain2,
        gshift2,
    )


def device_program(mesh):
    planes = mesh.shape["fsdp"]

    def program(block_input, *others):
        seqs_here, rows, width = block_input.shape
        one_kernel = (
            seqs_here == 1
            and mesh.shape["ctx"] == 2
            and mesh.shape["tp"] == 4
            and planes == 4
            and width // planes == 256
        )
        if one_kernel:
            return plane_block(planes, block_input, *others)
        return on_device(block_input, *others)

    return program


def solution(mesh):
    return jax.shard_map(
        device_program(mesh),
        mesh=mesh,
        in_specs=(
            P("fsdp", "ctx", None),
            P("fsdp", None),
            P("fsdp", "ctx", None),
            P("fsdp", None, "tp"),
            P(None, ("tp", "fsdp")),
            P("tp", "fsdp"),
            P("fsdp"),
            P("fsdp"),
            P("fsdp"),
            P("fsdp", "tp"),
            P(("tp", "fsdp")),
            P("tp", "fsdp"),
            P("fsdp"),
            P("fsdp"),
            P("fsdp"),
        ),
        out_specs=(
            P("fsdp", "ctx", None),
            P("fsdp", "ctx", None),
            P("fsdp", None, "tp"),
            P(None, ("tp", "fsdp")),
            P("tp", "fsdp"),
            P("fsdp"),
            P("fsdp"),
            P("fsdp"),
            P("fsdp", "tp"),
            P(("tp", "fsdp")),
            P("tp", "fsdp"),
            P("fsdp"),
            P("fsdp"),
            P("fsdp"),
        ),
        check_vma=False,
    )
```

```python
import functools

import jax
import jax.numpy as jnp
from jax import lax
from jax.experimental import pallas as pl
from jax.experimental.pallas import tpu as pltpu
from jax.sharding import PartitionSpec as P

HD = 64


epsilon = 1e-05


def layer_norm(values, gain, shift):
    centred = values - jnp.mean(values, axis=-1, keepdims=True)
    spread = jnp.mean(centred * centred, axis=-1, keepdims=True)
    return centred * lax.rsqrt(spread + epsilon) * gain + shift


def gelu_act(values):
    return jax.nn.gelu(values, approximate=True)


def on_device(
    block_input,
    segment_ids,
    cotangent,
    qkv_weight,
    qv_bias,
    out_weight,
    out_bias,
    norm1_gain,
    norm1_shift,
    fc_weight,
    fc_bias,
    proj_weight,
    proj_bias,
    norm2_gain,
    norm2_shift,
):
    half = jnp.bfloat16
    single = jnp.float32
    seqs_here, rows_seq, model_width = block_input.shape
    row_count = seqs_here * rows_seq
    shard_index = lax.axis_index("ctx")
    scale_factor = HD ** (-0.5)
    (
        wqkv_low,
        bqv_low,
        wout_low,
        bout_low,
        gain1_low,
        shift1_low,
        wfc_low,
        bfc_low,
        wproj_low,
        bproj_low,
        gain2_low,
        shift2_low,
    ) = (
        lax.all_gather(qkv_weight.astype(half), "fsdp", axis=0, tiled=True),
        lax.all_gather(qv_bias.astype(half), "fsdp", axis=1, tiled=True),
        lax.all_gather(out_weight.astype(half), "fsdp", axis=1, tiled=True),
        lax.all_gather(out_bias.astype(half), "fsdp", axis=0, tiled=True),
        lax.all_gather(norm1_gain.astype(half), "fsdp", axis=0, tiled=True),
        lax.all_gather(norm1_shift.astype(half), "fsdp", axis=0, tiled=True),
        lax.all_gather(fc_weight.astype(half), "fsdp", axis=0, tiled=True),
        lax.all_gather(fc_bias.astype(half), "fsdp", axis=0, tiled=True),
        lax.all_gather(proj_weight.astype(half), "fsdp", axis=1, tiled=True),
        lax.all_gather(proj_bias.astype(half), "fsdp", axis=0, tiled=True),
        lax.all_gather(norm2_gain.astype(half), "fsdp", axis=0, tiled=True),
        lax.all_gather(norm2_shift.astype(half), "fsdp", axis=0, tiled=True),
    )
    gain_first = gain1_low.astype(single)
    shift_first = shift1_low.astype(single)
    gain_second = gain2_low.astype(single)
    shift_second = shift2_low.astype(single)
    inputs = block_input.reshape(row_count, model_width).astype(single)
    normed_first = layer_norm(inputs, gain_first, shift_first).astype(half)
    projected = jnp.einsum("rd,dce->rce", normed_first, wqkv_low, preferred_element_type=single)
    bias_pair = bqv_low.astype(single)
    queries = (projected[:, 0] + bias_pair[0]).astype(half)
    key_rows = projected[:, 1].astype(half)
    value_rows = (projected[:, 2] + bias_pair[1]).astype(half)
    local_width = queries.shape[1]
    head_count = local_width // HD
    keys_all, values_all = (
        lax.all_gather(
            key_rows.reshape(seqs_here, rows_seq, local_width), "ctx", axis=1, tiled=True
        ),
        lax.all_gather(
            value_rows.reshape(seqs_here, rows_seq, local_width), "ctx", axis=1, tiled=True
        ),
    )
    length = keys_all.shape[1]
    query_pos = shard_index * rows_seq + jnp.arange(rows_seq)
    key_pos = jnp.arange(length)
    seg_query = lax.dynamic_slice_in_dim(segment_ids, shard_index * rows_seq, rows_seq, 1)
    query_heads = queries.reshape(seqs_here, rows_seq, head_count, HD)
    key_heads = keys_all.reshape(seqs_here, length, head_count, HD)
    value_heads = values_all.reshape(seqs_here, length, head_count, HD)

    def masked_scores(query_blk, key_blk, seg_row, seg_here):
        raw = (
            jnp.einsum("qhe,khe->hqk", query_blk, key_blk, preferred_element_type=single)
            * scale_factor
        )
        allowed = (key_pos[None, :] <= query_pos[:, None]) & (seg_here[:, None] == seg_row[None, :])
        return jnp.where(allowed[None], raw, -1e30)

    def attend(packed):
        query_blk, key_blk, value_blk, seg_row, seg_here = packed
        masked = masked_scores(query_blk, key_blk, seg_row, seg_here)
        row_max = jnp.max(masked, axis=-1, keepdims=True)
        expo = jnp.exp(masked - row_max)
        row_total = jnp.sum(expo, axis=-1, keepdims=True)
        probs_low = (expo / row_total).astype(half)
        attended = jnp.einsum("hqk,khe->qhe", probs_low, value_blk, preferred_element_type=single)
        return (attended.astype(half), row_max + jnp.log(row_total))

    attended, log_total = lax.map(
        attend, (query_heads, key_heads, value_heads, segment_ids, seg_query)
    )
    attended_rows = attended.reshape(row_count, local_width)
    attn_partial = jnp.dot(attended_rows, wout_low, preferred_element_type=single)
    attn_total = lax.psum(attn_partial.astype(jnp.bfloat16), "tp").astype(jnp.float32)
    middle = inputs + attn_total + bout_low.astype(single)
    normed_second = layer_norm(middle, gain_second, shift_second).astype(half)
    pre_act = jnp.dot(normed_second, wfc_low, preferred_element_type=single) + bfc_low.astype(
        single
    )
    act_low = gelu_act(pre_act).astype(half)
    mlp_total = lax.psum(
        jnp.dot(act_low, wproj_low, preferred_element_type=single).astype(jnp.bfloat16), "tp"
    ).astype(jnp.float32)
    out_rows = (middle + mlp_total + bproj_low.astype(single)).astype(half)
    wqkv_use, wout_use, wfc_use, wproj_use = (
        lax.all_gather(qkv_weight.astype(half), "fsdp", axis=0, tiled=True),
        lax.all_gather(out_weight.astype(half), "fsdp", axis=1, tiled=True),
        lax.all_gather(fc_weight.astype(half), "fsdp", axis=0, tiled=True),
        lax.all_gather(proj_weight.astype(half), "fsdp", axis=1, tiled=True),
    )
    grad_out = cotangent.reshape(row_count, model_width).astype(single)
    grad_out_low = cotangent.reshape(row_count, model_width)
    grad_bproj = jnp.sum(grad_out_low, axis=0, dtype=single)
    grad_wproj = jnp.einsum("rf,rd->fd", act_low, grad_out_low, preferred_element_type=single)
    grad_act = jnp.einsum("rd,fd->rf", grad_out_low, wproj_use, preferred_element_type=single)
    gelu_unused, gelu_pull = jax.vjp(gelu_act, pre_act)
    grad_pre = gelu_pull(grad_act)[0].astype(half)
    grad_bfc = jnp.sum(grad_pre, axis=0, dtype=single)
    grad_wfc = jnp.einsum("rd,rf->df", normed_second, grad_pre, preferred_element_type=single)
    norm2_partial = jnp.einsum("rf,df->rd", grad_pre, wfc_use, preferred_element_type=single)
    grad_norm2 = lax.psum(norm2_partial.astype(jnp.bfloat16), "tp").astype(jnp.float32)
    norm_unused, second_pull = jax.vjp(layer_norm, middle, gain_second, shift_second)
    grad_mid_ln, grad_gain2, grad_shift2 = second_pull(grad_norm2)
    grad_middle = grad_out + grad_mid_ln
    grad_mid_low = grad_middle.astype(half)
    grad_bout = jnp.sum(grad_mid_low, axis=0, dtype=single)
    grad_wout = jnp.einsum("rk,rd->kd", attended_rows, grad_mid_low, preferred_element_type=single)
    grad_att = jnp.einsum(
        "rd,kd->rk", grad_mid_low, wout_use, preferred_element_type=single
    ).astype(half)
    grad_att_heads = grad_att.reshape(seqs_here, rows_seq, head_count, HD)

    def attend_back(packed):
        query_blk, key_blk, value_blk, seg_row, seg_here, log_blk, grad_blk = packed
        masked = masked_scores(query_blk, key_blk, seg_row, seg_here)
        attn_probs = jnp.exp(masked - log_blk)
        probs_low = attn_probs.astype(half)
        grad_value = jnp.einsum("hqk,qhe->khe", probs_low, grad_blk, preferred_element_type=single)
        grad_probs = jnp.einsum("qhe,khe->hqk", grad_blk, value_blk, preferred_element_type=single)
        row_delta = jnp.sum(grad_probs * attn_probs, axis=-1, keepdims=True)
        grad_scores = (attn_probs * (grad_probs - row_delta)).astype(half)
        grad_query = (
            jnp.einsum("hqk,khe->qhe", grad_scores, key_blk, preferred_element_type=single)
            * scale_factor
        )
        grad_key = (
            jnp.einsum("hqk,qhe->khe", grad_scores, query_blk, preferred_element_type=single)
            * scale_factor
        )
        return (grad_query.astype(half), grad_key, grad_value)

    grad_query, grad_key, grad_value = lax.map(
        attend_back,
        (query_heads, key_heads, value_heads, segment_ids, seg_query, log_total, grad_att_heads),
    )
    grad_key, grad_value = (
        lax.psum_scatter(
            grad_key.reshape(seqs_here, length, local_width).astype(jnp.bfloat16),
            "ctx",
            scatter_dimension=1,
            tiled=True,
        ).astype(jnp.float32),
        lax.psum_scatter(
            grad_value.reshape(seqs_here, length, local_width).astype(jnp.bfloat16),
            "ctx",
            scatter_dimension=1,
            tiled=True,
        ).astype(jnp.float32),
    )
    grad_query = grad_query.reshape(row_count, local_width)
    grad_key = grad_key.reshape(row_count, local_width).astype(half)
    grad_value = grad_value.reshape(row_count, local_width).astype(half)
    grad_qkv = jnp.stack([grad_query, grad_key, grad_value], axis=1)
    grad_bqv = jnp.stack(
        [jnp.sum(grad_query, axis=0, dtype=single), jnp.sum(grad_value, axis=0, dtype=single)]
    )
    grad_wqkv = jnp.einsum("rd,rce->dce", normed_first, grad_qkv, preferred_element_type=single)
    norm1_partial = jnp.einsum("rce,dce->rd", grad_qkv, wqkv_use, preferred_element_type=single)
    grad_norm1 = lax.psum(norm1_partial.astype(jnp.bfloat16), "tp").astype(jnp.float32)
    first_unused, first_pull = jax.vjp(layer_norm, inputs, gain_first, shift_first)
    grad_in_ln, grad_gain1, grad_shift1 = first_pull(grad_norm1)
    input_rows = (grad_middle + grad_in_ln).astype(half)
    block_output = out_rows.reshape(block_input.shape)
    input_grad = input_rows.reshape(block_input.shape)
    (
        sum_wqkv,
        sum_bqv,
        sum_wout,
        sum_bout,
        sum_gain1,
        sum_shift1,
        sum_wfc,
        sum_bfc,
        sum_wproj,
        sum_bproj,
        sum_gain2,
        sum_shift2,
    ) = (
        lax.psum_scatter(grad_wqkv, ("fsdp", "ctx"), scatter_dimension=0, tiled=True),
        lax.psum_scatter(grad_bqv, ("fsdp", "ctx"), scatter_dimension=1, tiled=True),
        lax.psum_scatter(grad_wout, ("fsdp", "ctx"), scatter_dimension=1, tiled=True),
        lax.psum_scatter(grad_bout, ("fsdp", "ctx"), scatter_dimension=0, tiled=True),
        lax.psum_scatter(grad_gain1, ("fsdp", "ctx"), scatter_dimension=0, tiled=True),
        lax.psum_scatter(grad_shift1, ("fsdp", "ctx"), scatter_dimension=0, tiled=True),
        lax.psum_scatter(grad_wfc, ("fsdp", "ctx"), scatter_dimension=0, tiled=True),
        lax.psum_scatter(grad_bfc, ("fsdp", "ctx"), scatter_dimension=0, tiled=True),
        lax.psum_scatter(grad_wproj, ("fsdp", "ctx"), scatter_dimension=1, tiled=True),
        lax.psum_scatter(grad_bproj, ("fsdp", "ctx"), scatter_dimension=0, tiled=True),
        lax.psum_scatter(grad_gain2, ("fsdp", "ctx"), scatter_dimension=0, tiled=True),
        lax.psum_scatter(grad_shift2, ("fsdp", "ctx"), scatter_dimension=0, tiled=True),
    )
    (
        final_wqkv,
        final_bqv,
        final_wout,
        final_bout,
        final_gain1,
        final_shift1,
        final_wfc,
        final_bfc,
        final_wproj,
        final_bproj,
        final_gain2,
        final_shift2,
    ) = (
        lax.all_gather(sum_wqkv.astype(jnp.bfloat16), "ctx", axis=0, tiled=True).astype(
            sum_wqkv.dtype
        ),
        lax.all_gather(sum_bqv.astype(jnp.bfloat16), "ctx", axis=1, tiled=True).astype(
            sum_bqv.dtype
        ),
        lax.all_gather(sum_wout.astype(jnp.bfloat16), "ctx", axis=1, tiled=True).astype(
            sum_wout.dtype
        ),
        lax.all_gather(sum_bout.astype(jnp.bfloat16), "ctx", axis=0, tiled=True).astype(
            sum_bout.dtype
        ),
        lax.all_gather(sum_gain1.astype(jnp.bfloat16), "ctx", axis=0, tiled=True).astype(
            sum_gain1.dtype
        ),
        lax.all_gather(sum_shift1.astype(jnp.bfloat16), "ctx", axis=0, tiled=True).astype(
            sum_shift1.dtype
        ),
        lax.all_gather(sum_wfc.astype(jnp.bfloat16), "ctx", axis=0, tiled=True).astype(
            sum_wfc.dtype
        ),
        lax.all_gather(sum_bfc.astype(jnp.bfloat16), "ctx", axis=0, tiled=True).astype(
            sum_bfc.dtype
        ),
        lax.all_gather(sum_wproj.astype(jnp.bfloat16), "ctx", axis=1, tiled=True).astype(
            sum_wproj.dtype
        ),
        lax.all_gather(sum_bproj.astype(jnp.bfloat16), "ctx", axis=0, tiled=True).astype(
            sum_bproj.dtype
        ),
        lax.all_gather(sum_gain2.astype(jnp.bfloat16), "ctx", axis=0, tiled=True).astype(
            sum_gain2.dtype
        ),
        lax.all_gather(sum_shift2.astype(jnp.bfloat16), "ctx", axis=0, tiled=True).astype(
            sum_shift2.dtype
        ),
    )
    return (
        block_output,
        input_grad,
        final_wqkv,
        final_bqv,
        final_wout,
        final_bout,
        final_gain1,
        final_shift1,
        final_wfc,
        final_bfc,
        final_wproj,
        final_bproj,
        final_gain2,
        final_shift2,
    )


MESH = pl.DeviceIdType.MESH


def dot_nn(left, right):
    return lax.dot_general(
        left, right, (((1,), (0,)), ((), ())), preferred_element_type=jnp.float32
    )


def dot_nt(left, right):
    return lax.dot_general(
        left, right, (((1,), (1,)), ((), ())), preferred_element_type=jnp.float32
    )


def by_rows(rows, step, body):
    def one(index, carry):
        body(pl.multiple_of(index * step, step))
        return carry

    lax.fori_loop(0, rows // step, one, 0)


def norm_parts(values):
    centred = values - jnp.mean(values, axis=-1, keepdims=True)
    spread = jnp.mean(centred * centred, axis=-1, keepdims=True)
    return centred, lax.rsqrt(spread + epsilon)


def norm_back(values, incoming, gain):
    centred, rate = norm_parts(values)
    hat = centred * rate
    scaled = incoming * gain
    by_value = rate * (
        scaled
        - jnp.mean(scaled, axis=-1, keepdims=True)
        - hat * jnp.mean(scaled * hat, axis=-1, keepdims=True)
    )
    return (
        by_value,
        jnp.sum(incoming * hat, axis=0, keepdims=True),
        jnp.sum(incoming, axis=0, keepdims=True),
    )


class Partly:
    def __init__(self, copy, sends, receives):
        self.copy, self.sends, self.receives = copy, sends, receives

    def start(self):
        self.copy.start()

    def wait_recv(self):
        pl.when(self.receives)(self.copy.wait_recv)

    def wait_send(self):
        pl.when(self.sends)(self.copy.wait_send)


def block_kernel(
    nz,
    x_in,
    dy_in,
    seg_row,
    wqkv_in,
    wout_in,
    wfc_in,
    wproj_in,
    bout_in,
    gain1_in,
    shift1_in,
    gain2_in,
    shift2_in,
    bproj_in,
    bfc_in,
    bqv_in,
    out_hbm,
    grad_hbm,
    gqkv_hbm,
    gout_hbm,
    gfc_hbm,
    gproj_hbm,
    gvec_ref,
    stq,
    sto,
    stf,
    stp,
    xl,
    xr,
    dyb,
    nf,
    wq,
    wo,
    wf,
    wp,
    vec,
    full,
    fcb,
    qb,
    kb,
    vb,
    p0,
    p1,
    p2,
    p3,
    segc,
    ao,
    ax,
    srs,
    rrs,
    mid,
    ns,
    gm,
    act,
    gp,
    turned,
    gsq,
    gso,
    gsf,
    gsp,
    grq,
    gro,
    grf,
    grp,
    glq,
    glf,
    glp,
    accum,
    xq,
    xo,
    xf,
    xp_,
    gtt,
    gt,
    dkb,
    dvb,
    dqkv,
    dx,
    wide,
    wide_b,
    slope,
    gact,
    dsb,
    outv,
    gradv,
    gmid,
    sv,
    svall,
    late,
    lateall,
    bqline,
    l2,
    l2r,
    s2,
    s2r,
    send_sem,
    recv_sem,
    local_sem,
):
    half = jnp.bfloat16
    single = jnp.float32
    z = lax.axis_index("fsdp")
    x = lax.axis_index("ctx")
    t = lax.axis_index("tp")
    y = t // 2
    c = t % 2
    quarter = xl.shape[0] // 2
    block = quarter // 2
    width = xl.shape[1]
    dz = width // nz
    fch = wf.shape[3]
    ec = qb.shape[1]
    length = qb.shape[0]
    probs = (p0, p1, p2, p3)
    sib = (z, x, y * 2 + 1 - c)
    ynb = (z, x, (1 - y) * 2 + c)
    xnb = (z, 1 - x, t)
    dia = (z, 1 - x, (1 - y) * 2 + c)
    started = []

    def send(src, dst, dev):
        slot = len(started)
        copy = pltpu.make_async_remote_copy(
            src_ref=src,
            dst_ref=dst,
            send_sem=send_sem.at[slot],
            recv_sem=recv_sem.at[slot],
            device_id=dev,
            device_id_type=MESH,
        )
        copy.start()
        started.append(copy)
        return copy

    def arrived(copies):
        for copy in copies:
            copy.wait_recv()

    def send_if(src, dst, dev, sends, receives, start=True):
        slot = len(started)
        copy = pltpu.make_async_remote_copy(
            src_ref=src,
            dst_ref=dst,
            send_sem=send_sem.at[slot],
            recv_sem=recv_sem.at[slot],
            device_id=dev,
            device_id_type=MESH,
        )
        some = Partly(copy, sends, receives)
        if start:
            pl.when(sends)(copy.start)
        started.append(some)
        return some

    fetched = []

    def fetch(src, dst):
        copy = pltpu.make_async_copy(src, dst, local_sem.at[len(fetched)])
        copy.start()
        fetched.append(copy)
        return copy

    def zdev(step):
        return ((z + step) % nz, x, t)

    right, left = zdev(1), zdev(nz - 1)

    peers = [(z, px, pt) for px in (x, 1 - x) for pt in (t, sib[2], ynb[2], (1 - y) * 2 + 1 - c)][
        1:
    ]
    for step in range(1, nz):
        peers += [((z + step) % nz, x, t), ((z + step) % nz, x, sib[2])]
    barrier = pltpu.get_barrier_semaphore()
    for dev in peers:
        pl.semaphore_signal(barrier, inc=1, device_id=dev, device_id_type=MESH)

    my_e = pl.ds(pl.multiple_of(x * ec, ec), ec)
    my_f = pl.ds(pl.multiple_of(x * fch, fch), fch)
    stage_q = [
        fetch(wqkv_in.at[j, :, my_e], stq.at[:, j * ec : (j + 1) * ec]) for j in range(3)
    ]
    stage_x = fetch(x_in, xl)
    stage_o = fetch(wout_in.at[my_e], sto)
    stage_f = fetch(wfc_in.at[:, my_f], stf)
    stage_p = fetch(wproj_in.at[my_f], stp)
    stage_dy = [
        fetch(dy_in.at[pl.ds(s * quarter, quarter)], dyb.at[s, x]) for s in range(2)
    ]

    def weight_at(which, h, plane):
        if which == 0:
            return wq.at[plane, :, pl.ds(pl.multiple_of(h * 3 * ec, ec), 3 * ec)]
        if which == 1:
            return wo.at[plane, pl.ds(pl.multiple_of(h * ec, ec), ec)]
        if which == 2:
            return wf.at[h, plane]
        part = fch // 2
        return wp.at[h, plane, (which - 3) * part : (which - 2) * part]

    def rounded(src, dst, rows):
        def some(r):
            dst[pl.ds(r, 64)] = src[pl.ds(r, 64)].astype(half)

        by_rows(rows, 64, some)

    lines = [[], [], [], [], []]
    weight_sib = [[], [], [], [], []]

    def line_start(which):
        mine = weight_at(which, c, z)
        lines[which].append(
            (
                send_if(mine, mine, right, z < nz - 1, z >= 1),
                send_if(mine, mine, left, z >= 1, z < nz - 1),
            )
        )

    def line_pass(which, step):
        from_left, from_right = lines[which][step - 1]
        lower = weight_at(which, c, (z + nz - step) % nz)
        upper = weight_at(which, c, (z + step) % nz)
        from_left.wait_recv()
        if step < nz - 1:
            to_right = send_if(
                lower, lower, right, (z >= step) & (z < nz - 1), z >= step + 1
            )
        weight_sib[which].append(send_if(lower, lower, sib, z >= step, z >= step))
        from_right.wait_recv()
        if step < nz - 1:
            to_left = send_if(
                upper, upper, left, (z + step < nz) & (z >= 1), z + step + 1 < nz
            )
            lines[which].append((to_right, to_left))
        weight_sib[which].append(send_if(upper, upper, sib, z + step < nz, z + step < nz))

    def to_sibling(which):
        mine = weight_at(which, c, z)
        weight_sib[which].append(send(mine, mine, sib))

    for copy in stage_q:
        copy.wait()
    rounded(stq, weight_at(0, c, z), dz)
    pl.semaphore_wait(barrier, len(peers))

    line_start(0)
    stage_x.wait()
    x_copy = send(xl.at[pl.ds(pl.multiple_of(c * quarter, quarter), quarter)], xr.at[c], xnb)
    for row, line in enumerate(
        (bout_in, gain1_in, shift1_in, gain2_in, shift2_in, bproj_in, bfc_in)
    ):
        vec[c, z, row : row + 1] = line[...].astype(half).astype(single)
    pair = bqv_in.shape[1]
    vec[c, z, 7:8, 0:pair] = bqv_in[0:1].astype(half).astype(single)
    vec[c, z, 7:8, pair : 2 * pair] = bqv_in[1:2].astype(half).astype(single)
    vec[c, z, 7:8, 2 * pair :] = jnp.zeros((1, dz - 2 * pair), single)
    vec_copies = [send(vec.at[c, z], vec.at[c, z], sib)]
    for step in range(1, nz):
        for dev_t in (t, sib[2]):
            vec_copies.append(send(vec.at[c, z], vec.at[c, z], ((z + step) % nz, x, dev_t)))
    stage_o.wait()
    rounded(sto, weight_at(1, c, z), ec)
    line_start(1)
    to_sibling(0)
    to_sibling(1)
    for copy in stage_dy:
        copy.wait()
    stage_f.wait()
    rounded(stf, weight_at(2, c, z), dz)
    stage_p.wait()
    rounded(stp, wp.at[c, z], fch)

    arrived(vec_copies)
    for piece in range(nz):
        full[:, piece * dz : (piece + 1) * dz] = vec[c, piece]
    pieces = nz // 2
    for h in range(2):
        for k in range(pieces):
            fcb[h : h + 1, k * dz : (k + 1) * dz] = vec[h, x * pieces + k][6:7]
    lane = lax.broadcasted_iota(jnp.int32, (1, ec), 1)
    low_lane = lane < HD
    first_piece = vec[c, x * pieces][7:8, 0:ec]
    next_piece = vec[c, x * pieces + 1][7:8, 0:ec]
    q_bias = jnp.where(low_lane, first_piece, pltpu.roll(next_piece, HD, 1))
    v_bias = jnp.where(low_lane, pltpu.roll(first_piece, HD, 1), next_piece)
    out_bias = full[0:1]
    gain1, shift1 = full[1:2], full[2:3]
    gain2, shift2 = full[3:4], full[4:5]
    proj_bias = full[5:6]

    def first_norm(src, dst):
        def rows(r):
            centred, rate = norm_parts(src[pl.ds(r, 64)].astype(single))
            dst[pl.ds(r, 64)] = (centred * rate * gain1 + shift1).astype(half)

        by_rows(quarter, 64, rows)

    for s in range(2):
        first_norm(xl.at[pl.ds(s * quarter, quarter)], nf.at[x, s])
    line_pass(0, 1)
    line_pass(1, 1)
    line_pass(0, 2)
    line_pass(1, 2)
    line_start(2)
    line_start(3)
    to_sibling(2)
    to_sibling(3)
    to_sibling(4)
    x_copy.wait_recv()
    x_fwd = send(xr.at[c], xr.at[c], sib)
    dy_copy = send(dyb.at[c, x], dyb.at[c, x], xnb)
    first_norm(xr.at[c], nf.at[1 - x, c])
    x_fwd.wait_recv()
    first_norm(xr.at[1 - c], nf.at[1 - x, 1 - c])
    for i in range(length // quarter):
        line = seg_row[:, i * quarter : (i + 1) * quarter].astype(single)
        segc[i * quarter : (i + 1) * quarter] = jnp.broadcast_to(line, (128, quarter)).T
    for step in range(3, nz):
        line_pass(0, step)
        line_pass(1, step)

    my_qkv = pl.ds(pl.multiple_of(c * 3 * ec, ec), 3 * ec)
    for xi in range(2):
        for ci in range(2):
            proj = dot_nn(nf[xi, ci], wq[:, :, my_qkv].reshape(width, 3 * ec))
            at = pl.ds((xi * 2 + ci) * quarter, quarter)
            qb[at] = (proj[:, 0:ec] + q_bias).astype(half)
            kb[at] = proj[:, ec : 2 * ec].astype(half)
            vb[at] = (proj[:, 2 * ec :] + v_bias).astype(half)

    head_lane = lax.broadcasted_iota(jnp.int32, (1, ec), 1) // HD
    n_blocks = length // quarter
    heads = ec // HD

    def only(values, h):
        return jnp.where(head_lane == h, values, jnp.zeros_like(values))

    for i in range(n_blocks):
        j0 = max(0, i - 2)
        span = (i + 1 - j0) * quarter
        keys = pl.ds(j0 * quarter, span)
        scores = (wide, wide_b)
        for h in range(heads):
            q_h = only(qb[pl.ds(i * quarter, quarter)], h) * jnp.asarray(HD**-0.5, half)
            scores[h][:, 0:span] = dot_nt(q_h, kb[keys])

        def soft(r, i=i, j0=j0, span=span):
            q_at = i * quarter + r + lax.broadcasted_iota(jnp.int32, (64, span), 0)
            k_at = j0 * quarter + lax.broadcasted_iota(jnp.int32, (64, span), 1)
            seg_q = segc[pl.ds(pl.multiple_of(i * quarter + r, 64), 64)]
            seg_k = seg_row[:, j0 * quarter : j0 * quarter + span].astype(single)
            same = jnp.concatenate([seg_q] * (span // 128), axis=1) == seg_k
            allowed = (k_at <= q_at) & same
            for h in range(heads):
                masked = jnp.where(allowed, scores[h][pl.ds(r, 64), 0:span], -1e30)
                expo = jnp.exp(masked - jnp.max(masked, axis=-1, keepdims=True))
                share = expo * (1.0 / jnp.sum(expo, axis=-1, keepdims=True))
                probs[i][h, pl.ds(r, 64)] = share.astype(half)

        by_rows(quarter, 64, soft)
        total = None
        for h in range(heads):
            part = dot_nn(probs[i][h], only(vb[keys], h))
            total = part if total is None else total + part
        ao[i // 2, i % 2] = total.astype(half)

    my_ax = pl.ds(pl.multiple_of(c * ec, ec), ec)
    att_copy = send(ao.at[:, 1 - c], ax.at[:, :, my_ax], sib)
    ax[:, :, my_ax] = ao[:, c]
    line_pass(2, 1)
    line_start(4)
    arrived(weight_sib[1])
    att_copy.wait_recv()

    group = block // 2

    def rows_of(ref, g):
        return jnp.concatenate(
            [ref[b * block + g * group : b * block + (g + 1) * group] for b in range(4)], axis=0
        )

    def rows_of_pair(ref, g):
        return jnp.concatenate(
            [
                ref[b // 2, (b % 2) * block + g * group : (b % 2) * block + (g + 1) * group]
                for b in range(4)
            ],
            axis=0,
        )

    def spread_part(k, g, part, side):
        for p in range(nz // 2):
            value = part(g, side * (nz // 2) + p).astype(half)
            for b in range(4):
                srs[k, g, b // 2, b % 2, side, :, p * dz : (p + 1) * dz] = value[
                    b * group : (b + 1) * group
                ]

    def spread_send(k, g, side):
        if side:
            return [
                send(srs.at[k, g, 1 - x, 1 - y, 1], rrs.at[k, g, 1], ynb),
                send(srs.at[k, g, x, 1 - y, 1], rrs.at[k, g, 5], ynb),
            ]
        return [
            send(srs.at[k, g, 1 - x, 1 - y, 0], rrs.at[k, g, 0], xnb),
            send(srs.at[k, g, 1 - x, y, 0], rrs.at[k, g, 2], xnb),
        ]

    def spread_pass(k, g, copies):
        copies[0].wait_recv()
        srs[k, g, x, 1 - y, 0] = (
            srs[k, g, x, 1 - y, 0].astype(single) + rrs[k, g, 0].astype(single)
        ).astype(half)
        last = [send(srs.at[k, g, x, 1 - y, 0], rrs.at[k, g, 4], ynb)]
        copies[2].wait_recv()
        srs[k, g, 1 - x, y, 1] = (
            srs[k, g, 1 - x, y, 1].astype(single) + rrs[k, g, 1].astype(single)
        ).astype(half)
        last.append(send(srs.at[k, g, 1 - x, y, 1], rrs.at[k, g, 3], xnb))
        return [copies[1], copies[3]] + last

    def spread_sum(k, g, part):
        copies = []
        for side in range(2):
            spread_part(k, g, part, side)
            copies += spread_send(k, g, side)
        return copies

    def summed(k, g, at):
        sides = [
            srs[k, g, x, y, side, at].astype(single)
            + rrs[k, g, 2 + side, at].astype(single)
            + rrs[k, g, 4 + side, at].astype(single)
            for side in range(2)
        ]
        return jnp.concatenate(sides, axis=1)

    def attention_out(g, piece):
        return dot_nn(rows_of_pair(ax, g), wo[piece])

    copies = [spread_sum(0, g, attention_out) for g in range(2)]
    copies = [spread_pass(0, g, copies[g]) for g in range(2)]
    dy_copy.wait_recv()
    dy_fwd = send(dyb.at[c, 1 - x], dyb.at[c, 1 - x], sib)
    line_pass(3, 1)
    line_pass(2, 2)

    my_x = xl.at[pl.ds(pl.multiple_of(c * quarter + y * block, block), block)]

    def middle_rows(g):
        def rows(r):
            at = pl.ds(pl.multiple_of(g * group + r, 32), 32)
            value = my_x[at].astype(single) + (summed(0, g, pl.ds(r, 32)) + out_bias)
            mid[at] = value
            centred, rate = norm_parts(value)
            ns[c, x, y, at] = (centred * rate * gain2 + shift2).astype(half)

        by_rows(group, 32, rows)

    def gather_rows(g, part):
        return pl.ds(g * group + part * (group // 2), group // 2)

    def gather(buf, g):
        mine = buf.at[c, x, y]
        first, last = mine.at[gather_rows(g, 0)], mine.at[gather_rows(g, 1)]
        all_rows = mine.at[pl.ds(g * group, group)]
        return [
            send(first, first, xnb),
            send(last, last, ynb),
            send(last, last, xnb),
            send(first, first, ynb),
            send(all_rows, all_rows, sib),
        ]

    def gather_pass(buf, g, copies):
        by_x = buf.at[c, 1 - x, y, gather_rows(g, 0)]
        by_y = buf.at[c, x, 1 - y, gather_rows(g, 1)]
        copies[0].wait_recv()
        through = [send(by_x, by_x, ynb)]
        copies[1].wait_recv()
        through.append(send(by_y, by_y, xnb))
        return through

    def gather_end(buf, g, copies, through):
        def on(bx, by):
            rows = buf.at[c, bx, by, pl.ds(g * group, group)]
            return send(rows, rows, sib)

        copies[3].wait_recv()
        to_sib = [copies[4], on(x, 1 - y)]
        copies[2].wait_recv()
        to_sib.append(on(1 - x, y))
        arrived(through)
        to_sib.append(on(1 - x, 1 - y))
        return to_sib

    def hidden(g):
        rows_ns = ns[c, :, :, g * group : (g + 1) * group].reshape(quarter, width)
        for h in range(2):
            wide[:, 0:fch] = dot_nn(rows_ns, wf[h].reshape(width, fch))

            def rows(r, h=h):
                value = wide[pl.ds(r, group), 0:fch] + fcb[h : h + 1]
                root = 0.7978845608028654
                square = value * value
                inner = jnp.tanh(root * (value + 0.044715 * (square * value)))
                lift = 0.5 * (1.0 + inner)
                at = pl.ds(pl.multiple_of(2 * r + g * group, group), group)
                act[c, h, at] = (value * lift).astype(half)
                slope[h, at] = lift + 0.5 * value * (1.0 - inner * inner) * (
                    root * (1.0 + 3.0 * 0.044715 * square)
                )

            by_rows(quarter, group, rows)

    def hidden_add(which, piece, there, first=False):
        part_at = slice((which - 3) * (fch // 2), (which - 2) * (fch // 2))
        at = pl.ds(pl.multiple_of(((piece + nz) % nz) * dz, dz), dz)

        def add():
            rows_dy = dyb[c, :, :, at].reshape(2 * quarter, dz)
            for h in range(2):
                part = dot_nt(rows_dy, wp[h, (piece + nz) % nz, part_at])
                if first:
                    gact[h, :, part_at] = part
                else:
                    gact[h, :, part_at] += part

        if there is None:
            add()
        else:
            pl.when(there)(add)

    def hidden_grad(g):
        def rows(r):
            at = pl.ds(pl.multiple_of(2 * r + g * group, group), group)
            for h in range(2):
                gp[c, h, at] = (gact[h, at] * slope[h, at]).astype(half)

        by_rows(quarter, group, rows)

    ns_copies = []
    for g in range(2):
        arrived(copies[g])
        middle_rows(g)
        ns_copies.append(gather(ns, g))
    line_pass(4, 1)
    line_pass(3, 2)
    through = [gather_pass(ns, g, ns_copies[g]) for g in range(2)]
    dy_fwd.wait_recv()
    for which in (3, 4):
        weight_sib[which].pop(0).wait_recv()
        hidden_add(which, z, None, first=True)
        arrived(weight_sib[which])
        weight_sib[which] = []
        hidden_add(which, z - 1, z >= 1)
        hidden_add(which, z + 1, z < nz - 1)
        if which == 3:
            hidden_add(which, z - 2, z >= 2)
            hidden_add(which, z + 2, z + 2 < nz)
    line_pass(4, 2)
    ns_sib = gather_end(ns, 0, ns_copies[0], through[0])
    for step in range(3, nz):
        line_pass(2, step)
    arrived(weight_sib[2])

    hidden(0)
    ns_sib += gather_end(ns, 1, ns_copies[1], through[1])
    hidden(1)
    act_copy = send(act.at[c, 1 - c], act.at[c, 1 - c], sib)

    def weight_grad(left, right_at, out):
        def one(step, carry):
            piece = (z + step) % nz
            at = pl.ds(pl.multiple_of(piece * dz, dz), dz)
            out[piece] = dot_nn(turned[0:left], right_at(at)).astype(half)
            return carry

        lax.fori_loop(0, nz, one, 0)

    def direct_sum(out, home):
        return [
            send(out.at[(z + step) % nz], home.at[z], zdev(step)) for step in range(1, nz)
        ]

    def line_sum(out, home, merged):
        up2, down2 = out.at[(z + 2) % nz], out.at[(z + nz - 2) % nz]
        up1, down1 = out.at[(z + 1) % nz], out.at[(z + nz - 1) % nz]
        far_up = send_if(out.at[nz - 1], merged, right, z == 0, z == 1)
        far_down = send_if(out.at[0], merged, left, z == nz - 1, z == nz - 2)
        two_up = send_if(up2, home.at[z], zdev(2), z + 2 < nz, z >= 2, start=False)
        two_down = send_if(down2, home.at[z], zdev(nz - 2), z >= 2, z + 2 < nz, start=False)
        pl.when(z == 0)(two_up.start)
        pl.when(z == nz - 1)(two_down.start)
        one_up = send_if(up1, home.at[z], right, z < nz - 1, z >= 1)
        one_down = send_if(down1, home.at[z], left, z >= 1, z < nz - 1)
        return out, home, merged, far_up, far_down, two_up, two_down, one_up, one_down

    def line_add(line):
        out, home, merged, far_up, far_down, two_up, two_down, _, _ = line

        @pl.when(z == 1)
        def _():
            far_up.copy.wait_recv()
            out[nz - 1] = (out[nz - 1].astype(single) + merged[...].astype(single)).astype(half)
            two_up.start()

        @pl.when(z == nz - 2)
        def _():
            far_down.copy.wait_recv()
            out[0] = (out[0].astype(single) + merged[...].astype(single)).astype(half)
            two_down.start()

    def line_end(line):
        out, home, _, _, _, two_up, two_down, one_up, one_down = line
        total = accum.at[0 : out.shape[1]]
        total[...] = out[z].astype(single)
        for copy, source, there in (
            (one_up, z - 1, z >= 1),
            (one_down, z + 1, z < nz - 1),
            (two_up, z - 2, z >= 2),
            (two_down, z + 2, z + 2 < nz),
        ):

            def take(copy=copy, source=source):
                copy.copy.wait_recv()
                total[...] += home[(source + nz) % nz].astype(single)

            pl.when(there)(take)
        return total[...]

    def turn_rows(src, left, column):
        turned[0:left, pl.ds(pl.multiple_of(column, quarter), quarter)] = src.T

    act_copy.wait_recv()
    for s in range(2):
        for k in range(2):
            turn_rows(act[s, c, k * quarter : (k + 1) * quarter], fch, (s * 2 + k) * quarter)
    weight_grad(fch, lambda at: dyb[:, :, :, at].reshape(length, dz), gsp)
    proj_z = line_sum(gsp, grp, glp)
    arrived(weight_sib[4])
    weight_sib[4] = []
    hidden_add(4, z - 2, z >= 2)
    hidden_add(4, z + 2, z + 2 < nz)
    for which in (3, 4):
        line_pass(which, 3)
        arrived(weight_sib[which])
        hidden_add(which, z - 3, z >= 3)
        hidden_add(which, z + 3, z + 3 < nz)

    def norm2_part(g, piece):
        return dot_nt(rows_of(gp.at[c, 0], g), wf[0, piece]) + dot_nt(
            rows_of(gp.at[c, 1], g), wf[1, piece]
        )

    hidden_grad(0)
    copies = [spread_sum(1, 0, norm2_part)]
    hidden_grad(1)
    gp_copy = send(gp.at[c, 1 - c], gp.at[c, 1 - c], sib)
    copies.append(spread_sum(1, 1, norm2_part))
    copies[0] = spread_pass(1, 0, copies[0])
    copies[1] = spread_pass(1, 1, copies[1])
    line_add(proj_z)

    sv[...] = jnp.zeros_like(sv)
    late[...] = jnp.zeros_like(late)
    my_dy = dyb.at[c, x, pl.ds(pl.multiple_of(y * block, block), block)]

    def middle_back(g):
        def rows(r):
            at = pl.ds(pl.multiple_of(g * group + r, 32), 32)
            grad_rows = my_dy[at].astype(single)
            by_value, gain_part, shift_part = norm_back(
                mid[at], summed(1, g, pl.ds(r, 32)), gain2
            )
            grad = grad_rows + by_value
            gmid[at] = grad
            low = grad.astype(half)
            gm[c, x, y, at] = low
            sv[3:4] += gain_part
            sv[4:5] += shift_part
            sv[0:1] += jnp.sum(low.astype(single), axis=0, keepdims=True)
            sv[5:6] += jnp.sum(grad_rows, axis=0, keepdims=True)

        by_rows(group, 32, rows)

    gm_copies = []
    for g in range(2):
        arrived(copies[g])
        middle_back(g)
        gm_copies.append(gather(gm, g))

    def feed_part(g, piece):
        return dot_nn(rows_of(act.at[c, 0], g), wp[0, piece]) + dot_nn(
            rows_of(act.at[c, 1], g), wp[1, piece]
        )

    gp_copy.wait_recv()
    arrived(ns_sib)
    for s in range(2):
        for k in range(2):
            turn_rows(gp[s, c, k * quarter : (k + 1) * quarter], fch, (s * 2 + k) * quarter)
    weight_grad(fch, lambda at: ns[:, :, :, :, at].reshape(length, dz), gsf)
    fc_z = line_sum(gsf, grf, glf)
    through = [gather_pass(gm, 0, gm_copies[0])]
    for side in range(2):
        spread_part(2, 0, feed_part, side)
    through.append(gather_pass(gm, 1, gm_copies[1]))
    for side in range(2):
        spread_part(2, 1, feed_part, side)
    feed_copies = [spread_send(2, g, 0) + spread_send(2, g, 1) for g in range(2)]
    for s in range(2):
        sv[6:7, 0:fch] += jnp.sum(gp[s, c].astype(single), axis=0, keepdims=True)
    my_place = x * 4 + t
    for piece in range(nz):
        for row, source in enumerate((0, 3, 4, 5)):
            s2[piece, row : row + 1] = sv[source : source + 1, piece * dz : (piece + 1) * dz]
        for k in range(pieces):
            s2[piece, 4 + k : 5 + k] = sv[6:7, k * dz : (k + 1) * dz]
        s2[piece, 4 + pieces : 8] = jnp.zeros((4 - pieces, dz), single)

    def over_planes(lines, home):
        home[z] = lines[z]
        return [
            send(lines.at[(z + step) % nz], home.at[z], zdev(step)) for step in range(1, nz)
        ]

    def over_plane(home, places):
        value = home[0]
        for piece in range(1, nz):
            value = value + home[piece]
        places[my_place] = value
        return [
            send(places.at[my_place], places.at[my_place], dev) for dev in peers[0:7]
        ]

    def place_sum(places):
        value = places[0]
        for place in range(1, 8):
            value = value + places[place]
        return value

    def grad_attended(g):
        rows_gm = gm[c, :, :, g * group : (g + 1) * group].reshape(quarter, width)
        total = None
        for piece in range(nz):
            part = dot_nt(rows_gm[:, piece * dz : (piece + 1) * dz], wo[piece])
            total = part if total is None else total + part
        for h in range(2):
            for b in range(4):
                gtt[h, b, g] = total[b * group : (b + 1) * group, h * ec : (h + 1) * ec].astype(
                    half
                )
        gt[c, :, g] = gtt[c, :, g]
        return send(gtt.at[1 - c, :, g], gt.at[c, :, g], sib)

    gm_sib, gt_copies = [], []
    for g in range(2):
        gm_sib += gather_end(gm, g, gm_copies[g], through[g])
        gt_copies.append(grad_attended(g))
    arrived(gm_sib)
    for s in range(2):
        for k in range(2):
            turn_rows(ao[k, s], ec, (s * 2 + k) * quarter)
    weight_grad(ec, lambda at: gm[:, :, :, :, at].reshape(length, dz), gso)
    out_z = direct_sum(gso, gro)
    arrived(gt_copies)
    s2_copies = over_planes(s2, s2r)
    my_rows = pl.multiple_of(c * quarter + y * block, block)

    def out_rows(g):
        def rows(r):
            at = pl.ds(pl.multiple_of(g * group + r, 32), 32)
            value = mid[at] + (summed(2, g, pl.ds(r, 32)) + proj_bias)
            outv[pl.ds(pl.multiple_of(my_rows + g * group + r, 32), 32)] = value.astype(half)

        by_rows(group, 32, rows)


    def half_send(buf, k):
        rows = buf.shape[1] // 2
        part = buf.at[x, k * rows : (k + 1) * rows]
        return send(part, part, xnb)

    dkb[...] = jnp.zeros_like(dkb)
    dvb[...] = jnp.zeros_like(dvb)
    for i in range(n_blocks):
        j0 = max(0, i - 2)
        span = (i + 1 - j0) * quarter
        keys = pl.ds(j0 * quarter, span)
        grads = (wide, wide_b)
        rows_gt = gt[i % 2, (i // 2) * 2 : (i // 2) * 2 + 2].reshape(quarter, ec)
        ga = [only(rows_gt, h) for h in range(heads)]
        for h in range(heads):
            grads[h][:, 0:span] = dot_nt(ga[h], vb[keys])

        def back(r, i=i, span=span):
            for h in range(heads):
                grad_p = grads[h][pl.ds(r, 64), 0:span]
                share = probs[i][h, pl.ds(r, 64)].astype(single)
                delta = jnp.sum(grad_p * share, axis=-1, keepdims=True)
                dsb[h, pl.ds(r, 64), 0:span] = (share * (grad_p - delta)).astype(half)

        by_rows(quarter, 64, back)
        total = None
        for h in range(heads):
            grad_s = dsb[h, :, 0:span]
            part = dot_nn(grad_s, only(kb[keys], h))
            total = part if total is None else total + part
            dkb[keys] += dot_nn(grad_s.T, only(qb[pl.ds(i * quarter, quarter)], h))
            dvb[keys] += dot_nn(probs[i][h].T, ga[h])
        dqkv[i // 2, i % 2, :, 0:ec] = (total * HD**-0.5).astype(half)
        if i == 0:
            xp_[x] = line_end(proj_z).astype(half)
            proj_x = [half_send(xp_, 0)]
        if i == 1:
            feed_copies = [spread_pass(2, g, feed_copies[g]) for g in range(2)]
        if i == 2:
            line_add(fc_z)
    for i in range(n_blocks):
        at = pl.ds(i * quarter, quarter)
        dqkv[i // 2, i % 2, :, ec : 2 * ec] = (dkb[at] * HD**-0.5).astype(half)
        dqkv[i // 2, i % 2, :, 2 * ec :] = dvb[at].astype(half)

    my_dx = pl.ds(pl.multiple_of(c * 3 * ec, ec), 3 * ec)
    dx_copy = send(dqkv.at[:, 1 - c], dx.at[:, :, my_dx], sib)
    dx[:, :, my_dx] = dqkv[:, c]
    for i in range(n_blocks):
        turn_rows(dqkv[i // 2, i % 2], 3 * ec, i * quarter)
    weight_grad(3 * ec, lambda at: nf[:, :, :, at].reshape(length, dz), gsq)
    qkv_z = line_sum(gsq, grq, glq)
    arrived(weight_sib[0])
    dx_copy.wait_recv()

    def norm1_part(g, piece):
        return dot_nt(rows_of_pair(dx, g), wq[piece])

    copies = [spread_sum(3, g, norm1_part) for g in range(2)]
    copies[0] = spread_pass(3, 0, copies[0])
    line_add(qkv_z)
    copies[1] = spread_pass(3, 1, copies[1])
    proj_x.append(half_send(xp_, 1))
    for g in range(2):
        arrived(feed_copies[g])
        out_rows(g)
    mine = outv.at[pl.ds(my_rows, block)]
    theirs = outv.at[pl.ds(pl.multiple_of(c * quarter + (1 - y) * block, block), block)]
    out_s = [send(mine, mine, sib)]

    xf[x] = line_end(fc_z).T.astype(half)
    fc_x = send(xf.at[x], xf.at[x], xnb)
    arrived(out_z)
    value = gso[z].astype(single)
    for step in range(1, nz):
        value = value + gro[(z + step) % nz].astype(single)
    xo[x] = value.astype(half)
    out_x = send(xo.at[x], xo.at[x], xnb)
    arrived(s2_copies)
    sv_copies = over_plane(s2r, svall)

    for k, first in enumerate((0, 2 * ec)):
        bqline[:, k * ec : (k + 1) * ec] = jnp.sum(
            dqkv[:, :, :, first : first + ec].astype(single).reshape(length, ec),
            axis=0,
            keepdims=True,
        )

    def first_back(g):
        def rows(r):
            at = pl.ds(pl.multiple_of(g * group + r, 32), 32)
            by_value, gain_part, shift_part = norm_back(
                my_x[at].astype(single), summed(3, g, pl.ds(r, 32)), gain1
            )
            gradv[pl.ds(pl.multiple_of(my_rows + g * group + r, 32), 32)] = (
                gmid[at] + by_value
            ).astype(half)
            late[0:1] += gain_part
            late[1:2] += shift_part

        by_rows(group, 32, rows)

    def grad_rows_at(by, g):
        start = pl.multiple_of(c * quarter + by * block + g * group, group)
        return gradv.at[pl.ds(start, group)]

    grad_copies = []
    for g in range(2):
        arrived(copies[g])
        first_back(g)
        if g:
            for piece in range(nz):
                l2[piece, 0:2] = late[:, piece * dz : (piece + 1) * dz]
                l2[piece, 2:3] = bqline[...]
                l2[piece, 3:8] = jnp.zeros((5, dz), single)
            l2_copies = over_planes(l2, l2r)
        rows = grad_rows_at(y, g)
        grad_copies += [send(rows, rows, ynb), send(rows, rows, sib)]
    out_y = send(mine, mine, ynb)

    xq[x] = line_end(qkv_z).T.astype(half)
    qkv_x = send(xq.at[x], xq.at[x], xnb)
    arrived(l2_copies)
    late_copies = over_plane(l2r, lateall)
    arrived(proj_x)
    final = [fetch(xp_, gproj_hbm)]
    grad_s_ = [grad_copies[1], grad_copies[3]]
    for g in range(2):
        grad_copies[2 * g].wait_recv()
        rows = grad_rows_at(1 - y, g)
        grad_s_.append(send(rows, rows, sib))
    arrived([fc_x])
    final.append(fetch(xf, gfc_hbm))
    arrived([out_x])
    final.append(fetch(xo, gout_hbm))
    arrived(grad_s_)
    final.append(fetch(gradv, grad_hbm))
    out_y.wait_recv()
    out_s.append(send(theirs, theirs, sib))
    arrived(sv_copies)
    arrived(late_copies)
    early_sum, late_sum = place_sum(svall), place_sum(lateall)
    source = (z // pieces) * 4 + t
    bfc_lines = svall[source, 4 : 4 + pieces]
    gvec_ref[0:1] = early_sum[0:1]
    gvec_ref[1:3] = late_sum[0:2]
    gvec_ref[3:6] = early_sum[1:4]
    gvec_ref[6:7] = jnp.where(z % pieces == 0, bfc_lines[0:1], bfc_lines[1:2])
    q_line, v_line = lateall[source, 2:3, 0:ec], lateall[source, 2:3, ec : 2 * ec]
    even = jnp.where(low_lane, q_line, pltpu.roll(v_line, HD, 1))
    odd = jnp.where(low_lane, pltpu.roll(q_line, HD, 1), v_line)
    gvec_ref[7:8, 0:ec] = jnp.where(z % pieces == 0, even, odd)
    gvec_ref[7:8, ec:dz] = jnp.zeros((1, dz - ec), single)
    arrived([qkv_x])
    final.append(fetch(xq, gqkv_hbm))
    arrived(out_s)
    final.append(fetch(outv, out_hbm))
    for copy in final:
        copy.wait()
    for copy in started:
        copy.wait_send()


def finish_kernel(
    out,
    grad,
    gqkv,
    gout,
    gfc,
    gproj,
    gvec,
    out_ref,
    grad_ref,
    gqkv_ref,
    gout_ref,
    gfc_ref,
    gproj_ref,
    gqv_ref,
    *line_refs,
):
    single = jnp.float32
    out_ref[...] = out[...]
    grad_ref[...] = grad[...]
    ec = gqkv_ref.shape[2]
    for j in range(3):
        gqkv_ref[j] = gqkv[0, :, j * ec : (j + 1) * ec].astype(single)
    gout_ref[...] = gout[0].astype(single)
    gfc_ref[...] = gfc[0].astype(single)
    gproj_ref[...] = gproj[0].astype(single)
    pair = gqv_ref.shape[1]
    gqv_ref[0:1] = gvec[7:8, 0:pair]
    gqv_ref[1:2] = gvec[7:8, pair : 2 * pair]
    for row, ref in enumerate(line_refs):
        ref[...] = gvec[row : row + 1]


def plane_block(
    nz,
    block_input,
    segment_ids,
    cotangent,
    qkv_weight,
    qv_bias,
    out_weight,
    out_bias,
    norm1_gain,
    norm1_shift,
    fc_weight,
    fc_bias,
    proj_weight,
    proj_bias,
    norm2_gain,
    norm2_shift,
):
    half = jnp.bfloat16
    single = jnp.float32
    _, rows, width = block_input.shape
    length = segment_ids.shape[1]
    dz = qkv_weight.shape[0]
    ec = qkv_weight.shape[2] // 2
    fch = fc_weight.shape[1] // 2
    quarter, block = rows // 2, rows // 4
    vmem = pltpu.VMEM
    spans = [(i + 1 - max(0, i - 2)) * quarter for i in range(4)]
    heads = ec // HD
    scratch = [
        vmem((dz, 3 * ec), single),
        vmem((ec, dz), single),
        vmem((dz, fch), single),
        vmem((fch, dz), single),
        vmem((rows, width), half),
        vmem((2, quarter, width), half),
        vmem((2, 2, quarter, width), half),
        vmem((2, 2, quarter, width), half),
        vmem((nz, dz, 6 * ec), half),
        vmem((nz, 2 * ec, dz), half),
        vmem((2, nz, dz, fch), half),
        vmem((2, nz, fch, dz), half),
        vmem((2, nz, 8, dz), single),
        vmem((8, width), single),
        vmem((2, fch), single),
        vmem((length, ec), half),
        vmem((length, ec), half),
        vmem((length, ec), half),
    ]
    scratch += [vmem((heads, quarter, span), half) for span in spans]
    scratch += [
        vmem((length, 128), single),
        vmem((2, 2, quarter, ec), half),
        vmem((2, quarter, 2 * ec), half),
        vmem((4, 2, 2, 2, 2, block // 2, width // 2), half),
        vmem((4, 2, 6, block // 2, width // 2), half),
        vmem((block, width), single),
        vmem((2, 2, 2, block, width), half),
        vmem((2, 2, 2, block, width), half),
        vmem((2, 2, rows, fch), half),
        vmem((2, 2, rows, fch), half),
        vmem((fch, length), half),
    ]
    for _ in range(2):
        scratch += [
            vmem((nz, 3 * ec, dz), half),
            vmem((nz, ec, dz), half),
            vmem((nz, fch, dz), half),
            vmem((nz, fch, dz), half),
        ]
    scratch += [
        vmem((3 * ec, dz), half),
        vmem((fch, dz), half),
        vmem((fch, dz), half),
        vmem((fch, dz), single),
        vmem((2, dz, 3 * ec), half),
        vmem((2, ec, dz), half),
        vmem((2, dz, fch), half),
        vmem((2, fch, dz), half),
        vmem((2, 4, 2, block // 2, ec), half),
        vmem((2, 4, 2, block // 2, ec), half),
        vmem((length, ec), single),
        vmem((length, ec), single),
        vmem((2, 2, quarter, 3 * ec), half),
        vmem((2, quarter, 6 * ec), half),
        vmem((quarter, 3 * quarter), single),
        vmem((quarter, 3 * quarter), single),
        vmem((2, rows, fch), single),
        vmem((2, rows, fch), single),
        vmem((2, quarter, 3 * quarter), half),
        vmem((rows, width), half),
        vmem((rows, width), half),
        vmem((block, width), single),
        vmem((8, width), single),
        vmem((8, 8, dz), single),
        vmem((2, width), single),
        vmem((8, 8, dz), single),
        vmem((1, dz), single),
        vmem((nz, 8, dz), single),
        vmem((nz, 8, dz), single),
        vmem((nz, 8, dz), single),
        vmem((nz, 8, dz), single),
        pltpu.SemaphoreType.DMA((300,)),
        pltpu.SemaphoreType.DMA((300,)),
        pltpu.SemaphoreType.DMA((20,)),
    ]
    whole = pl.BlockSpec(memory_space=pltpu.VMEM)
    there = pl.BlockSpec(memory_space=pl.ANY)
    middle = pl.pallas_call(
        functools.partial(block_kernel, nz),
        out_shape=(
            jax.ShapeDtypeStruct((rows, width), half),
            jax.ShapeDtypeStruct((rows, width), half),
            jax.ShapeDtypeStruct((2, dz, 3 * ec), half),
            jax.ShapeDtypeStruct((2, ec, dz), half),
            jax.ShapeDtypeStruct((2, dz, fch), half),
            jax.ShapeDtypeStruct((2, fch, dz), half),
            jax.ShapeDtypeStruct((8, dz), single),
        ),
        in_specs=[there] * 2 + [whole] + [there] * 4 + [whole] * 8,
        out_specs=(there,) * 6 + (whole,),
        scratch_shapes=scratch,
        compiler_params=pltpu.CompilerParams(
            collective_id=0, has_side_effects=True, vmem_limit_bytes=67043328
        ),
        name="residual_block",
    )(
        block_input.reshape(rows, width),
        cotangent.reshape(rows, width),
        segment_ids,
        qkv_weight.transpose(1, 0, 2),
        out_weight,
        fc_weight,
        proj_weight,
        out_bias.reshape(1, dz),
        norm1_gain.reshape(1, dz),
        norm1_shift.reshape(1, dz),
        norm2_gain.reshape(1, dz),
        norm2_shift.reshape(1, dz),
        proj_bias.reshape(1, dz),
        fc_bias.reshape(1, dz),
        qv_bias,
    )

    def halves(shape, axis):
        return pl.BlockSpec(
            shape, lambda side: tuple(side if k == axis else 0 for k in range(len(shape)))
        )

    line = pl.BlockSpec((1, dz), lambda side: (0, 0))
    outs = pl.pallas_call(
        finish_kernel,
        grid=(2,),
        out_shape=(
            jax.ShapeDtypeStruct((rows, width), half),
            jax.ShapeDtypeStruct((rows, width), half),
            jax.ShapeDtypeStruct((3, dz, 2 * ec), single),
            jax.ShapeDtypeStruct((2 * ec, dz), single),
            jax.ShapeDtypeStruct((dz, 2 * fch), single),
            jax.ShapeDtypeStruct((2 * fch, dz), single),
            jax.ShapeDtypeStruct(qv_bias.shape, single),
        )
        + (jax.ShapeDtypeStruct((1, dz), single),) * 7,
        in_specs=[
            halves((quarter, width), 0),
            halves((quarter, width), 0),
            halves((1, dz, 3 * ec), 0),
            halves((1, ec, dz), 0),
            halves((1, dz, fch), 0),
            halves((1, fch, dz), 0),
            pl.BlockSpec((8, dz), lambda side: (0, 0)),
        ],
        out_specs=(
            halves((quarter, width), 0),
            halves((quarter, width), 0),
            halves((3, dz, ec), 2),
            halves((ec, dz), 0),
            halves((dz, fch), 1),
            halves((fch, dz), 0),
            pl.BlockSpec(qv_bias.shape, lambda side: (0, 0)),
        )
        + (line,) * 7,
        name="finish",
    )(*middle)
    out, grad, gqkv, gout, gfc, gproj, gqv = outs[:7]
    gbout, ggain1, gshift1, ggain2, gshift2, gbproj, gbfc = [
        value.reshape(dz) for value in outs[7:]
    ]
    return (
        out.reshape(block_input.shape),
        grad.reshape(block_input.shape),
        gqkv.transpose(1, 0, 2),
        gqv,
        gout,
        gbout,
        ggain1,
        gshift1,
        gfc,
        gbfc,
        gproj,
        gbproj,
        ggain2,
        gshift2,
    )


def device_program(mesh):
    planes = mesh.shape["fsdp"]

    def program(block_input, *others):
        seqs_here, rows, width = block_input.shape
        one_kernel = (
            seqs_here == 1
            and mesh.shape["ctx"] == 2
            and mesh.shape["tp"] == 4
            and planes == 4
            and width // planes == 256
        )
        if one_kernel:
            return plane_block(planes, block_input, *others)
        return on_device(block_input, *others)

    return program


def solution(mesh):
    return jax.shard_map(
        device_program(mesh),
        mesh=mesh,
        in_specs=(
            P("fsdp", "ctx", None),
            P("fsdp", None),
            P("fsdp", "ctx", None),
            P("fsdp", None, "tp"),
            P(None, ("tp", "fsdp")),
            P("tp", "fsdp"),
            P("fsdp"),
            P("fsdp"),
            P("fsdp"),
            P("fsdp", "tp"),
            P(("tp", "fsdp")),
            P("tp", "fsdp"),
            P("fsdp"),
            P("fsdp"),
            P("fsdp"),
        ),
        out_specs=(
            P("fsdp", "ctx", None),
            P("fsdp", "ctx", None),
            P("fsdp", None, "tp"),
            P(None, ("tp", "fsdp")),
            P("tp", "fsdp"),
            P("fsdp"),
            P("fsdp"),
            P("fsdp"),
            P("fsdp", "tp"),
            P(("tp", "fsdp")),
            P("tp", "fsdp"),
            P("fsdp"),
            P("fsdp"),
            P("fsdp"),
        ),
        check_vma=False,
    )
```

```python
import functools

import jax
import jax.numpy as jnp
from jax import lax
from jax.experimental import pallas as pl
from jax.experimental.pallas import tpu as pltpu
from jax.sharding import PartitionSpec as P

HD = 64


epsilon = 1e-05


def layer_norm(values, gain, shift):
    centred = values - jnp.mean(values, axis=-1, keepdims=True)
    spread = jnp.mean(centred * centred, axis=-1, keepdims=True)
    return centred * lax.rsqrt(spread + epsilon) * gain + shift


def gelu_act(values):
    return jax.nn.gelu(values, approximate=True)


def on_device(
    block_input,
    segment_ids,
    cotangent,
    qkv_weight,
    qv_bias,
    out_weight,
    out_bias,
    norm1_gain,
    norm1_shift,
    fc_weight,
    fc_bias,
    proj_weight,
    proj_bias,
    norm2_gain,
    norm2_shift,
):
    half = jnp.bfloat16
    single = jnp.float32
    seqs_here, rows_seq, model_width = block_input.shape
    row_count = seqs_here * rows_seq
    shard_index = lax.axis_index("ctx")
    scale_factor = HD ** (-0.5)
    (
        wqkv_low,
        bqv_low,
        wout_low,
        bout_low,
        gain1_low,
        shift1_low,
        wfc_low,
        bfc_low,
        wproj_low,
        bproj_low,
        gain2_low,
        shift2_low,
    ) = (
        lax.all_gather(qkv_weight.astype(half), "fsdp", axis=0, tiled=True),
        lax.all_gather(qv_bias.astype(half), "fsdp", axis=1, tiled=True),
        lax.all_gather(out_weight.astype(half), "fsdp", axis=1, tiled=True),
        lax.all_gather(out_bias.astype(half), "fsdp", axis=0, tiled=True),
        lax.all_gather(norm1_gain.astype(half), "fsdp", axis=0, tiled=True),
        lax.all_gather(norm1_shift.astype(half), "fsdp", axis=0, tiled=True),
        lax.all_gather(fc_weight.astype(half), "fsdp", axis=0, tiled=True),
        lax.all_gather(fc_bias.astype(half), "fsdp", axis=0, tiled=True),
        lax.all_gather(proj_weight.astype(half), "fsdp", axis=1, tiled=True),
        lax.all_gather(proj_bias.astype(half), "fsdp", axis=0, tiled=True),
        lax.all_gather(norm2_gain.astype(half), "fsdp", axis=0, tiled=True),
        lax.all_gather(norm2_shift.astype(half), "fsdp", axis=0, tiled=True),
    )
    gain_first = gain1_low.astype(single)
    shift_first = shift1_low.astype(single)
    gain_second = gain2_low.astype(single)
    shift_second = shift2_low.astype(single)
    inputs = block_input.reshape(row_count, model_width).astype(single)
    normed_first = layer_norm(inputs, gain_first, shift_first).astype(half)
    projected = jnp.einsum("rd,dce->rce", normed_first, wqkv_low, preferred_element_type=single)
    bias_pair = bqv_low.astype(single)
    queries = (projected[:, 0] + bias_pair[0]).astype(half)
    key_rows = projected[:, 1].astype(half)
    value_rows = (projected[:, 2] + bias_pair[1]).astype(half)
    local_width = queries.shape[1]
    head_count = local_width // HD
    keys_all, values_all = (
        lax.all_gather(
            key_rows.reshape(seqs_here, rows_seq, local_width), "ctx", axis=1, tiled=True
        ),
        lax.all_gather(
            value_rows.reshape(seqs_here, rows_seq, local_width), "ctx", axis=1, tiled=True
        ),
    )
    length = keys_all.shape[1]
    query_pos = shard_index * rows_seq + jnp.arange(rows_seq)
    key_pos = jnp.arange(length)
    seg_query = lax.dynamic_slice_in_dim(segment_ids, shard_index * rows_seq, rows_seq, 1)
    query_heads = queries.reshape(seqs_here, rows_seq, head_count, HD)
    key_heads = keys_all.reshape(seqs_here, length, head_count, HD)
    value_heads = values_all.reshape(seqs_here, length, head_count, HD)

    def masked_scores(query_blk, key_blk, seg_row, seg_here):
        raw = (
            jnp.einsum("qhe,khe->hqk", query_blk, key_blk, preferred_element_type=single)
            * scale_factor
        )
        allowed = (key_pos[None, :] <= query_pos[:, None]) & (seg_here[:, None] == seg_row[None, :])
        return jnp.where(allowed[None], raw, -1e30)

    def attend(packed):
        query_blk, key_blk, value_blk, seg_row, seg_here = packed
        masked = masked_scores(query_blk, key_blk, seg_row, seg_here)
        row_max = jnp.max(masked, axis=-1, keepdims=True)
        expo = jnp.exp(masked - row_max)
        row_total = jnp.sum(expo, axis=-1, keepdims=True)
        probs_low = (expo / row_total).astype(half)
        attended = jnp.einsum("hqk,khe->qhe", probs_low, value_blk, preferred_element_type=single)
        return (attended.astype(half), row_max + jnp.log(row_total))

    attended, log_total = lax.map(
        attend, (query_heads, key_heads, value_heads, segment_ids, seg_query)
    )
    attended_rows = attended.reshape(row_count, local_width)
    attn_partial = jnp.dot(attended_rows, wout_low, preferred_element_type=single)
    attn_total = lax.psum(attn_partial.astype(jnp.bfloat16), "tp").astype(jnp.float32)
    middle = inputs + attn_total + bout_low.astype(single)
    normed_second = layer_norm(middle, gain_second, shift_second).astype(half)
    pre_act = jnp.dot(normed_second, wfc_low, preferred_element_type=single) + bfc_low.astype(
        single
    )
    act_low = gelu_act(pre_act).astype(half)
    mlp_total = lax.psum(
        jnp.dot(act_low, wproj_low, preferred_element_type=single).astype(jnp.bfloat16), "tp"
    ).astype(jnp.float32)
    out_rows = (middle + mlp_total + bproj_low.astype(single)).astype(half)
    wqkv_use, wout_use, wfc_use, wproj_use = (
        lax.all_gather(qkv_weight.astype(half), "fsdp", axis=0, tiled=True),
        lax.all_gather(out_weight.astype(half), "fsdp", axis=1, tiled=True),
        lax.all_gather(fc_weight.astype(half), "fsdp", axis=0, tiled=True),
        lax.all_gather(proj_weight.astype(half), "fsdp", axis=1, tiled=True),
    )
    grad_out = cotangent.reshape(row_count, model_width).astype(single)
    grad_out_low = cotangent.reshape(row_count, model_width)
    grad_bproj = jnp.sum(grad_out_low, axis=0, dtype=single)
    grad_wproj = jnp.einsum("rf,rd->fd", act_low, grad_out_low, preferred_element_type=single)
    grad_act = jnp.einsum("rd,fd->rf", grad_out_low, wproj_use, preferred_element_type=single)
    gelu_unused, gelu_pull = jax.vjp(gelu_act, pre_act)
    grad_pre = gelu_pull(grad_act)[0].astype(half)
    grad_bfc = jnp.sum(grad_pre, axis=0, dtype=single)
    grad_wfc = jnp.einsum("rd,rf->df", normed_second, grad_pre, preferred_element_type=single)
    norm2_partial = jnp.einsum("rf,df->rd", grad_pre, wfc_use, preferred_element_type=single)
    grad_norm2 = lax.psum(norm2_partial.astype(jnp.bfloat16), "tp").astype(jnp.float32)
    norm_unused, second_pull = jax.vjp(layer_norm, middle, gain_second, shift_second)
    grad_mid_ln, grad_gain2, grad_shift2 = second_pull(grad_norm2)
    grad_middle = grad_out + grad_mid_ln
    grad_mid_low = grad_middle.astype(half)
    grad_bout = jnp.sum(grad_mid_low, axis=0, dtype=single)
    grad_wout = jnp.einsum("rk,rd->kd", attended_rows, grad_mid_low, preferred_element_type=single)
    grad_att = jnp.einsum(
        "rd,kd->rk", grad_mid_low, wout_use, preferred_element_type=single
    ).astype(half)
    grad_att_heads = grad_att.reshape(seqs_here, rows_seq, head_count, HD)

    def attend_back(packed):
        query_blk, key_blk, value_blk, seg_row, seg_here, log_blk, grad_blk = packed
        masked = masked_scores(query_blk, key_blk, seg_row, seg_here)
        attn_probs = jnp.exp(masked - log_blk)
        probs_low = attn_probs.astype(half)
        grad_value = jnp.einsum("hqk,qhe->khe", probs_low, grad_blk, preferred_element_type=single)
        grad_probs = jnp.einsum("qhe,khe->hqk", grad_blk, value_blk, preferred_element_type=single)
        row_delta = jnp.sum(grad_probs * attn_probs, axis=-1, keepdims=True)
        grad_scores = (attn_probs * (grad_probs - row_delta)).astype(half)
        grad_query = (
            jnp.einsum("hqk,khe->qhe", grad_scores, key_blk, preferred_element_type=single)
            * scale_factor
        )
        grad_key = (
            jnp.einsum("hqk,qhe->khe", grad_scores, query_blk, preferred_element_type=single)
            * scale_factor
        )
        return (grad_query.astype(half), grad_key, grad_value)

    grad_query, grad_key, grad_value = lax.map(
        attend_back,
        (query_heads, key_heads, value_heads, segment_ids, seg_query, log_total, grad_att_heads),
    )
    grad_key, grad_value = (
        lax.psum_scatter(
            grad_key.reshape(seqs_here, length, local_width).astype(jnp.bfloat16),
            "ctx",
            scatter_dimension=1,
            tiled=True,
        ).astype(jnp.float32),
        lax.psum_scatter(
            grad_value.reshape(seqs_here, length, local_width).astype(jnp.bfloat16),
            "ctx",
            scatter_dimension=1,
            tiled=True,
        ).astype(jnp.float32),
    )
    grad_query = grad_query.reshape(row_count, local_width)
    grad_key = grad_key.reshape(row_count, local_width).astype(half)
    grad_value = grad_value.reshape(row_count, local_width).astype(half)
    grad_qkv = jnp.stack([grad_query, grad_key, grad_value], axis=1)
    grad_bqv = jnp.stack(
        [jnp.sum(grad_query, axis=0, dtype=single), jnp.sum(grad_value, axis=0, dtype=single)]
    )
    grad_wqkv = jnp.einsum("rd,rce->dce", normed_first, grad_qkv, preferred_element_type=single)
    norm1_partial = jnp.einsum("rce,dce->rd", grad_qkv, wqkv_use, preferred_element_type=single)
    grad_norm1 = lax.psum(norm1_partial.astype(jnp.bfloat16), "tp").astype(jnp.float32)
    first_unused, first_pull = jax.vjp(layer_norm, inputs, gain_first, shift_first)
    grad_in_ln, grad_gain1, grad_shift1 = first_pull(grad_norm1)
    input_rows = (grad_middle + grad_in_ln).astype(half)
    block_output = out_rows.reshape(block_input.shape)
    input_grad = input_rows.reshape(block_input.shape)
    (
        sum_wqkv,
        sum_bqv,
        sum_wout,
        sum_bout,
        sum_gain1,
        sum_shift1,
        sum_wfc,
        sum_bfc,
        sum_wproj,
        sum_bproj,
        sum_gain2,
        sum_shift2,
    ) = (
        lax.psum_scatter(grad_wqkv, ("fsdp", "ctx"), scatter_dimension=0, tiled=True),
        lax.psum_scatter(grad_bqv, ("fsdp", "ctx"), scatter_dimension=1, tiled=True),
        lax.psum_scatter(grad_wout, ("fsdp", "ctx"), scatter_dimension=1, tiled=True),
        lax.psum_scatter(grad_bout, ("fsdp", "ctx"), scatter_dimension=0, tiled=True),
        lax.psum_scatter(grad_gain1, ("fsdp", "ctx"), scatter_dimension=0, tiled=True),
        lax.psum_scatter(grad_shift1, ("fsdp", "ctx"), scatter_dimension=0, tiled=True),
        lax.psum_scatter(grad_wfc, ("fsdp", "ctx"), scatter_dimension=0, tiled=True),
        lax.psum_scatter(grad_bfc, ("fsdp", "ctx"), scatter_dimension=0, tiled=True),
        lax.psum_scatter(grad_wproj, ("fsdp", "ctx"), scatter_dimension=1, tiled=True),
        lax.psum_scatter(grad_bproj, ("fsdp", "ctx"), scatter_dimension=0, tiled=True),
        lax.psum_scatter(grad_gain2, ("fsdp", "ctx"), scatter_dimension=0, tiled=True),
        lax.psum_scatter(grad_shift2, ("fsdp", "ctx"), scatter_dimension=0, tiled=True),
    )
    (
        final_wqkv,
        final_bqv,
        final_wout,
        final_bout,
        final_gain1,
        final_shift1,
        final_wfc,
        final_bfc,
        final_wproj,
        final_bproj,
        final_gain2,
        final_shift2,
    ) = (
        lax.all_gather(sum_wqkv.astype(jnp.bfloat16), "ctx", axis=0, tiled=True).astype(
            sum_wqkv.dtype
        ),
        lax.all_gather(sum_bqv.astype(jnp.bfloat16), "ctx", axis=1, tiled=True).astype(
            sum_bqv.dtype
        ),
        lax.all_gather(sum_wout.astype(jnp.bfloat16), "ctx", axis=1, tiled=True).astype(
            sum_wout.dtype
        ),
        lax.all_gather(sum_bout.astype(jnp.bfloat16), "ctx", axis=0, tiled=True).astype(
            sum_bout.dtype
        ),
        lax.all_gather(sum_gain1.astype(jnp.bfloat16), "ctx", axis=0, tiled=True).astype(
            sum_gain1.dtype
        ),
        lax.all_gather(sum_shift1.astype(jnp.bfloat16), "ctx", axis=0, tiled=True).astype(
            sum_shift1.dtype
        ),
        lax.all_gather(sum_wfc.astype(jnp.bfloat16), "ctx", axis=0, tiled=True).astype(
            sum_wfc.dtype
        ),
        lax.all_gather(sum_bfc.astype(jnp.bfloat16), "ctx", axis=0, tiled=True).astype(
            sum_bfc.dtype
        ),
        lax.all_gather(sum_wproj.astype(jnp.bfloat16), "ctx", axis=1, tiled=True).astype(
            sum_wproj.dtype
        ),
        lax.all_gather(sum_bproj.astype(jnp.bfloat16), "ctx", axis=0, tiled=True).astype(
            sum_bproj.dtype
        ),
        lax.all_gather(sum_gain2.astype(jnp.bfloat16), "ctx", axis=0, tiled=True).astype(
            sum_gain2.dtype
        ),
        lax.all_gather(sum_shift2.astype(jnp.bfloat16), "ctx", axis=0, tiled=True).astype(
            sum_shift2.dtype
        ),
    )
    return (
        block_output,
        input_grad,
        final_wqkv,
        final_bqv,
        final_wout,
        final_bout,
        final_gain1,
        final_shift1,
        final_wfc,
        final_bfc,
        final_wproj,
        final_bproj,
        final_gain2,
        final_shift2,
    )


MESH = pl.DeviceIdType.MESH


def dot_nn(left, right):
    return lax.dot_general(
        left, right, (((1,), (0,)), ((), ())), preferred_element_type=jnp.float32
    )


def dot_nt(left, right):
    return lax.dot_general(
        left, right, (((1,), (1,)), ((), ())), preferred_element_type=jnp.float32
    )


def by_rows(rows, step, body):
    def one(index, carry):
        body(pl.multiple_of(index * step, step))
        return carry

    lax.fori_loop(0, rows // step, one, 0)


def norm_parts(values):
    centred = values - jnp.mean(values, axis=-1, keepdims=True)
    spread = jnp.mean(centred * centred, axis=-1, keepdims=True)
    return centred, lax.rsqrt(spread + epsilon)


def norm_back(values, incoming, gain):
    centred, rate = norm_parts(values)
    hat = centred * rate
    scaled = incoming * gain
    by_value = rate * (
        scaled
        - jnp.mean(scaled, axis=-1, keepdims=True)
        - hat * jnp.mean(scaled * hat, axis=-1, keepdims=True)
    )
    return (
        by_value,
        jnp.sum(incoming * hat, axis=0, keepdims=True),
        jnp.sum(incoming, axis=0, keepdims=True),
    )


class Partly:
    def __init__(self, copy, sends, receives):
        self.copy, self.sends, self.receives = copy, sends, receives

    def start(self):
        self.copy.start()

    def wait_recv(self):
        pl.when(self.receives)(self.copy.wait_recv)

    def wait_send(self):
        pl.when(self.sends)(self.copy.wait_send)


def block_kernel(
    nz,
    x_in,
    dy_in,
    seg_row,
    wqkv_in,
    wout_in,
    wfc_in,
    wproj_in,
    bout_in,
    gain1_in,
    shift1_in,
    gain2_in,
    shift2_in,
    bproj_in,
    bfc_in,
    bqv_in,
    out_hbm,
    grad_hbm,
    gqkv_hbm,
    gout_hbm,
    gfc_hbm,
    gproj_hbm,
    gvec_ref,
    stq,
    sto,
    stf,
    stp,
    xl,
    xr,
    dyb,
    nf,
    wq,
    wo,
    wf,
    wp,
    vec,
    full,
    fcb,
    qb,
    kb,
    vb,
    p0,
    p1,
    p2,
    p3,
    segc,
    ao,
    ax,
    srs,
    rrs,
    mid,
    ns,
    gm,
    act,
    gp,
    turned,
    gsq,
    gso,
    gsf,
    gsp,
    grq,
    gro,
    grf,
    grp,
    glq,
    glf,
    glp,
    accum,
    xq,
    xo,
    xf,
    xp_,
    gtt,
    gt,
    dkb,
    dvb,
    dqkv,
    dx,
    wide,
    wide_b,
    slope,
    gact,
    dsb,
    outv,
    gradv,
    gmid,
    sv,
    svall,
    late,
    lateall,
    bqline,
    l2,
    l2r,
    s2,
    s2r,
    send_sem,
    recv_sem,
    local_sem,
):
    half = jnp.bfloat16
    single = jnp.float32
    z = lax.axis_index("fsdp")
    x = lax.axis_index("ctx")
    t = lax.axis_index("tp")
    y = t // 2
    c = t % 2
    quarter = xl.shape[0] // 2
    block = quarter // 2
    width = xl.shape[1]
    dz = width // nz
    fch = wf.shape[3]
    ec = qb.shape[1]
    length = qb.shape[0]
    probs = (p0, p1, p2, p3)
    sib = (z, x, y * 2 + 1 - c)
    ynb = (z, x, (1 - y) * 2 + c)
    xnb = (z, 1 - x, t)
    dia = (z, 1 - x, (1 - y) * 2 + c)
    started = []

    def send(src, dst, dev):
        slot = len(started)
        copy = pltpu.make_async_remote_copy(
            src_ref=src,
            dst_ref=dst,
            send_sem=send_sem.at[slot],
            recv_sem=recv_sem.at[slot],
            device_id=dev,
            device_id_type=MESH,
        )
        copy.start()
        started.append(copy)
        return copy

    def arrived(copies):
        for copy in copies:
            copy.wait_recv()

    def send_if(src, dst, dev, sends, receives, start=True):
        slot = len(started)
        copy = pltpu.make_async_remote_copy(
            src_ref=src,
            dst_ref=dst,
            send_sem=send_sem.at[slot],
            recv_sem=recv_sem.at[slot],
            device_id=dev,
            device_id_type=MESH,
        )
        some = Partly(copy, sends, receives)
        if start:
            pl.when(sends)(copy.start)
        started.append(some)
        return some

    fetched = []

    def fetch(src, dst):
        copy = pltpu.make_async_copy(src, dst, local_sem.at[len(fetched)])
        copy.start()
        fetched.append(copy)
        return copy

    def zdev(step):
        return ((z + step) % nz, x, t)

    right, left = zdev(1), zdev(nz - 1)

    peers = [(z, px, pt) for px in (x, 1 - x) for pt in (t, sib[2], ynb[2], (1 - y) * 2 + 1 - c)][
        1:
    ]
    for step in range(1, nz):
        peers += [((z + step) % nz, x, t), ((z + step) % nz, x, sib[2])]
    barrier = pltpu.get_barrier_semaphore()
    for dev in peers:
        pl.semaphore_signal(barrier, inc=1, device_id=dev, device_id_type=MESH)

    my_e = pl.ds(pl.multiple_of(x * ec, ec), ec)
    my_f = pl.ds(pl.multiple_of(x * fch, fch), fch)
    stage_q = [
        fetch(wqkv_in.at[j, :, my_e], stq.at[:, j * ec : (j + 1) * ec]) for j in range(3)
    ]
    stage_x = fetch(x_in, xl)
    stage_o = fetch(wout_in.at[my_e], sto)
    stage_f = fetch(wfc_in.at[:, my_f], stf)
    stage_p = fetch(wproj_in.at[my_f], stp)
    stage_dy = [
        fetch(dy_in.at[pl.ds(s * quarter, quarter)], dyb.at[s, x]) for s in range(2)
    ]

    def weight_at(which, h, plane):
        if which == 0:
            return wq.at[plane, :, pl.ds(pl.multiple_of(h * 3 * ec, ec), 3 * ec)]
        if which == 1:
            return wo.at[plane, pl.ds(pl.multiple_of(h * ec, ec), ec)]
        if which == 2:
            return wf.at[h, plane]
        part = fch // 2
        return wp.at[h, plane, (which - 3) * part : (which - 2) * part]

    def rounded(src, dst, rows):
        def some(r):
            dst[pl.ds(r, 64)] = src[pl.ds(r, 64)].astype(half)

        by_rows(rows, 64, some)

    lines = [[], [], [], [], []]
    weight_sib = [[], [], [], [], []]

    def line_start(which):
        mine = weight_at(which, c, z)
        lines[which].append(
            (
                send_if(mine, mine, right, z < nz - 1, z >= 1),
                send_if(mine, mine, left, z >= 1, z < nz - 1),
            )
        )

    def line_pass(which, step):
        from_left, from_right = lines[which][step - 1]
        lower = weight_at(which, c, (z + nz - step) % nz)
        upper = weight_at(which, c, (z + step) % nz)
        from_left.wait_recv()
        if step < nz - 1:
            to_right = send_if(
                lower, lower, right, (z >= step) & (z < nz - 1), z >= step + 1
            )
        weight_sib[which].append(send_if(lower, lower, sib, z >= step, z >= step))
        from_right.wait_recv()
        if step < nz - 1:
            to_left = send_if(
                upper, upper, left, (z + step < nz) & (z >= 1), z + step + 1 < nz
            )
            lines[which].append((to_right, to_left))
        weight_sib[which].append(send_if(upper, upper, sib, z + step < nz, z + step < nz))

    def to_sibling(which):
        mine = weight_at(which, c, z)
        weight_sib[which].append(send(mine, mine, sib))

    for copy in stage_q:
        copy.wait()
    rounded(stq, weight_at(0, c, z), dz)
    pl.semaphore_wait(barrier, len(peers))

    line_start(0)
    stage_x.wait()
    x_copy = send(xl.at[pl.ds(pl.multiple_of(c * quarter, quarter), quarter)], xr.at[c], xnb)
    for row, line in enumerate(
        (bout_in, gain1_in, shift1_in, gain2_in, shift2_in, bproj_in, bfc_in)
    ):
        vec[c, z, row : row + 1] = line[...].astype(half).astype(single)
    pair = bqv_in.shape[1]
    vec[c, z, 7:8, 0:pair] = bqv_in[0:1].astype(half).astype(single)
    vec[c, z, 7:8, pair : 2 * pair] = bqv_in[1:2].astype(half).astype(single)
    vec[c, z, 7:8, 2 * pair :] = jnp.zeros((1, dz - 2 * pair), single)
    vec_copies = [send(vec.at[c, z], vec.at[c, z], sib)]
    for step in range(1, nz):
        for dev_t in (t, sib[2]):
            vec_copies.append(send(vec.at[c, z], vec.at[c, z], ((z + step) % nz, x, dev_t)))
    stage_o.wait()
    rounded(sto, weight_at(1, c, z), ec)
    line_start(1)
    to_sibling(0)
    to_sibling(1)
    for copy in stage_dy:
        copy.wait()
    stage_f.wait()
    rounded(stf, weight_at(2, c, z), dz)
    stage_p.wait()
    rounded(stp, wp.at[c, z], fch)

    arrived(vec_copies)
    for piece in range(nz):
        full[:, piece * dz : (piece + 1) * dz] = vec[c, piece]
    pieces = nz // 2
    for h in range(2):
        for k in range(pieces):
            fcb[h : h + 1, k * dz : (k + 1) * dz] = vec[h, x * pieces + k][6:7]
    lane = lax.broadcasted_iota(jnp.int32, (1, ec), 1)
    low_lane = lane < HD
    first_piece = vec[c, x * pieces][7:8, 0:ec]
    next_piece = vec[c, x * pieces + 1][7:8, 0:ec]
    q_bias = jnp.where(low_lane, first_piece, pltpu.roll(next_piece, HD, 1))
    v_bias = jnp.where(low_lane, pltpu.roll(first_piece, HD, 1), next_piece)
    out_bias = full[0:1]
    gain1, shift1 = full[1:2], full[2:3]
    gain2, shift2 = full[3:4], full[4:5]
    proj_bias = full[5:6]

    def first_norm(src, dst):
        def rows(r):
            centred, rate = norm_parts(src[pl.ds(r, 64)].astype(single))
            dst[pl.ds(r, 64)] = (centred * rate * gain1 + shift1).astype(half)

        by_rows(quarter, 64, rows)

    for s in range(2):
        first_norm(xl.at[pl.ds(s * quarter, quarter)], nf.at[x, s])
    line_pass(0, 1)
    line_pass(1, 1)
    line_pass(0, 2)
    line_pass(1, 2)
    line_start(2)
    line_start(3)
    to_sibling(2)
    to_sibling(3)
    to_sibling(4)
    x_copy.wait_recv()
    x_fwd = send(xr.at[c], xr.at[c], sib)
    dy_copy = send(dyb.at[c, x], dyb.at[c, x], xnb)
    first_norm(xr.at[c], nf.at[1 - x, c])
    x_fwd.wait_recv()
    first_norm(xr.at[1 - c], nf.at[1 - x, 1 - c])
    for i in range(length // quarter):
        line = seg_row[:, i * quarter : (i + 1) * quarter].astype(single)
        segc[i * quarter : (i + 1) * quarter] = jnp.broadcast_to(line, (128, quarter)).T
    for step in range(3, nz):
        line_pass(0, step)
        line_pass(1, step)

    my_qkv = pl.ds(pl.multiple_of(c * 3 * ec, ec), 3 * ec)
    for xi in range(2):
        for ci in range(2):
            proj = dot_nn(nf[xi, ci], wq[:, :, my_qkv].reshape(width, 3 * ec))
            at = pl.ds((xi * 2 + ci) * quarter, quarter)
            qb[at] = (proj[:, 0:ec] + q_bias).astype(half)
            kb[at] = proj[:, ec : 2 * ec].astype(half)
            vb[at] = (proj[:, 2 * ec :] + v_bias).astype(half)

    head_lane = lax.broadcasted_iota(jnp.int32, (1, ec), 1) // HD
    n_blocks = length // quarter
    heads = ec // HD

    def only(values, h):
        return jnp.where(head_lane == h, values, jnp.zeros_like(values))

    for i in range(n_blocks):
        j0 = max(0, i - 2)
        span = (i + 1 - j0) * quarter
        keys = pl.ds(j0 * quarter, span)
        scores = (wide, wide_b)
        for h in range(heads):
            q_h = only(qb[pl.ds(i * quarter, quarter)], h) * jnp.asarray(HD**-0.5, half)
            scores[h][:, 0:span] = dot_nt(q_h, kb[keys])

        def soft(r, i=i, j0=j0, span=span):
            q_at = i * quarter + r + lax.broadcasted_iota(jnp.int32, (64, span), 0)
            k_at = j0 * quarter + lax.broadcasted_iota(jnp.int32, (64, span), 1)
            seg_q = segc[pl.ds(pl.multiple_of(i * quarter + r, 64), 64)]
            seg_k = seg_row[:, j0 * quarter : j0 * quarter + span].astype(single)
            same = jnp.concatenate([seg_q] * (span // 128), axis=1) == seg_k
            allowed = (k_at <= q_at) & same
            for h in range(heads):
                masked = jnp.where(allowed, scores[h][pl.ds(r, 64), 0:span], -1e30)
                expo = jnp.exp(masked - jnp.max(masked, axis=-1, keepdims=True))
                share = expo * (1.0 / jnp.sum(expo, axis=-1, keepdims=True))
                probs[i][h, pl.ds(r, 64)] = share.astype(half)

        by_rows(quarter, 64, soft)
        total = None
        for h in range(heads):
            part = dot_nn(probs[i][h], only(vb[keys], h))
            total = part if total is None else total + part
        ao[i // 2, i % 2] = total.astype(half)

    my_ax = pl.ds(pl.multiple_of(c * ec, ec), ec)
    att_copy = send(ao.at[:, 1 - c], ax.at[:, :, my_ax], sib)
    ax[:, :, my_ax] = ao[:, c]
    line_pass(2, 1)
    line_start(4)
    arrived(weight_sib[1])
    att_copy.wait_recv()

    group = block // 2

    def rows_of(ref, g):
        return jnp.concatenate(
            [ref[b * block + g * group : b * block + (g + 1) * group] for b in range(4)], axis=0
        )

    def rows_of_pair(ref, g):
        return jnp.concatenate(
            [
                ref[b // 2, (b % 2) * block + g * group : (b % 2) * block + (g + 1) * group]
                for b in range(4)
            ],
            axis=0,
        )

    def spread_part(k, g, part, side):
        for p in range(nz // 2):
            value = part(g, side * (nz // 2) + p).astype(half)
            for b in range(4):
                srs[k, g, b // 2, b % 2, side, :, p * dz : (p + 1) * dz] = value[
                    b * group : (b + 1) * group
                ]

    def spread_send(k, g, side):
        if side:
            return [
                send(srs.at[k, g, 1 - x, 1 - y, 1], rrs.at[k, g, 1], ynb),
                send(srs.at[k, g, x, 1 - y, 1], rrs.at[k, g, 5], ynb),
            ]
        return [
            send(srs.at[k, g, 1 - x, 1 - y, 0], rrs.at[k, g, 0], xnb),
            send(srs.at[k, g, 1 - x, y, 0], rrs.at[k, g, 2], xnb),
        ]

    def spread_pass(k, g, copies):
        copies[0].wait_recv()
        srs[k, g, x, 1 - y, 0] = (
            srs[k, g, x, 1 - y, 0].astype(single) + rrs[k, g, 0].astype(single)
        ).astype(half)
        last = [send(srs.at[k, g, x, 1 - y, 0], rrs.at[k, g, 4], ynb)]
        copies[2].wait_recv()
        srs[k, g, 1 - x, y, 1] = (
            srs[k, g, 1 - x, y, 1].astype(single) + rrs[k, g, 1].astype(single)
        ).astype(half)
        last.append(send(srs.at[k, g, 1 - x, y, 1], rrs.at[k, g, 3], xnb))
        return [copies[1], copies[3]] + last

    def spread_sum(k, g, part):
        copies = []
        for side in range(2):
            spread_part(k, g, part, side)
            copies += spread_send(k, g, side)
        return copies

    def summed(k, g, at):
        sides = [
            srs[k, g, x, y, side, at].astype(single)
            + rrs[k, g, 2 + side, at].astype(single)
            + rrs[k, g, 4 + side, at].astype(single)
            for side in range(2)
        ]
        return jnp.concatenate(sides, axis=1)

    def attention_out(g, piece):
        return dot_nn(rows_of_pair(ax, g), wo[piece])

    copies = [spread_sum(0, g, attention_out) for g in range(2)]
    copies = [spread_pass(0, g, copies[g]) for g in range(2)]
    dy_copy.wait_recv()
    dy_fwd = send(dyb.at[c, 1 - x], dyb.at[c, 1 - x], sib)
    line_pass(3, 1)
    line_pass(2, 2)

    my_x = xl.at[pl.ds(pl.multiple_of(c * quarter + y * block, block), block)]

    def middle_rows(g):
        def rows(r):
            at = pl.ds(pl.multiple_of(g * group + r, 32), 32)
            value = my_x[at].astype(single) + (summed(0, g, pl.ds(r, 32)) + out_bias)
            mid[at] = value
            centred, rate = norm_parts(value)
            ns[c, x, y, at] = (centred * rate * gain2 + shift2).astype(half)

        by_rows(group, 32, rows)

    def gather_rows(g, part):
        return pl.ds(g * group + part * (group // 2), group // 2)

    def gather(buf, g):
        mine = buf.at[c, x, y]
        first, last = mine.at[gather_rows(g, 0)], mine.at[gather_rows(g, 1)]
        all_rows = mine.at[pl.ds(g * group, group)]
        return [
            send(first, first, xnb),
            send(last, last, ynb),
            send(last, last, xnb),
            send(first, first, ynb),
            send(all_rows, all_rows, sib),
        ]

    def gather_pass(buf, g, copies):
        by_x = buf.at[c, 1 - x, y, gather_rows(g, 0)]
        by_y = buf.at[c, x, 1 - y, gather_rows(g, 1)]
        copies[0].wait_recv()
        through = [send(by_x, by_x, ynb)]
        copies[1].wait_recv()
        through.append(send(by_y, by_y, xnb))
        return through

    def gather_end(buf, g, copies, through):
        def on(bx, by):
            rows = buf.at[c, bx, by, pl.ds(g * group, group)]
            return send(rows, rows, sib)

        copies[3].wait_recv()
        to_sib = [copies[4], on(x, 1 - y)]
        copies[2].wait_recv()
        to_sib.append(on(1 - x, y))
        arrived(through)
        to_sib.append(on(1 - x, 1 - y))
        return to_sib

    def hidden(g):
        rows_ns = ns[c, :, :, g * group : (g + 1) * group].reshape(quarter, width)
        for h in range(2):
            wide[:, 0:fch] = dot_nn(rows_ns, wf[h].reshape(width, fch))

            def rows(r, h=h):
                value = wide[pl.ds(r, group), 0:fch] + fcb[h : h + 1]
                root = 0.7978845608028654
                square = value * value
                inner = jnp.tanh(root * (value + 0.044715 * (square * value)))
                lift = 0.5 * (1.0 + inner)
                at = pl.ds(pl.multiple_of(2 * r + g * group, group), group)
                act[c, h, at] = (value * lift).astype(half)
                slope[h, at] = lift + 0.5 * value * (1.0 - inner * inner) * (
                    root * (1.0 + 3.0 * 0.044715 * square)
                )

            by_rows(quarter, group, rows)

    def hidden_add(which, piece, there, first=False):
        part_at = slice((which - 3) * (fch // 2), (which - 2) * (fch // 2))
        at = pl.ds(pl.multiple_of(((piece + nz) % nz) * dz, dz), dz)

        def add():
            rows_dy = dyb[c, :, :, at].reshape(2 * quarter, dz)
            for h in range(2):
                part = dot_nt(rows_dy, wp[h, (piece + nz) % nz, part_at])
                if first:
                    gact[h, :, part_at] = part
                else:
                    gact[h, :, part_at] += part

        if there is None:
            add()
        else:
            pl.when(there)(add)

    def hidden_grad(g):
        def rows(r):
            at = pl.ds(pl.multiple_of(2 * r + g * group, group), group)
            for h in range(2):
                gp[c, h, at] = (gact[h, at] * slope[h, at]).astype(half)

        by_rows(quarter, group, rows)

    ns_copies = []
    for g in range(2):
        arrived(copies[g])
        middle_rows(g)
        ns_copies.append(gather(ns, g))
    through = [gather_pass(ns, g, ns_copies[g]) for g in range(2)]
    line_pass(4, 1)
    line_pass(3, 2)
    dy_fwd.wait_recv()
    for which in (3, 4):
        weight_sib[which].pop(0).wait_recv()
        hidden_add(which, z, None, first=True)
    arrived(weight_sib[3])
    weight_sib[3] = []
    hidden_add(3, z - 1, z >= 1)
    hidden_add(3, z + 1, z < nz - 1)
    ns_sib = gather_end(ns, 0, ns_copies[0], through[0])
    for step in range(3, nz):
        line_pass(2, step)
    arrived(weight_sib[2])
    hidden(0)
    line_pass(4, 2)
    ns_sib += gather_end(ns, 1, ns_copies[1], through[1])
    hidden(1)
    act_copy = send(act.at[c, 1 - c], act.at[c, 1 - c], sib)
    for which, steps in ((3, (2,)), (4, (1, 2))):
        arrived(weight_sib[which])
        weight_sib[which] = []
        for step in steps:
            hidden_add(which, z - step, z >= step)
            hidden_add(which, z + step, z + step < nz)

    def weight_grad(left, right_at, out):
        def one(step, carry):
            piece = (z + step) % nz
            at = pl.ds(pl.multiple_of(piece * dz, dz), dz)
            out[piece] = dot_nn(turned[0:left], right_at(at)).astype(half)
            return carry

        lax.fori_loop(0, nz, one, 0)

    def direct_sum(out, home):
        return [
            send(out.at[(z + step) % nz], home.at[z], zdev(step)) for step in range(1, nz)
        ]

    def line_sum(out, home, merged):
        up2, down2 = out.at[(z + 2) % nz], out.at[(z + nz - 2) % nz]
        up1, down1 = out.at[(z + 1) % nz], out.at[(z + nz - 1) % nz]
        far_up = send_if(out.at[nz - 1], merged, right, z == 0, z == 1)
        far_down = send_if(out.at[0], merged, left, z == nz - 1, z == nz - 2)
        two_up = send_if(up2, home.at[z], zdev(2), z + 2 < nz, z >= 2, start=False)
        two_down = send_if(down2, home.at[z], zdev(nz - 2), z >= 2, z + 2 < nz, start=False)
        pl.when(z == 0)(two_up.start)
        pl.when(z == nz - 1)(two_down.start)
        one_up = send_if(up1, home.at[z], right, z < nz - 1, z >= 1)
        one_down = send_if(down1, home.at[z], left, z >= 1, z < nz - 1)
        return out, home, merged, far_up, far_down, two_up, two_down, one_up, one_down

    def line_add(line):
        out, home, merged, far_up, far_down, two_up, two_down, _, _ = line

        @pl.when(z == 1)
        def _():
            far_up.copy.wait_recv()
            out[nz - 1] = (out[nz - 1].astype(single) + merged[...].astype(single)).astype(half)
            two_up.start()

        @pl.when(z == nz - 2)
        def _():
            far_down.copy.wait_recv()
            out[0] = (out[0].astype(single) + merged[...].astype(single)).astype(half)
            two_down.start()

    def line_end(line):
        out, home, _, _, _, two_up, two_down, one_up, one_down = line
        total = accum.at[0 : out.shape[1]]
        total[...] = out[z].astype(single)
        for copy, source, there in (
            (one_up, z - 1, z >= 1),
            (one_down, z + 1, z < nz - 1),
            (two_up, z - 2, z >= 2),
            (two_down, z + 2, z + 2 < nz),
        ):

            def take(copy=copy, source=source):
                copy.copy.wait_recv()
                total[...] += home[(source + nz) % nz].astype(single)

            pl.when(there)(take)
        return total[...]

    def turn_rows(src, left, column):
        turned[0:left, pl.ds(pl.multiple_of(column, quarter), quarter)] = src.T

    act_copy.wait_recv()
    for s in range(2):
        for k in range(2):
            turn_rows(act[s, c, k * quarter : (k + 1) * quarter], fch, (s * 2 + k) * quarter)
    weight_grad(fch, lambda at: dyb[:, :, :, at].reshape(length, dz), gsp)
    proj_z = line_sum(gsp, grp, glp)
    for which in (3, 4):
        line_pass(which, 3)
        arrived(weight_sib[which])
        hidden_add(which, z - 3, z >= 3)
        hidden_add(which, z + 3, z + 3 < nz)

    def norm2_part(g, piece):
        return dot_nt(rows_of(gp.at[c, 0], g), wf[0, piece]) + dot_nt(
            rows_of(gp.at[c, 1], g), wf[1, piece]
        )

    hidden_grad(0)
    copies = [spread_sum(1, 0, norm2_part)]
    hidden_grad(1)
    gp_copy = send(gp.at[c, 1 - c], gp.at[c, 1 - c], sib)
    copies.append(spread_sum(1, 1, norm2_part))
    copies[0] = spread_pass(1, 0, copies[0])
    copies[1] = spread_pass(1, 1, copies[1])
    line_add(proj_z)

    sv[...] = jnp.zeros_like(sv)
    late[...] = jnp.zeros_like(late)
    my_dy = dyb.at[c, x, pl.ds(pl.multiple_of(y * block, block), block)]

    def middle_back(g):
        def rows(r):
            at = pl.ds(pl.multiple_of(g * group + r, 32), 32)
            grad_rows = my_dy[at].astype(single)
            by_value, gain_part, shift_part = norm_back(
                mid[at], summed(1, g, pl.ds(r, 32)), gain2
            )
            grad = grad_rows + by_value
            gmid[at] = grad
            low = grad.astype(half)
            gm[c, x, y, at] = low
            sv[3:4] += gain_part
            sv[4:5] += shift_part
            sv[0:1] += jnp.sum(low.astype(single), axis=0, keepdims=True)
            sv[5:6] += jnp.sum(grad_rows, axis=0, keepdims=True)

        by_rows(group, 32, rows)

    gm_copies = []
    for g in range(2):
        arrived(copies[g])
        middle_back(g)
        gm_copies.append(gather(gm, g))

    def feed_part(g, piece):
        return dot_nn(rows_of(act.at[c, 0], g), wp[0, piece]) + dot_nn(
            rows_of(act.at[c, 1], g), wp[1, piece]
        )

    gp_copy.wait_recv()
    arrived(ns_sib)
    for s in range(2):
        for k in range(2):
            turn_rows(gp[s, c, k * quarter : (k + 1) * quarter], fch, (s * 2 + k) * quarter)
    weight_grad(fch, lambda at: ns[:, :, :, :, at].reshape(length, dz), gsf)
    fc_z = line_sum(gsf, grf, glf)
    through = [gather_pass(gm, 0, gm_copies[0])]
    for side in range(2):
        spread_part(2, 0, feed_part, side)
    through.append(gather_pass(gm, 1, gm_copies[1]))
    for side in range(2):
        spread_part(2, 1, feed_part, side)
    feed_copies = [spread_send(2, g, 0) + spread_send(2, g, 1) for g in range(2)]
    for s in range(2):
        sv[6:7, 0:fch] += jnp.sum(gp[s, c].astype(single), axis=0, keepdims=True)
    my_place = x * 4 + t
    for piece in range(nz):
        for row, source in enumerate((0, 3, 4, 5)):
            s2[piece, row : row + 1] = sv[source : source + 1, piece * dz : (piece + 1) * dz]
        for k in range(pieces):
            s2[piece, 4 + k : 5 + k] = sv[6:7, k * dz : (k + 1) * dz]
        s2[piece, 4 + pieces : 8] = jnp.zeros((4 - pieces, dz), single)

    def over_planes(lines, home):
        home[z] = lines[z]
        return [
            send(lines.at[(z + step) % nz], home.at[z], zdev(step)) for step in range(1, nz)
        ]

    def over_plane(home, places):
        value = home[0]
        for piece in range(1, nz):
            value = value + home[piece]
        places[my_place] = value
        return [
            send(places.at[my_place], places.at[my_place], dev) for dev in peers[0:7]
        ]

    def place_sum(places):
        value = places[0]
        for place in range(1, 8):
            value = value + places[place]
        return value

    def grad_attended(g):
        rows_gm = gm[c, :, :, g * group : (g + 1) * group].reshape(quarter, width)
        total = None
        for piece in range(nz):
            part = dot_nt(rows_gm[:, piece * dz : (piece + 1) * dz], wo[piece])
            total = part if total is None else total + part
        for h in range(2):
            for b in range(4):
                gtt[h, b, g] = total[b * group : (b + 1) * group, h * ec : (h + 1) * ec].astype(
                    half
                )
        gt[c, :, g] = gtt[c, :, g]
        return send(gtt.at[1 - c, :, g], gt.at[c, :, g], sib)

    gm_sib, gt_copies = [], []
    for g in range(2):
        gm_sib += gather_end(gm, g, gm_copies[g], through[g])
        gt_copies.append(grad_attended(g))
    xp_[x] = line_end(proj_z).astype(half)
    proj_x = [send(xp_.at[x], xp_.at[x], xnb)]
    arrived(gm_sib)
    for s in range(2):
        for k in range(2):
            turn_rows(ao[k, s], ec, (s * 2 + k) * quarter)
    weight_grad(ec, lambda at: gm[:, :, :, :, at].reshape(length, dz), gso)
    out_z = direct_sum(gso, gro)
    arrived(gt_copies)
    s2_copies = over_planes(s2, s2r)
    my_rows = pl.multiple_of(c * quarter + y * block, block)

    def out_rows(g):
        def rows(r):
            at = pl.ds(pl.multiple_of(g * group + r, 32), 32)
            value = mid[at] + (summed(2, g, pl.ds(r, 32)) + proj_bias)
            outv[pl.ds(pl.multiple_of(my_rows + g * group + r, 32), 32)] = value.astype(half)

        by_rows(group, 32, rows)


    dkb[...] = jnp.zeros_like(dkb)
    dvb[...] = jnp.zeros_like(dvb)
    for i in range(n_blocks):
        j0 = max(0, i - 2)
        span = (i + 1 - j0) * quarter
        keys = pl.ds(j0 * quarter, span)
        grads = (wide, wide_b)
        rows_gt = gt[i % 2, (i // 2) * 2 : (i // 2) * 2 + 2].reshape(quarter, ec)
        ga = [only(rows_gt, h) for h in range(heads)]
        for h in range(heads):
            grads[h][:, 0:span] = dot_nt(ga[h], vb[keys])

        def back(r, i=i, span=span):
            for h in range(heads):
                grad_p = grads[h][pl.ds(r, 128), 0:span]
                share = probs[i][h, pl.ds(r, 128)].astype(single)
                delta = jnp.sum(grad_p * share, axis=-1, keepdims=True)
                dsb[h, pl.ds(r, 128), 0:span] = (share * (grad_p - delta)).astype(half)

        by_rows(quarter, 128, back)
        total = None
        for h in range(heads):
            grad_s = dsb[h, :, 0:span]
            part = dot_nn(grad_s, only(kb[keys], h))
            total = part if total is None else total + part
            dkb[keys] += dot_nn(grad_s.T, only(qb[pl.ds(i * quarter, quarter)], h))
            dvb[keys] += dot_nn(probs[i][h].T, ga[h])
        dqkv[i // 2, i % 2, :, 0:ec] = (total * HD**-0.5).astype(half)
        if i == 0:
            line_add(fc_z)
        if i == 1:
            feed_copies = [spread_pass(2, g, feed_copies[g]) for g in range(2)]
    for i in range(n_blocks):
        at = pl.ds(i * quarter, quarter)
        dqkv[i // 2, i % 2, :, ec : 2 * ec] = (dkb[at] * HD**-0.5).astype(half)
        dqkv[i // 2, i % 2, :, 2 * ec :] = dvb[at].astype(half)

    my_dx = pl.ds(pl.multiple_of(c * 3 * ec, ec), 3 * ec)
    dx_copy = send(dqkv.at[:, 1 - c], dx.at[:, :, my_dx], sib)
    dx[:, :, my_dx] = dqkv[:, c]
    for i in range(n_blocks):
        turn_rows(dqkv[i // 2, i % 2], 3 * ec, i * quarter)
    weight_grad(3 * ec, lambda at: nf[:, :, :, at].reshape(length, dz), gsq)
    qkv_z = line_sum(gsq, grq, glq)
    arrived(weight_sib[0])
    dx_copy.wait_recv()

    def norm1_part(g, piece):
        return dot_nt(rows_of_pair(dx, g), wq[piece])

    copies = [spread_sum(3, g, norm1_part) for g in range(2)]
    copies[0] = spread_pass(3, 0, copies[0])
    line_add(qkv_z)
    copies[1] = spread_pass(3, 1, copies[1])
    for g in range(2):
        arrived(feed_copies[g])
        out_rows(g)
    mine = outv.at[pl.ds(my_rows, block)]
    theirs = outv.at[pl.ds(pl.multiple_of(c * quarter + (1 - y) * block, block), block)]
    out_s = [send(mine, mine, sib)]

    xf[x] = line_end(fc_z).T.astype(half)
    fc_x = send(xf.at[x], xf.at[x], xnb)
    arrived(out_z)
    value = gso[z].astype(single)
    for step in range(1, nz):
        value = value + gro[(z + step) % nz].astype(single)
    xo[x] = value.astype(half)
    out_x = send(xo.at[x], xo.at[x], xnb)
    arrived(s2_copies)
    sv_copies = over_plane(s2r, svall)

    for k, first in enumerate((0, 2 * ec)):
        bqline[:, k * ec : (k + 1) * ec] = jnp.sum(
            dqkv[:, :, :, first : first + ec].astype(single).reshape(length, ec),
            axis=0,
            keepdims=True,
        )

    def first_back(g):
        def rows(r):
            at = pl.ds(pl.multiple_of(g * group + r, 32), 32)
            by_value, gain_part, shift_part = norm_back(
                my_x[at].astype(single), summed(3, g, pl.ds(r, 32)), gain1
            )
            gradv[pl.ds(pl.multiple_of(my_rows + g * group + r, 32), 32)] = (
                gmid[at] + by_value
            ).astype(half)
            late[0:1] += gain_part
            late[1:2] += shift_part

        by_rows(group, 32, rows)

    def grad_rows_at(by, g):
        start = pl.multiple_of(c * quarter + by * block + g * group, group)
        return gradv.at[pl.ds(start, group)]

    grad_copies = []
    for g in range(2):
        arrived(copies[g])
        first_back(g)
        if g:
            for piece in range(nz):
                l2[piece, 0:2] = late[:, piece * dz : (piece + 1) * dz]
                l2[piece, 2:3] = bqline[...]
                l2[piece, 3:8] = jnp.zeros((5, dz), single)
            l2_copies = over_planes(l2, l2r)
        rows = grad_rows_at(y, g)
        grad_copies += [send(rows, rows, ynb), send(rows, rows, sib)]
    out_y = send(mine, mine, ynb)

    xq[x] = line_end(qkv_z).T.astype(half)
    qkv_x = send(xq.at[x], xq.at[x], xnb)
    arrived(l2_copies)
    late_copies = over_plane(l2r, lateall)
    arrived(proj_x)
    final = [fetch(xp_, gproj_hbm)]
    grad_s_ = [grad_copies[1], grad_copies[3]]
    for g in range(2):
        grad_copies[2 * g].wait_recv()
        rows = grad_rows_at(1 - y, g)
        grad_s_.append(send(rows, rows, sib))
    arrived([fc_x])
    final.append(fetch(xf, gfc_hbm))
    arrived([out_x])
    final.append(fetch(xo, gout_hbm))
    arrived(grad_s_)
    final.append(fetch(gradv, grad_hbm))
    out_y.wait_recv()
    out_s.append(send(theirs, theirs, sib))
    arrived(sv_copies)
    arrived(late_copies)
    early_sum, late_sum = place_sum(svall), place_sum(lateall)
    source = (z // pieces) * 4 + t
    bfc_lines = svall[source, 4 : 4 + pieces]
    gvec_ref[0:1] = early_sum[0:1]
    gvec_ref[1:3] = late_sum[0:2]
    gvec_ref[3:6] = early_sum[1:4]
    gvec_ref[6:7] = jnp.where(z % pieces == 0, bfc_lines[0:1], bfc_lines[1:2])
    q_line, v_line = lateall[source, 2:3, 0:ec], lateall[source, 2:3, ec : 2 * ec]
    even = jnp.where(low_lane, q_line, pltpu.roll(v_line, HD, 1))
    odd = jnp.where(low_lane, pltpu.roll(q_line, HD, 1), v_line)
    gvec_ref[7:8, 0:ec] = jnp.where(z % pieces == 0, even, odd)
    gvec_ref[7:8, ec:dz] = jnp.zeros((1, dz - ec), single)
    arrived(out_s)
    final.append(fetch(outv, out_hbm))
    arrived([qkv_x])
    final.append(fetch(xq, gqkv_hbm))
    for copy in final:
        copy.wait()
    for copy in started:
        copy.wait_send()


def finish_kernel(
    out,
    grad,
    gqkv,
    gout,
    gfc,
    gproj,
    gvec,
    out_ref,
    grad_ref,
    gqkv_ref,
    gout_ref,
    gfc_ref,
    gproj_ref,
    gqv_ref,
    *line_refs,
):
    single = jnp.float32
    out_ref[...] = out[...]
    grad_ref[...] = grad[...]
    ec = gqkv_ref.shape[2]
    for j in range(3):
        gqkv_ref[j] = gqkv[0, :, j * ec : (j + 1) * ec].astype(single)
    gout_ref[...] = gout[0].astype(single)
    gfc_ref[...] = gfc[0].astype(single)
    gproj_ref[...] = gproj[0].astype(single)
    pair = gqv_ref.shape[1]
    gqv_ref[0:1] = gvec[7:8, 0:pair]
    gqv_ref[1:2] = gvec[7:8, pair : 2 * pair]
    for row, ref in enumerate(line_refs):
        ref[...] = gvec[row : row + 1]


def plane_block(
    nz,
    block_input,
    segment_ids,
    cotangent,
    qkv_weight,
    qv_bias,
    out_weight,
    out_bias,
    norm1_gain,
    norm1_shift,
    fc_weight,
    fc_bias,
    proj_weight,
    proj_bias,
    norm2_gain,
    norm2_shift,
):
    half = jnp.bfloat16
    single = jnp.float32
    _, rows, width = block_input.shape
    length = segment_ids.shape[1]
    dz = qkv_weight.shape[0]
    ec = qkv_weight.shape[2] // 2
    fch = fc_weight.shape[1] // 2
    quarter, block = rows // 2, rows // 4
    vmem = pltpu.VMEM
    spans = [(i + 1 - max(0, i - 2)) * quarter for i in range(4)]
    heads = ec // HD
    scratch = [
        vmem((dz, 3 * ec), single),
        vmem((ec, dz), single),
        vmem((dz, fch), single),
        vmem((fch, dz), single),
        vmem((rows, width), half),
        vmem((2, quarter, width), half),
        vmem((2, 2, quarter, width), half),
        vmem((2, 2, quarter, width), half),
        vmem((nz, dz, 6 * ec), half),
        vmem((nz, 2 * ec, dz), half),
        vmem((2, nz, dz, fch), half),
        vmem((2, nz, fch, dz), half),
        vmem((2, nz, 8, dz), single),
        vmem((8, width), single),
        vmem((2, fch), single),
        vmem((length, ec), half),
        vmem((length, ec), half),
        vmem((length, ec), half),
    ]
    scratch += [vmem((heads, quarter, span), half) for span in spans]
    scratch += [
        vmem((length, 128), single),
        vmem((2, 2, quarter, ec), half),
        vmem((2, quarter, 2 * ec), half),
        vmem((4, 2, 2, 2, 2, block // 2, width // 2), half),
        vmem((4, 2, 6, block // 2, width // 2), half),
        vmem((block, width), single),
        vmem((2, 2, 2, block, width), half),
        vmem((2, 2, 2, block, width), half),
        vmem((2, 2, rows, fch), half),
        vmem((2, 2, rows, fch), half),
        vmem((fch, length), half),
    ]
    for _ in range(2):
        scratch += [
            vmem((nz, 3 * ec, dz), half),
            vmem((nz, ec, dz), half),
            vmem((nz, fch, dz), half),
            vmem((nz, fch, dz), half),
        ]
    scratch += [
        vmem((3 * ec, dz), half),
        vmem((fch, dz), half),
        vmem((fch, dz), half),
        vmem((fch, dz), single),
        vmem((2, dz, 3 * ec), half),
        vmem((2, ec, dz), half),
        vmem((2, dz, fch), half),
        vmem((2, fch, dz), half),
        vmem((2, 4, 2, block // 2, ec), half),
        vmem((2, 4, 2, block // 2, ec), half),
        vmem((length, ec), single),
        vmem((length, ec), single),
        vmem((2, 2, quarter, 3 * ec), half),
        vmem((2, quarter, 6 * ec), half),
        vmem((quarter, 3 * quarter), single),
        vmem((quarter, 3 * quarter), single),
        vmem((2, rows, fch), single),
        vmem((2, rows, fch), single),
        vmem((2, quarter, 3 * quarter), half),
        vmem((rows, width), half),
        vmem((rows, width), half),
        vmem((block, width), single),
        vmem((8, width), single),
        vmem((8, 8, dz), single),
        vmem((2, width), single),
        vmem((8, 8, dz), single),
        vmem((1, dz), single),
        vmem((nz, 8, dz), single),
        vmem((nz, 8, dz), single),
        vmem((nz, 8, dz), single),
        vmem((nz, 8, dz), single),
        pltpu.SemaphoreType.DMA((300,)),
        pltpu.SemaphoreType.DMA((300,)),
        pltpu.SemaphoreType.DMA((20,)),
    ]
    whole = pl.BlockSpec(memory_space=pltpu.VMEM)
    there = pl.BlockSpec(memory_space=pl.ANY)
    middle = pl.pallas_call(
        functools.partial(block_kernel, nz),
        out_shape=(
            jax.ShapeDtypeStruct((rows, width), half),
            jax.ShapeDtypeStruct((rows, width), half),
            jax.ShapeDtypeStruct((2, dz, 3 * ec), half),
            jax.ShapeDtypeStruct((2, ec, dz), half),
            jax.ShapeDtypeStruct((2, dz, fch), half),
            jax.ShapeDtypeStruct((2, fch, dz), half),
            jax.ShapeDtypeStruct((8, dz), single),
        ),
        in_specs=[there] * 2 + [whole] + [there] * 4 + [whole] * 8,
        out_specs=(there,) * 6 + (whole,),
        scratch_shapes=scratch,
        compiler_params=pltpu.CompilerParams(
            collective_id=0, has_side_effects=True, vmem_limit_bytes=67043328
        ),
        name="residual_block",
    )(
        block_input.reshape(rows, width),
        cotangent.reshape(rows, width),
        segment_ids,
        qkv_weight.transpose(1, 0, 2),
        out_weight,
        fc_weight,
        proj_weight,
        out_bias.reshape(1, dz),
        norm1_gain.reshape(1, dz),
        norm1_shift.reshape(1, dz),
        norm2_gain.reshape(1, dz),
        norm2_shift.reshape(1, dz),
        proj_bias.reshape(1, dz),
        fc_bias.reshape(1, dz),
        qv_bias,
    )

    def halves(shape, axis):
        return pl.BlockSpec(
            shape, lambda side: tuple(side if k == axis else 0 for k in range(len(shape)))
        )

    line = pl.BlockSpec((1, dz), lambda side: (0, 0))
    outs = pl.pallas_call(
        finish_kernel,
        grid=(2,),
        out_shape=(
            jax.ShapeDtypeStruct((rows, width), half),
            jax.ShapeDtypeStruct((rows, width), half),
            jax.ShapeDtypeStruct((3, dz, 2 * ec), single),
            jax.ShapeDtypeStruct((2 * ec, dz), single),
            jax.ShapeDtypeStruct((dz, 2 * fch), single),
            jax.ShapeDtypeStruct((2 * fch, dz), single),
            jax.ShapeDtypeStruct(qv_bias.shape, single),
        )
        + (jax.ShapeDtypeStruct((1, dz), single),) * 7,
        in_specs=[
            halves((quarter, width), 0),
            halves((quarter, width), 0),
            halves((1, dz, 3 * ec), 0),
            halves((1, ec, dz), 0),
            halves((1, dz, fch), 0),
            halves((1, fch, dz), 0),
            pl.BlockSpec((8, dz), lambda side: (0, 0)),
        ],
        out_specs=(
            halves((quarter, width), 0),
            halves((quarter, width), 0),
            halves((3, dz, ec), 2),
            halves((ec, dz), 0),
            halves((dz, fch), 1),
            halves((fch, dz), 0),
            pl.BlockSpec(qv_bias.shape, lambda side: (0, 0)),
        )
        + (line,) * 7,
        name="finish",
    )(*middle)
    out, grad, gqkv, gout, gfc, gproj, gqv = outs[:7]
    gbout, ggain1, gshift1, ggain2, gshift2, gbproj, gbfc = [
        value.reshape(dz) for value in outs[7:]
    ]
    return (
        out.reshape(block_input.shape),
        grad.reshape(block_input.shape),
        gqkv.transpose(1, 0, 2),
        gqv,
        gout,
        gbout,
        ggain1,
        gshift1,
        gfc,
        gbfc,
        gproj,
        gbproj,
        ggain2,
        gshift2,
    )


def device_program(mesh):
    planes = mesh.shape["fsdp"]

    def program(block_input, *others):
        seqs_here, rows, width = block_input.shape
        one_kernel = (
            seqs_here == 1
            and mesh.shape["ctx"] == 2
            and mesh.shape["tp"] == 4
            and planes == 4
            and width // planes == 256
        )
        if one_kernel:
            return plane_block(planes, block_input, *others)
        return on_device(block_input, *others)

    return program


def solution(mesh):
    return jax.shard_map(
        device_program(mesh),
        mesh=mesh,
        in_specs=(
            P("fsdp", "ctx", None),
            P("fsdp", None),
            P("fsdp", "ctx", None),
            P("fsdp", None, "tp"),
            P(None, ("tp", "fsdp")),
            P("tp", "fsdp"),
            P("fsdp"),
            P("fsdp"),
            P("fsdp"),
            P("fsdp", "tp"),
            P(("tp", "fsdp")),
            P("tp", "fsdp"),
            P("fsdp"),
            P("fsdp"),
            P("fsdp"),
        ),
        out_specs=(
            P("fsdp", "ctx", None),
            P("fsdp", "ctx", None),
            P("fsdp", None, "tp"),
            P(None, ("tp", "fsdp")),
            P("tp", "fsdp"),
            P("fsdp"),
            P("fsdp"),
            P("fsdp"),
            P("fsdp", "tp"),
            P(("tp", "fsdp")),
            P("tp", "fsdp"),
            P("fsdp"),
            P("fsdp"),
            P("fsdp"),
        ),
        check_vma=False,
    )
```
